128 devices in a mesh: fsdp: 32 (over y_lo, z, x), tp: 4 (over y_hi, core).
Axes of the slice: x: 4, y: 4 (y_hi: 2, y_lo: 2; y = y_hi * 2 + y_lo), z: 4, core: 2. Of those that a mesh axis runs over, the one named last changes fastest.
Arguments:
- residual: float32 [32, 768, 1152], P('fsdp', 'tp'), may hold values from -60 to 60
- valid_keys: int32 [32, 768], P('fsdp'), may hold values from 0 to 1, as said below
- pre_gain: float32 [1152], replicated, may hold values from 0.1 to 1.9
- pre_shift: float32 [1152], replicated, may hold values from -4 to 4
- query_weight: bfloat16 [1152, 1152], P('fsdp', 'tp'), may hold values from -2 to 2
- query_bias: float32 [1152], replicated, may hold values from -4 to 4
- key_weight: bfloat16 [1152, 1152], P('fsdp', 'tp'), may hold values from -2 to 2
- value_weight: bfloat16 [1152, 1152], P('fsdp', 'tp'), may hold values from -0.1875 to 0.1875
- value_bias: float32 [1152], replicated, may hold values from -0.4375 to 0.4375
- out_weight: bfloat16 [1152, 1152], P('tp', 'fsdp'), may hold values from -1.25 to 1.25
- out_bias: float32 [1152], replicated, may hold values from -4 to 4
- mid_gain: float32 [1152], replicated, may hold values from 0.1 to 1.9
- mid_shift: float32 [1152], replicated, may hold values from -4 to 4
- up_weight: bfloat16 [1152, 4304], P('fsdp', 'tp'), may hold values from -0.1875 to 0.1875
- up_bias: float32 [4304], replicated, may hold values from -4 to 4
- down_weight: bfloat16 [4304, 1152], P('tp', 'fsdp'), may hold values from -0.09375 to 0.09375
- down_bias: float32 [1152], replicated, may hold values from -4 to 4
- cotangent: float32 [32, 768, 1152], P('fsdp', 'tp'), may hold values from -6 to 6
Outputs:
- result: float32 [32, 768, 1152], P('fsdp', 'tp')
- residual_grad: float32 [32, 768, 1152], P('fsdp', 'tp')
- query_grad: float32 [1152, 1152], P('fsdp', 'tp')
- key_grad: float32 [1152, 1152], P('fsdp', 'tp')
- value_grad: float32 [1152, 1152], P('fsdp', 'tp')
- out_grad: float32 [1152, 1152], P('tp', 'fsdp')
- up_grad: float32 [1152, 4304], P('fsdp', 'tp')
- down_grad: float32 [4304, 1152], P('tp', 'fsdp')
- pregain_grad: float32 [1152], replicated
- preshift_grad: float32 [1152], replicated
- querybias_grad: float32 [1152], replicated
- valuebias_grad: float32 [1152], replicated
- outbias_grad: float32 [1152], replicated
- midgain_grad: float32 [1152], replicated
- midshift_grad: float32 [1152], replicated
- upbias_grad: float32 [4304], replicated
- downbias_grad: float32 [1152], replicated
The draws below stay inside these ranges and needn't reach their ends.
Inputs may be any that keep to these rules, and one draw needn't show every extreme that they name: `valid_keys`: each image has exactly 729 positions equal to 1, the others 0.
All inputs are finite; a program needn't handle non-finite values.
Results may differ from the reference program's by a relative error of at most 0.011.
The reference program's roundings to bfloat16 on the way count: a program that leaves them out, or rounds other values in their place, can miss the bound.
Values may be sent and summed in bfloat16 or wider, within the bound.
A program may use at most 192 MiB of HBM per device.

```python
import math
import jax
import jax.numpy as jnp
from jax import lax

D = 1152
HEADS = 16
FF = 4304
VALID = 729
SEQ = 768
HD = 72
IMAGES = 32


def draw_residual(key, part):
    full_shape = (IMAGES, SEQ, D)
    col_scale = jnp.exp(jax.random.uniform(jax.random.fold_in(key, 2), (D,), jnp.float32, math.log(0.3), math.log(3.0)))
    row_scale = jnp.exp(jax.random.uniform(jax.random.fold_in(key, 3), (IMAGES, SEQ, 1), jnp.float32, math.log(0.3), math.log(3.0)))
    entries = jnp.clip(jax.random.normal(jax.random.fold_in(key, 1), full_shape, jnp.float32), -6.0, 6.0)
    return entries * col_scale * row_scale


def attention_pair(key):
    query_base = jnp.clip(jax.random.normal(jax.random.fold_in(key, 7), (D, D), jnp.float32), -6.0, 6.0) / math.sqrt(D)
    key_base = jnp.clip(jax.random.normal(jax.random.fold_in(key, 8), (D, D), jnp.float32), -6.0, 6.0) / math.sqrt(D)
    query_draw = query_base
    key_draw = key_base
    return (jnp.clip(query_draw, -2.0, 2.0), jnp.clip(key_draw, -2.0, 2.0))


def draw_query_weight(key, part):
    return attention_pair(key)[0].astype(jnp.bfloat16)


def draw_key_weight(key, part):
    return attention_pair(key)[1].astype(jnp.bfloat16)


def draw_valid_keys(key, part):
    subkeys = jax.random.split(jax.random.fold_in(key, 5), IMAGES)
    orders = jax.vmap(lambda single: jax.random.permutation(single, SEQ))(subkeys)
    return (orders < VALID).astype(jnp.int32)


def raised(result, rng, source, target, shards_of, factor):
    def block_of(axis_at):
        return (jnp.arange(result.shape[axis_at]) // (result.shape[axis_at] // shards_of)).reshape((-1,) + (1,) * (result.ndim - 1 - axis_at))

    one_side = jax.random.permutation(rng, shards_of)[block_of(target)]
    second = (block_of(target) + shards_of // 2) % shards_of
    return jnp.where((block_of(source) == one_side) | (block_of(source) == second), factor * result, result)


def block_levels(key, dims, cuts, least, top_value):
    def one(axis_at, shards_of):
        heights = jax.random.uniform(jax.random.fold_in(jax.random.fold_in(key, 6), axis_at), (shards_of,), jnp.float32, least / len(cuts), top_value / len(cuts))
        return jnp.repeat(jnp.exp(heights), dims[axis_at] // shards_of).reshape((-1,) + (1,) * (len(dims) - axis_at - 1))

    gain = one(*cuts[0])
    for cut in cuts[1:]:
        gain = gain * one(*cut)
    return gain


def scatter_about(rng, shape, scale, reach, cuts=(), held_as=jnp.bfloat16):
    drawn = jax.random.normal(rng, shape, jnp.float32) * scale
    if len(cuts) > 0:
        drawn = block_levels(rng, shape, cuts, -0.22, 0.18) * drawn
    return jnp.clip(drawn, min=-reach, max=reach).astype(held_as)


def bell_draw_with(own_key, shape, scale, reach, shards, heavy, dtype=jnp.bfloat16):
    array = scale * jax.random.normal(own_key, shape, jnp.float32)
    if shards:
        array = array * block_levels(own_key, shape, shards, -0.22, 0.18)
    return jnp.clip(raised(array, jax.random.fold_in(own_key, 3), *heavy), -reach, reach).astype(dtype)


def setup_inputs(seed: int = 0) -> dict:
    splits = jax.random.split(jax.random.key(seed), 19)
    residual = draw_residual(jax.random.fold_in(splits[18], 71), 0)
    valid_keys = draw_valid_keys(jax.random.fold_in(splits[18], 71), 0)
    pre_gain = jnp.clip(1.0 + 0.18 * jax.random.normal(splits[2], (D,), jnp.float32), 0.1, 1.9)
    pre_shift = scatter_about(splits[3], (D,), 0.3, 4.0, (), jnp.float32)
    query_weight = draw_query_weight(jax.random.fold_in(splits[18], 71), 0)
    query_bias = scatter_about(splits[5], (D,), 0.3, 4.0, (), jnp.float32)
    key_weight = draw_key_weight(jax.random.fold_in(splits[18], 71), 0)
    value_weight = scatter_about(splits[7], (D, D), D ** -0.5, 0.1875, ((0, 32), (1, 4)))
    value_bias = scatter_about(splits[8], (D,), 0.03, 0.4375, (), jnp.float32)
    out_weight = scatter_about(splits[9], (D, D), (D * 16 // VALID) ** -0.5, 1.25, ((0, 4), (1, 32)))
    out_bias = scatter_about(splits[10], (D,), 0.3, 4.0, (), jnp.float32)
    mid_gain = jnp.clip(1.0 + 0.18 * jax.random.normal(splits[11], (D,), jnp.float32), 0.1, 1.9)
    mid_shift = scatter_about(splits[12], (D,), 0.3, 4.0, (), jnp.float32)
    up_weight = scatter_about(splits[13], (D, FF), D ** -0.5, 0.1875, ((0, 32), (1, 4)))
    up_bias = scatter_about(splits[14], (FF,), 0.3, 4.0, (), jnp.float32)
    down_weight = scatter_about(splits[15], (FF, D), FF ** -0.5, 0.09375, ((0, 4), (1, 32)))
    down_bias = scatter_about(splits[16], (D,), 0.3, 4.0, (), jnp.float32)
    cotangent = bell_draw_with(splits[17], (IMAGES, SEQ, D), 1.0, 6.0, ((0, 32), (1, 4)), (0, 2, 32, 2.75), jnp.float32)
    return {"residual": residual, "valid_keys": valid_keys, "pre_gain": pre_gain, "pre_shift": pre_shift, "query_weight": query_weight, "query_bias": query_bias, "key_weight": key_weight, "value_weight": value_weight, "value_bias": value_bias, "out_weight": out_weight, "out_bias": out_bias, "mid_gain": mid_gain, "mid_shift": mid_shift, "up_weight": up_weight, "up_bias": up_bias, "down_weight": down_weight, "down_bias": down_bias, "cotangent": cotangent}


EPS = 1e-06
GELU_C = math.sqrt(2.0 / math.pi)
CUBIC = 0.044715

def layer_norm(stream, gain_vec, shift_vec):
    average = lax.optimization_barrier(jnp.mean(stream, -1, keepdims=True))
    centered = stream - average
    variance = lax.optimization_barrier(jnp.mean(centered * centered, -1, keepdims=True))
    inverse = lax.rsqrt(variance + EPS)
    normed = centered * inverse
    return (normed * gain_vec + shift_vec, normed, inverse)

def norm_back(upstream, normed, inverse, gain_vec):
    scaled = upstream * gain_vec
    return inverse * (scaled - lax.optimization_barrier(jnp.mean(scaled, -1, keepdims=True)) - normed * lax.optimization_barrier(jnp.mean(scaled * normed, -1, keepdims=True)))

def gelu_tanh(pre_act):
    tangent = jnp.tanh(GELU_C * (pre_act + CUBIC * pre_act * pre_act * pre_act))
    return 0.5 * pre_act * (1.0 + tangent)

def gelu_slope(pre_act):
    tangent = jnp.tanh(GELU_C * (pre_act + CUBIC * pre_act * pre_act * pre_act))
    return 0.5 * (1.0 + tangent) + 0.5 * pre_act * (1.0 - tangent * tangent) * GELU_C * (1.0 + 3.0 * CUBIC * pre_act * pre_act)

def rounded(values):
    return lax.optimization_barrier(values.astype(jnp.bfloat16)).astype(jnp.float32)

def reference(residual, valid_keys, pre_gain, pre_shift, query_weight, query_bias, key_weight, value_weight, value_bias, out_weight, out_bias, mid_gain, mid_shift, up_weight, up_bias, down_weight, down_bias, cotangent):
    score_scale = 1.0 / math.sqrt(HD)

    def attention_scores(query_heads, key_heads, key_live):
        scores = jnp.einsum('qhd,khd->hqk', query_heads, key_heads) * score_scale
        return jnp.where(key_live, scores, -jnp.inf)

    def one_image(totals, inputs):
        stream, valid_row, upstream = inputs
        key_live = (valid_row > 0)[None, None, :]
        attn_float, pre_normed, pre_rstd = layer_norm(stream, pre_gain, pre_shift)
        attn_in = attn_float.astype(jnp.bfloat16)
        queries = (jnp.dot(attn_in, query_weight, preferred_element_type=jnp.float32) + query_bias).astype(jnp.bfloat16)
        keys_all = jnp.dot(attn_in, key_weight, preferred_element_type=jnp.float32).astype(jnp.bfloat16)
        values_all = (jnp.dot(attn_in, value_weight, preferred_element_type=jnp.float32) + value_bias).astype(jnp.bfloat16)
        query_heads = lax.optimization_barrier(queries).astype(jnp.float32).reshape(SEQ, HEADS, HD)
        key_heads = lax.optimization_barrier(keys_all).astype(jnp.float32).reshape(SEQ, HEADS, HD)
        value_heads = lax.optimization_barrier(values_all).astype(jnp.float32).reshape(SEQ, HEADS, HD)
        scores = attention_scores(query_heads, key_heads, key_live)
        maximum = lax.optimization_barrier(jnp.max(scores, -1, keepdims=True))
        logsum = maximum + jnp.log(lax.optimization_barrier(jnp.sum(jnp.exp(scores - maximum), -1, keepdims=True)))
        attn_probs = jnp.exp(scores - logsum)
        mixed_heads = jnp.einsum('hqk,khd->qhd', rounded(attn_probs), value_heads).reshape(SEQ, D).astype(jnp.bfloat16)
        midstream = stream + jnp.dot(mixed_heads, out_weight, preferred_element_type=jnp.float32) + out_bias
        mlp_float, mid_normed, mid_rstd = layer_norm(midstream, mid_gain, mid_shift)
        mlp_in = mlp_float.astype(jnp.bfloat16)
        pre_act = jnp.dot(mlp_in, up_weight, preferred_element_type=jnp.float32) + up_bias
        hidden = gelu_tanh(pre_act).astype(jnp.bfloat16)
        block_out = midstream + jnp.dot(hidden, down_weight, preferred_element_type=jnp.float32) + down_bias
        cot_low = upstream.astype(jnp.bfloat16)
        down_term = jnp.dot(hidden.T, cot_low, preferred_element_type=jnp.float32)
        act_grad = jnp.dot(cot_low, down_weight.T, preferred_element_type=jnp.float32) * gelu_slope(pre_act)
        act_low = act_grad.astype(jnp.bfloat16)
        up_term = jnp.dot(mlp_in.T, act_low, preferred_element_type=jnp.float32)
        mlp_in_grad = jnp.dot(act_low, up_weight.T, preferred_element_type=jnp.float32)
        mid_grad = upstream + norm_back(mlp_in_grad, mid_normed, mid_rstd, mid_gain)
        mid_low = mid_grad.astype(jnp.bfloat16)
        out_term = jnp.dot(mixed_heads.T, mid_low, preferred_element_type=jnp.float32)
        mixed_grad = rounded(jnp.dot(mid_low, out_weight.T, preferred_element_type=jnp.float32)).reshape(SEQ, HEADS, HD)
        scores_again = attention_scores(query_heads, key_heads, key_live)
        probs_again = jnp.exp(scores_again - logsum)
        value_rows_grad = jnp.einsum('hqk,qhd->khd', rounded(probs_again), mixed_grad)
        prob_grad = jnp.einsum('qhd,khd->hqk', mixed_grad, value_heads)
        delta_rows = lax.optimization_barrier(jnp.sum(probs_again * prob_grad, -1, keepdims=True))
        score_grad = rounded(probs_again * (prob_grad - delta_rows) * score_scale)
        query_rows_grad = jnp.einsum('hqk,khd->qhd', score_grad, key_heads).reshape(SEQ, D)
        key_rows_grad = jnp.einsum('hqk,qhd->khd', score_grad, query_heads).reshape(SEQ, D)
        value_rows_grad = value_rows_grad.reshape(SEQ, D)
        query_low = query_rows_grad.astype(jnp.bfloat16)
        key_low = key_rows_grad.astype(jnp.bfloat16)
        value_low = value_rows_grad.astype(jnp.bfloat16)
        query_term = jnp.dot(attn_in.T, query_low, preferred_element_type=jnp.float32)
        key_term = jnp.dot(attn_in.T, key_low, preferred_element_type=jnp.float32)
        value_term = jnp.dot(attn_in.T, value_low, preferred_element_type=jnp.float32)
        attn_in_grad = jnp.dot(query_low, query_weight.T, preferred_element_type=jnp.float32) + jnp.dot(key_low, key_weight.T, preferred_element_type=jnp.float32) + jnp.dot(value_low, value_weight.T, preferred_element_type=jnp.float32)
        input_grad = mid_grad + norm_back(attn_in_grad, pre_normed, pre_rstd, pre_gain)
        terms = (query_term, key_term, value_term, out_term, up_term, down_term, lax.optimization_barrier(jnp.sum(attn_in_grad * pre_normed, 0)), lax.optimization_barrier(jnp.sum(attn_in_grad, 0)), lax.optimization_barrier(jnp.sum(query_rows_grad, 0)), lax.optimization_barrier(jnp.sum(value_rows_grad, 0)), lax.optimization_barrier(jnp.sum(mid_grad, 0)), lax.optimization_barrier(jnp.sum(mlp_in_grad * mid_normed, 0)), lax.optimization_barrier(jnp.sum(mlp_in_grad, 0)), lax.optimization_barrier(jnp.sum(act_grad, 0)), lax.optimization_barrier(jnp.sum(upstream, 0)))
        totals = jax.tree.map(lambda running, addend: running + addend, totals, terms)
        return (totals, (block_out, input_grad))
    square = jnp.zeros((D, D), jnp.float32)
    vector_d = jnp.zeros((D,), jnp.float32)
    start_totals = (square, square, square, square, jnp.zeros((D, FF), jnp.float32), jnp.zeros((FF, D), jnp.float32), vector_d, vector_d, vector_d, vector_d, vector_d, vector_d, vector_d, jnp.zeros((FF,), jnp.float32), vector_d)
    totals, (outputs, input_grads) = lax.scan(one_image, start_totals, (residual, valid_keys, cotangent))
    return (outputs, input_grads, totals[0], totals[1], totals[2], totals[3], totals[4], totals[5], totals[6], totals[7], totals[8], totals[9], totals[10], totals[11], totals[12], totals[13], totals[14])
```

```python
import math

import jax
import jax.numpy as jnp
from jax import lax
from jax.experimental import pallas as pl
from jax.experimental.pallas import tpu as pltpu
from jax.sharding import Mesh
from jax.sharding import PartitionSpec as P

HD = 72
D = 1152
ROWS = 192
SHARD = 36
MAIN = 32
QKV = 896
OUT = 384
HID = 1152
WIDE = QKV + OUT + 2 * HID
TAIL = 512
PACKED = WIDE + TAIL
HALF = PACKED // 2
EPS = 1e-06
GELU_C = math.sqrt(2.0 / math.pi)
CUBIC = 0.044715
SIZE = {"yl": 2, "z": 4, "x": 4, "yh": 2, "c": 2}
FSDP = ("yl", "z", "x")
TP = ("yh", "c")
MESH = pl.DeviceIdType.MESH
BF = jnp.bfloat16
F32 = jnp.float32
SECTIONS = ((0, QKV), (QKV, QKV + OUT), (QKV + OUT, QKV + OUT + HID), (QKV + OUT + HID, WIDE))
NEAR = (1, 3, 2)


def ahead(axis, step):
    return lax.rem(lax.axis_index(axis) + step, SIZE[axis])


def peer(axis, step=1):
    return {axis: ahead(axis, step)}


def greet(pairs):
    barrier = pltpu.get_barrier_semaphore()
    for axis, step in pairs:
        pl.semaphore_signal(barrier, inc=1, device_id=peer(axis, step), device_id_type=MESH)
    pl.semaphore_wait(barrier, len(pairs))


TP_PAIRS = (("c", 1), ("yh", 1))
ALL_PAIRS = TP_PAIRS + (("yl", 1),) + tuple((a, s) for a in ("x", "z") for s in NEAR)


def send(src, dst, sems, k, axis, step=1):
    copy = pltpu.make_async_remote_copy(
        src_ref=src,
        dst_ref=dst,
        send_sem=sems.at[0, k],
        recv_sem=sems.at[1, k],
        device_id=peer(axis, step),
        device_id_type=MESH,
    )
    copy.start()
    return copy


def ranks():
    yh, c = lax.axis_index("yh"), lax.axis_index("c")
    return yh * 2 + c, (1 - yh) * 2 + c, yh * 2 + 1 - c, (1 - yh) * 2 + 1 - c


def rows_out(src, rows, sems):
    mine = ranks()[0]
    return [
        send(src, rows.at[mine], sems, 0, "yh"),
        send(src, rows.at[mine], sems, 1, "c"),
    ]


def rows_forward(copies, rows, sems):
    over = ranks()[1]
    copies[0].wait_recv()
    copies.append(send(rows.at[over], rows.at[over], sems, 2, "c"))


def rows_end(copies):
    copies[0].wait_send()
    copies[1].wait()
    copies[2].wait()


class TpSum:
    def __init__(self, part, first, second, out, sems):
        self.part, self.first, self.second, self.out, self.sems = part, first, second, out, sems

    def start(self):
        _, _, sib, cross = ranks()
        self.cross = send(self.part.at[cross], self.first.at[0], self.sems, 0, "c")
        self.sib = send(self.part.at[sib], self.first.at[1], self.sems, 1, "c")

    def middle(self):
        over = ranks()[1]
        self.cross.wait_recv()
        self.out[...] = (self.part[over].astype(F32) + self.first[0].astype(F32)).astype(BF)
        self.over = send(self.out, self.second, self.sems, 2, "yh")

    def total(self):
        mine = ranks()[0]
        self.sib.wait_recv()
        self.over.wait_recv()
        return (
            self.part[mine].astype(F32) + self.first[1].astype(F32) + self.second[...].astype(F32)
        )

    def end(self):
        self.cross.wait_send()
        self.sib.wait_send()
        self.over.wait_send()


def tp_sum_scratch():
    return [
        pltpu.VMEM((2, ROWS, D), BF),
        pltpu.VMEM((ROWS, D), BF),
        pltpu.VMEM((ROWS, D), BF),
        pltpu.SemaphoreType.DMA((2, 3)),
    ]


def layer_norm(stream):
    average = jnp.mean(stream, -1, keepdims=True)
    centered = stream - average
    variance = jnp.mean(centered * centered, -1, keepdims=True)
    inverse = lax.rsqrt(variance + EPS)
    return centered * inverse, inverse


def norm_back(upstream, normed, inverse, gain_vec):
    scaled = upstream * gain_vec
    return inverse * (
        scaled
        - jnp.mean(scaled, -1, keepdims=True)
        - normed * jnp.mean(scaled * normed, -1, keepdims=True)
    )


def gather_kernel(w, a, c, wqkv, wout, wup, wdown, arows, crows, held, s0, sa, sb, s1, s2):
    yl, z, x = lax.axis_index("yl"), lax.axis_index("z"), lax.axis_index("x")
    mine = ranks()[0]
    greet(ALL_PAIRS)
    first = send(w, held.at[yl, z, x], s0, 0, "yl")
    ca = rows_out(a, arows, s1)
    cc = rows_out(c, crows, s2)
    held[yl, z, x] = w[...]
    arows[mine] = a[...]
    crows[mine] = c[...]
    first.wait_recv()
    lo, hi = pl.ds(0, HALF), pl.ds(HALF, HALF)
    one = []
    for k, step in enumerate(NEAR):
        blk = held.at[:, z, x, :, lo]
        one.append(send(blk, blk, sa, k, "x", step))
        blk = held.at[:, z, x, :, hi]
        one.append(send(blk, blk, sb, k, "z", step))
    rows_forward(ca, arows, s1)
    for copy in one:
        copy.wait_recv()
    two = []
    for k, step in enumerate(NEAR):
        blk = held.at[:, z, :, :, lo]
        two.append(send(blk, blk, sa, 3 + k, "z", step))
        blk = held.at[:, :, x, :, hi]
        two.append(send(blk, blk, sb, 3 + k, "x", step))
    rows_forward(cc, crows, s2)
    for copy in two:
        copy.wait_recv()
    for i in range(32):
        at = (i // 16, (i // 4) % 4, i % 4)
        for ref, (b, e) in zip((wqkv, wout, wup, wdown), SECTIONS):
            ref[SHARD * i : SHARD * i + MAIN, :] = held[at[0], at[1], at[2], :, b:e]
            j = b
            while j < e:
                piece = j // TAIL
                stop = min(e, (piece + 1) * TAIL)
                ref[SHARD * i + MAIN : SHARD * (i + 1), j - b : stop - b] = held[
                    at[0],
                    at[1],
                    at[2],
                    4 * piece : 4 * piece + 4,
                    WIDE + j - piece * TAIL : WIDE + stop - piece * TAIL,
                ]
                j = stop
    first.wait_send()
    for copy in one + two:
        copy.wait_send()
    rows_end(ca)
    rows_end(cc)


def mid_kernel(part, stream, bias, gain, shift, midstream, rows, f1, f2, f3, ss, own, sr):
    mine = ranks()[0]
    greet(TP_PAIRS)
    job = TpSum(part, f1, f2, f3, ss)
    job.start()
    job.middle()
    mid = stream[...] + job.total() + bias[...]
    midstream[...] = mid
    normed, _ = layer_norm(mid)
    low = (normed * gain[...] + shift[...]).astype(BF)
    own[...] = low
    rows[mine] = low
    copies = rows_out(own, rows, sr)
    rows_forward(copies, rows, sr)
    rows_end(copies)
    job.end()


def back_kernel(part, midstream, upstream, gain, mid_grad, vecs, rows, f1, f2, f3, ss, own, sr):
    mine = ranks()[0]
    greet(TP_PAIRS)
    job = TpSum(part, f1, f2, f3, ss)
    job.start()
    job.middle()
    normed, inverse = layer_norm(midstream[...])
    grad = job.total()
    back = upstream[...] + norm_back(grad, normed, inverse, gain[...])
    mid_grad[...] = back
    low = back.astype(BF)
    own[...] = low
    rows[mine] = low
    copies = rows_out(own, rows, sr)
    vecs[...] = jnp.concatenate(
        [
            jnp.sum(back, 0, keepdims=True),
            jnp.sum(grad * normed, 0, keepdims=True),
            jnp.sum(grad, 0, keepdims=True),
            jnp.sum(upstream[...], 0, keepdims=True),
            jnp.zeros((4, D), F32),
        ],
        0,
    )
    rows_forward(copies, rows, sr)
    rows_end(copies)
    job.end()


def tail_kernel(
    gqkv, gout, gup, gdown, apart, dpart, stream, mid_grad, midstream, gain, dbias, vec_in,
    grads, block_out, input_grad, vecs,
    held, ra1, rb1, qa, qb, ra2, rb2, ta, tb, ra3, rb3, sa, sb,
    f1, f2, f3, ss, h1, h2, h3, hs, vown, varr, sv,
):
    yl, z, x = lax.axis_index("yl"), lax.axis_index("z"), lax.axis_index("x")
    greet(ALL_PAIRS)
    att = TpSum(apart, f1, f2, f3, ss)
    att.start()
    down = TpSum(dpart, h1, h2, h3, hs)
    down.start()
    for i in range(32):
        at = (i // 16, (i // 4) % 4, i % 4)
        for ref, (b, e) in zip((gqkv, gout, gup, gdown), SECTIONS):
            held[at[0], at[1], at[2], :, b:e] = ref[SHARD * i : SHARD * i + MAIN, :].astype(BF)
            j = b
            while j < e:
                piece = j // TAIL
                stop = min(e, (piece + 1) * TAIL)
                held[
                    at[0],
                    at[1],
                    at[2],
                    4 * piece : 4 * piece + 4,
                    WIDE + j - piece * TAIL : WIDE + stop - piece * TAIL,
                ] = ref[SHARD * i + MAIN : SHARD * (i + 1), j - b : stop - b].astype(BF)
                j = stop
        held[at[0], at[1], at[2], 28:32, WIDE:PACKED] = jnp.zeros((4, TAIL), BF)
    lo, hi = pl.ds(0, HALF), pl.ds(HALF, HALF)
    one = []
    for k, step in enumerate(NEAR):
        one.append(send(held.at[:, ahead("z", step), :, :, lo], ra1.at[k], sa, k, "z", step))
        one.append(send(held.at[:, :, ahead("x", step), :, hi], rb1.at[k], sb, k, "x", step))
    att.middle()
    normed, inverse = layer_norm(stream[...])
    grad = att.total()
    input_grad[...] = mid_grad[...] + norm_back(grad, normed, inverse, gain[...])
    vown[0] = vec_in[...]
    vown[0, 0:1, :] = jnp.sum(grad * normed, 0, keepdims=True)
    vown[0, 1:2, :] = jnp.sum(grad, 0, keepdims=True)
    vc = [send(vown.at[0], varr.at[0], sv, 0, "c")]
    down.middle()
    vc[0].wait_recv()
    vown[1] = vown[0] + varr[0]
    vc.append(send(vown.at[1], varr.at[1], sv, 1, "yh"))
    for copy in one:
        copy.wait_recv()

    def add_one(n, carry):
        a, b = n // 4, n % 4
        at_a = held[a, z, b, :, :HALF].astype(F32)
        at_b = held[a, b, x, :, HALF:].astype(F32)
        for k in range(3):
            at_a = at_a + ra1[k, a, b].astype(F32)
            at_b = at_b + rb1[k, a, b].astype(F32)
        qa[a, b] = at_a.astype(BF)
        qb[a, b] = at_b.astype(BF)
        return carry

    lax.fori_loop(0, 8, add_one, 0)
    two = []
    for k, step in enumerate(NEAR):
        two.append(send(qa.at[:, ahead("x", step)], ra2.at[k], sa, 3 + k, "x", step))
        two.append(send(qb.at[:, ahead("z", step)], rb2.at[k], sb, 3 + k, "z", step))
    block_out[...] = midstream[...] + down.total() + dbias[...]
    vc[1].wait_recv()
    vown[2] = vown[1] + varr[1]
    vc.append(send(vown.at[2], varr.at[2], sv, 2, "yl"))
    for copy in two:
        copy.wait_recv()
    for a in range(2):
        at_a = qa[a, x].astype(F32)
        at_b = qb[a, z].astype(F32)
        for k in range(3):
            at_a = at_a + ra2[k, a].astype(F32)
            at_b = at_b + rb2[k, a].astype(F32)
        ta[a] = at_a.astype(BF)
        tb[a] = at_b.astype(BF)
    three = [
        send(ta.at[1 - yl], ra3, sa, 6, "yl"),
        send(tb.at[1 - yl], rb3, sb, 6, "yl"),
    ]
    vc[2].wait_recv()
    vown[3] = vown[2] + varr[2]
    for k, step in enumerate(NEAR):
        vc.append(send(vown.at[3], varr.at[3 + x], sv, 3 + k, "x", step))
    varr[3 + x] = vown[3]
    for copy in three:
        copy.wait_recv()
    fa = ta[yl].astype(F32) + ra3[...].astype(F32)
    fb = tb[yl].astype(F32) + rb3[...].astype(F32)
    grads[0:MAIN, 0:HALF] = fa
    grads[0:MAIN, HALF:WIDE] = fb[:, : WIDE - HALF]
    for j in range(WIDE // TAIL):
        grads[MAIN:SHARD, j * TAIL : (j + 1) * TAIL] = fb[4 * j : 4 * j + 4, WIDE - HALF :]
    for copy in vc[3:6]:
        copy.wait_recv()
    vown[4] = varr[3] + varr[4] + varr[5] + varr[6]
    for k, step in enumerate(NEAR):
        vc.append(send(vown.at[4], varr.at[7 + z], sv, 6 + k, "z", step))
    varr[7 + z] = vown[4]
    for copy in vc[6:9]:
        copy.wait_recv()
    vecs[...] = varr[7] + varr[8] + varr[9] + varr[10]
    for copy in vc + one + two + three:
        copy.wait_send()
    att.end()
    down.end()


def call(kernel, name, cid, outs, scratch, *args):
    vm = pl.BlockSpec(memory_space=pltpu.VMEM)
    return pl.pallas_call(
        kernel,
        name=name,
        out_shape=[jax.ShapeDtypeStruct(s, t) for s, t in outs],
        in_specs=[vm] * len(args),
        out_specs=[vm] * len(outs),
        scratch_shapes=scratch,
        compiler_params=pltpu.CompilerParams(
            collective_id=cid, has_side_effects=True, vmem_limit_bytes=60 * 2**20
        ),
    )(*args)


def pad_lanes(a, width):
    return jnp.pad(a, ((0, 0), (0, width - a.shape[1])))


def pack(wq, wk, wv, wo, wu, wd):
    flat = jnp.concatenate(
        [
            wq,
            wk,
            wv,
            jnp.zeros((SHARD, QKV - 864), BF),
            pad_lanes(wo.T, OUT),
            pad_lanes(wu, HID),
            pad_lanes(wd.T, HID),
        ],
        1,
    )
    tail = flat[MAIN:].reshape(4, WIDE // TAIL, TAIL).transpose(1, 0, 2).reshape(-1, TAIL)
    tail = jnp.pad(tail, ((0, MAIN - tail.shape[0]), (0, 0)))
    return jnp.concatenate([flat[:MAIN], tail], 1)


def gelu_parts(pre_act):
    tangent = jnp.tanh(GELU_C * (pre_act + CUBIC * pre_act * pre_act * pre_act))
    value = 0.5 * pre_act * (1.0 + tangent)
    slope = 0.5 * (1.0 + tangent) + 0.5 * pre_act * (1.0 - tangent * tangent) * GELU_C * (
        1.0 + 3.0 * CUBIC * pre_act * pre_act
    )
    return value, slope


def dot(a, b, spec):
    return jnp.einsum(spec, a, b, preferred_element_type=F32)


def per_device(
    residual, valid_keys, pre_gain, pre_shift, query_weight, query_bias, key_weight, value_weight,
    value_bias, out_weight, out_bias, mid_gain, mid_shift, up_weight, up_bias, down_weight,
    down_bias, cotangent,
):
    rank = lax.axis_index(TP)
    stream, upstream = residual[0], cotangent[0]
    seq, heads, cols, hid = 768, 4, 288, 1076
    row = lambda v: v.reshape(1, -1)
    bias_query = lax.dynamic_slice_in_dim(query_bias, rank * cols, cols)
    bias_value = lax.dynamic_slice_in_dim(value_bias, rank * cols, cols)
    bias_hidden = jnp.pad(lax.dynamic_slice_in_dim(up_bias, rank * hid, hid), (0, HID - hid))
    bias_qkv = jnp.concatenate(
        [bias_query, jnp.zeros((cols,), F32), bias_value, jnp.zeros((QKV - 3 * cols,), F32)]
    )
    key_live = (valid_keys[0] > 0)[None, None, :]
    scale = 1.0 / math.sqrt(HD)
    packed = pack(query_weight, key_weight, value_weight, out_weight, up_weight, down_weight)
    pre_normed, _ = layer_norm(stream)
    low = (pre_normed * pre_gain + pre_shift).astype(BF)
    wqkv, wout, wup, wdown, attn_rows, cot_rows = call(
        gather_kernel,
        "gather",
        0,
        [
            ((D, QKV), BF),
            ((D, OUT), BF),
            ((D, HID), BF),
            ((D, HID), BF),
            ((4, ROWS, D), BF),
            ((4, ROWS, D), BF),
        ],
        [
            pltpu.VMEM((2, 4, 4, MAIN, PACKED), BF),
            pltpu.SemaphoreType.DMA((2, 1)),
            pltpu.SemaphoreType.DMA((2, 6)),
            pltpu.SemaphoreType.DMA((2, 6)),
            pltpu.SemaphoreType.DMA((2, 3)),
            pltpu.SemaphoreType.DMA((2, 3)),
        ],
        packed,
        low,
        upstream.astype(BF),
    )
    attn_rows = attn_rows.reshape(seq, D)
    cot_rows = cot_rows.reshape(seq, D)
    qkv = (dot(attn_rows, wqkv, "sd,dc->sc") + bias_qkv).astype(BF)
    qh = qkv[:, :cols].reshape(seq, heads, HD)
    kh = qkv[:, cols : 2 * cols].reshape(seq, heads, HD)
    vh = qkv[:, 2 * cols : 3 * cols].reshape(seq, heads, HD)
    scores = jnp.where(key_live, dot(qh, kh, "qhd,khd->hqk") * scale, -jnp.inf)
    maximum = jnp.max(scores, -1, keepdims=True)
    logsum = maximum + jnp.log(jnp.sum(jnp.exp(scores - maximum), -1, keepdims=True))
    probs = jnp.exp(scores - logsum)
    mixed = dot(probs.astype(BF), vh, "hqk,khd->qhd").reshape(seq, cols).astype(BF)
    mixed = pad_lanes(mixed, OUT)
    out_part = dot(mixed, wout, "sc,dc->sd").astype(BF).reshape(4, ROWS, D)
    midstream, mlp_rows = call(
        mid_kernel,
        "middle",
        1,
        [((ROWS, D), F32), ((4, ROWS, D), BF)],
        tp_sum_scratch() + [pltpu.VMEM((ROWS, D), BF), pltpu.SemaphoreType.DMA((2, 3))],
        out_part,
        stream,
        row(out_bias),
        row(mid_gain),
        row(mid_shift),
    )
    mlp_rows = mlp_rows.reshape(seq, D)
    pre_act = dot(mlp_rows, wup, "sd,df->sf") + bias_hidden
    value, slope = gelu_parts(pre_act)
    hidden = value.astype(BF)
    act_grad = dot(cot_rows, wdown, "sd,df->sf") * slope
    act_low = act_grad.astype(BF)
    mlp_part = dot(act_low, wup, "sf,df->sd").astype(BF).reshape(4, ROWS, D)
    mid_grad, vec_mid, mid_rows = call(
        back_kernel,
        "back",
        2,
        [((ROWS, D), F32), ((8, D), F32), ((4, ROWS, D), BF)],
        tp_sum_scratch() + [pltpu.VMEM((ROWS, D), BF), pltpu.SemaphoreType.DMA((2, 3))],
        mlp_part,
        midstream,
        upstream,
        row(mid_gain),
    )
    mid_rows = mid_rows.reshape(seq, D)
    down_part = dot(hidden, wdown, "sf,df->sd").astype(BF).reshape(4, ROWS, D)
    gup = dot(mlp_rows, act_low, "sd,sf->df")
    gdown = dot(cot_rows, hidden, "sd,sf->df")
    gout = dot(mid_rows, mixed, "sd,sc->dc")
    mixed_grad = dot(mid_rows, wout, "sd,dc->sc")[:, :cols].astype(BF).reshape(seq, heads, HD)
    low_probs = probs.astype(BF)
    dv = dot(low_probs, mixed_grad, "hqk,qhd->khd").reshape(seq, cols)
    prob_grad = dot(mixed_grad, vh, "qhd,khd->hqk")
    delta = jnp.sum(probs * prob_grad, -1, keepdims=True)
    score_grad = (probs * (prob_grad - delta) * scale).astype(BF)
    dq = dot(score_grad, kh, "hqk,khd->qhd").reshape(seq, cols)
    dk = dot(score_grad, qh, "hqk,qhd->khd").reshape(seq, cols)
    dqkv = jnp.concatenate([dq, dk, dv, jnp.zeros((seq, QKV - 3 * cols), F32)], 1).astype(BF)
    gqkv = dot(attn_rows, dqkv, "sd,sc->dc")
    attn_part = dot(dqkv, wqkv, "sc,dc->sd").astype(BF).reshape(4, ROWS, D)

    def place(v, total, offset):
        return lax.dynamic_update_slice(jnp.zeros((total,), F32), v, (offset,))

    vec_in = jnp.concatenate(
        [
            jnp.zeros((2, D), F32),
            row(place(jnp.sum(dq, 0), D, rank * cols)),
            row(place(jnp.sum(dv, 0), D, rank * cols)),
            vec_mid[:4],
            place(jnp.sum(act_grad, 0), 4 * HID, rank * HID).reshape(4, HID),
            jnp.zeros((4, D), F32),
        ],
        0,
    )
    half_blk = (2, 4, MAIN, HALF)
    grads, block_out, input_grad, vecs = call(
        tail_kernel,
        "tail",
        3,
        [((SHARD, WIDE), F32), ((ROWS, D), F32), ((ROWS, D), F32), ((16, D), F32)],
        [
            pltpu.VMEM((2, 4, 4, MAIN, PACKED), BF),
            pltpu.VMEM((3, *half_blk), BF),
            pltpu.VMEM((3, *half_blk), BF),
            pltpu.VMEM(half_blk, BF),
            pltpu.VMEM(half_blk, BF),
            pltpu.VMEM((3, 2, MAIN, HALF), BF),
            pltpu.VMEM((3, 2, MAIN, HALF), BF),
            pltpu.VMEM((2, MAIN, HALF), BF),
            pltpu.VMEM((2, MAIN, HALF), BF),
            pltpu.VMEM((MAIN, HALF), BF),
            pltpu.VMEM((MAIN, HALF), BF),
            pltpu.SemaphoreType.DMA((2, 7)),
            pltpu.SemaphoreType.DMA((2, 7)),
        ]
        + tp_sum_scratch()
        + tp_sum_scratch()
        + [
            pltpu.VMEM((5, 16, D), F32),
            pltpu.VMEM((11, 16, D), F32),
            pltpu.SemaphoreType.DMA((2, 9)),
        ],
        gqkv,
        gout,
        gup,
        gdown,
        attn_part,
        down_part,
        stream,
        mid_grad,
        midstream,
        row(pre_gain),
        row(down_bias),
        vec_in,
    )
    gu = QKV + OUT
    return (
        block_out[None],
        input_grad[None],
        grads[:, :cols],
        grads[:, cols : 2 * cols],
        grads[:, 2 * cols : 3 * cols],
        grads[:, QKV : QKV + cols].T,
        grads[:, gu : gu + hid],
        grads[:, gu + HID : gu + HID + hid].T,
        vecs[0],
        vecs[1],
        vecs[2],
        vecs[3],
        vecs[4],
        vecs[5],
        vecs[6],
        vecs[8:12, :hid].reshape(4 * hid),
        vecs[7],
    )


def solution(mesh):
    split = Mesh(mesh.devices.reshape(2, 4, 4, 2, 2), ("yl", "z", "x", "yh", "c"))
    rows3 = P(FSDP, TP, None)
    down_cols = P(FSDP, TP)
    across = P(TP, FSDP)
    return jax.shard_map(
        per_device,
        mesh=split,
        in_specs=(
            rows3, P(FSDP, None), P(), P(), down_cols, P(), down_cols, down_cols, P(), across,
            P(), P(), P(), down_cols, P(), across, P(), rows3,
        ),
        out_specs=(
            rows3, rows3, down_cols, down_cols, down_cols, across, down_cols, across,
            P(), P(), P(), P(), P(), P(), P(), P(), P(),
        ),
        check_vma=False,
    )
```

```python
import math

import jax
import jax.numpy as jnp
from jax import lax
from jax.experimental import pallas as pl
from jax.experimental.pallas import tpu as pltpu
from jax.sharding import Mesh
from jax.sharding import PartitionSpec as P

HD = 72
HEADS = 4
COLS = HEADS * HD
D = 1152
SEQ = 768
ROWS = 192
CHUNKS = 2
CH = ROWS // CHUNKS
SHARD = 36
MAIN = 32
BAND = 4 * SHARD
QKV = 896
OUT = 384
HID = 1152
TRUE_HID = 1076
QC = 256
EPS = 1e-06
GELU_C = math.sqrt(2.0 / math.pi)
CUBIC = 0.044715
SCALE = 1.0 / math.sqrt(HD)
SIZE = {"yl": 2, "z": 4, "x": 4, "yh": 2, "c": 2}
FSDP = ("yl", "z", "x")
TP = ("yh", "c")
MESH = pl.DeviceIdType.MESH
BF = jnp.bfloat16
F32 = jnp.float32
NEAR = (1, 3, 2)
SPLIT1, PIECE1, WIDE1, PACK1 = ((0, QKV), (QKV, QKV + OUT)), 256, QKV + OUT, QKV + OUT + 256
SPLIT2, PIECE2, WIDE2, PACK2 = ((0, HID), (HID, 2 * HID)), 384, 2 * HID, 2 * HID + 384
CUT1, CUT2 = 768, 1408
TP_PAIRS = (("c", 1), ("yh", 1))
ALL_PAIRS = TP_PAIRS + (("yl", 1),) + tuple((a, s) for a in ("x", "z") for s in NEAR)


def ahead(axis, step):
    return lax.rem(lax.axis_index(axis) + step, SIZE[axis])


def peer(axis, step=1):
    return {axis: ahead(axis, step)}


def greet(pairs):
    barrier = pltpu.get_barrier_semaphore()
    for axis, step in pairs:
        pl.semaphore_signal(barrier, inc=1, device_id=peer(axis, step), device_id_type=MESH)
    pl.semaphore_wait(barrier, len(pairs))


def send(src, dst, sems, k, axis, step=1):
    copy = pltpu.make_async_remote_copy(
        src_ref=src,
        dst_ref=dst,
        send_sem=sems.at[0, k],
        recv_sem=sems.at[1, k],
        device_id=peer(axis, step),
        device_id_type=MESH,
    )
    copy.start()
    return copy


def ranks():
    yh, c = lax.axis_index("yh"), lax.axis_index("c")
    return yh * 2 + c, (1 - yh) * 2 + c, yh * 2 + 1 - c, (1 - yh) * 2 + 1 - c


class RowGather:
    def __init__(self, rows, sems):
        self.rows, self.sems, self.over, self.sib, self.fwd = rows, sems, {}, {}, {}

    def put(self, j):
        blk = self.rows.at[ranks()[0], pl.ds(j * CH, CH)]
        self.over[j] = send(blk, blk, self.sems, 3 * j, "yh")
        self.sib[j] = send(blk, blk, self.sems, 3 * j + 1, "c")

    def forward(self, j):
        blk = self.rows.at[ranks()[1], pl.ds(j * CH, CH)]
        self.over[j].wait_recv()
        self.fwd[j] = send(blk, blk, self.sems, 3 * j + 2, "c")

    def chip(self):
        for j in range(CHUNKS):
            self.sib[j].wait_recv()

    def rest(self):
        for j in range(CHUNKS):
            self.fwd[j].wait_recv()

    def end(self):
        for j in range(CHUNKS):
            self.over[j].wait_send()
            self.sib[j].wait_send()
            self.fwd[j].wait_send()


class TpSum:
    def __init__(self, part, first, second, out, sems):
        self.part, self.first, self.second, self.out, self.sems = part, first, second, out, sems

    def start_cross(self):
        self.cross = send(self.part.at[ranks()[3]], self.first.at[0], self.sems, 0, "c")

    def start_sib(self):
        self.sib = send(self.part.at[ranks()[2]], self.first.at[1], self.sems, 1, "c")

    def middle(self):
        over = ranks()[1]
        self.cross.wait_recv()
        self.over = []
        for j in range(CHUNKS):
            rows = pl.ds(j * CH, CH)
            self.out[rows] = (
                self.part[over, rows].astype(F32) + self.first[0, rows].astype(F32)
            ).astype(BF)
            self.over.append(
                send(self.out.at[rows], self.second.at[rows], self.sems, 2 + j, "yh")
            )

    def total(self, j):
        mine = ranks()[0]
        rows = pl.ds(j * CH, CH)
        if j == 0:
            self.sib.wait_recv()
        self.over[j].wait_recv()
        return (
            self.part[mine, rows].astype(F32)
            + self.first[1, rows].astype(F32)
            + self.second[rows].astype(F32)
        )

    def end(self):
        self.cross.wait_send()
        self.sib.wait_send()
        for copy in self.over:
            copy.wait_send()


class WeightGather:
    def __init__(self, held, cut, s0, sa, sb):
        self.held, self.s0, self.sa, self.sb = held, s0, sa, sb
        self.yl, self.z, self.x = (lax.axis_index(a) for a in FSDP)
        self.lo, self.hi = pl.ds(0, cut), pl.ds(cut, held.shape[-1] - cut)

    def start(self):
        blk = self.held.at[self.yl, self.z, self.x]
        self.zero = send(blk, blk, self.s0, 0, "yl")

    def step1(self):
        self.zero.wait_recv()
        self.one = []
        for k, step in enumerate(NEAR):
            blk = self.held.at[:, self.z, self.x, :, self.lo]
            self.one.append(send(blk, blk, self.sa, k, "x", step))
            blk = self.held.at[:, self.z, self.x, :, self.hi]
            self.one.append(send(blk, blk, self.sb, k, "z", step))

    def step2(self):
        for copy in self.one:
            copy.wait_recv()
        self.two = []
        for k, step in enumerate(NEAR):
            blk = self.held.at[:, self.z, :, :, self.lo]
            self.two.append(send(blk, blk, self.sa, 3 + k, "z", step))
            blk = self.held.at[:, :, self.x, :, self.hi]
            self.two.append(send(blk, blk, self.sb, 3 + k, "x", step))

    def finish(self):
        for copy in self.two:
            copy.wait_recv()

    def end(self):
        self.zero.wait_send()
        for copy in self.one + self.two:
            copy.wait_send()


class GradScatter:
    def __init__(self, held, cut, bufs):
        self.held, self.cut = held, cut
        (
            self.ra1, self.rb1, self.qa, self.qb, self.ra2, self.rb2, self.ta, self.tb,
            self.ra3, self.rb3, self.sa, self.sb,
        ) = bufs
        self.yl, self.z, self.x = (lax.axis_index(a) for a in FSDP)
        self.lo, self.hi = pl.ds(0, cut), pl.ds(cut, held.shape[-1] - cut)

    def step1(self):
        self.one = []
        for k, step in enumerate(NEAR):
            src = self.held.at[:, ahead("z", step), :, :, self.lo]
            self.one.append(send(src, self.ra1.at[k], self.sa, k, "z", step))
            src = self.held.at[:, :, ahead("x", step), :, self.hi]
            self.one.append(send(src, self.rb1.at[k], self.sb, k, "x", step))

    def step2(self):
        for copy in self.one:
            copy.wait_recv()

        def add(n, carry):
            a, b = n // 4, n % 4
            at_a = self.held[a, self.z, b, :, self.lo].astype(F32)
            at_b = self.held[a, b, self.x, :, self.hi].astype(F32)
            for k in range(3):
                at_a = at_a + self.ra1[k, a, b].astype(F32)
                at_b = at_b + self.rb1[k, a, b].astype(F32)
            self.qa[a, b] = at_a.astype(BF)
            self.qb[a, b] = at_b.astype(BF)
            return carry

        lax.fori_loop(0, 8, add, 0)
        self.two = []
        for k, step in enumerate(NEAR):
            src = self.qa.at[:, ahead("x", step)]
            self.two.append(send(src, self.ra2.at[k], self.sa, 3 + k, "x", step))
            src = self.qb.at[:, ahead("z", step)]
            self.two.append(send(src, self.rb2.at[k], self.sb, 3 + k, "z", step))

    def step3(self):
        for copy in self.two:
            copy.wait_recv()
        for a in range(2):
            at_a = self.qa[a, self.x].astype(F32)
            at_b = self.qb[a, self.z].astype(F32)
            for k in range(3):
                at_a = at_a + self.ra2[k, a].astype(F32)
                at_b = at_b + self.rb2[k, a].astype(F32)
            self.ta[a] = at_a.astype(BF)
            self.tb[a] = at_b.astype(BF)
        self.three = [
            send(self.ta.at[1 - self.yl], self.ra3, self.sa, 6, "yl"),
            send(self.tb.at[1 - self.yl], self.rb3, self.sb, 6, "yl"),
        ]

    def finish(self, flat, wide, piece):
        for copy in self.three:
            copy.wait_recv()
        half = self.cut
        fa = self.ta[self.yl].astype(F32) + self.ra3[...].astype(F32)
        fb = self.tb[self.yl].astype(F32) + self.rb3[...].astype(F32)
        flat[0:MAIN, 0:half] = fa
        flat[0:MAIN, half:wide] = fb[:, : wide - half]
        for j in range(wide // piece):
            flat[MAIN:SHARD, j * piece : (j + 1) * piece] = fb[4 * j : 4 * j + 4, wide - half :]

    def end(self):
        for copy in self.one + self.two + self.three:
            copy.wait_send()


def scatter_scratch(cut, lanes):
    shapes = ((3, 2, 4, MAIN), (2, 4, MAIN), (3, 2, MAIN), (2, MAIN), (MAIN,))
    return [pltpu.VMEM((*s, n), BF) for s in shapes for n in (cut, lanes - cut)] + [
        pltpu.SemaphoreType.DMA((2, 7)),
        pltpu.SemaphoreType.DMA((2, 7)),
    ]


def tail_pieces(b, e, piece):
    j = b
    while j < e:
        p = j // piece
        stop = min(e, (p + 1) * piece)
        yield p, j, stop
        j = stop


def unpack(held, refs, split, piece, wide):
    def band(g, carry):
        for j in range(4):
            src = held.at[g // 4, g % 4, j]
            for ref, (b, e) in zip(refs, split):
                ref[g, SHARD * j : SHARD * j + MAIN, :] = src[:, b:e]
                for p, lo, hi in tail_pieces(b, e, piece):
                    ref[g, SHARD * j + MAIN : SHARD * (j + 1), lo - b : hi - b] = src[
                        4 * p : 4 * p + 4, wide + lo - p * piece : wide + hi - p * piece
                    ]
        return carry

    lax.fori_loop(0, 8, band, 0)


def pack(held, grad, b, e, piece, wide):
    def band(g, carry):
        for j in range(4):
            dst = held.at[g // 4, g % 4, j]
            dst[:, b:e] = grad[g, SHARD * j : SHARD * j + MAIN, : e - b].astype(BF)
            for p, lo, hi in tail_pieces(b, e, piece):
                dst[4 * p : 4 * p + 4, wide + lo - p * piece : wide + hi - p * piece] = grad[
                    g, SHARD * j + MAIN : SHARD * (j + 1), lo - b : hi - b
                ].astype(BF)
        return carry

    lax.fori_loop(0, 8, band, 0)


def pack_own(dst, flat, wide, piece):
    dst[:, 0:wide] = flat[0:MAIN, 0:wide].astype(BF)
    for p in range(wide // piece):
        dst[4 * p : 4 * p + 4, wide : wide + piece] = flat[
            MAIN:SHARD, p * piece : (p + 1) * piece
        ].astype(BF)
    rest = 4 * (wide // piece)
    dst[rest:MAIN, wide : wide + piece] = jnp.zeros((MAIN - rest, piece), BF)


def layer_norm(stream):
    average = jnp.mean(stream, -1, keepdims=True)
    centered = stream - average
    variance = jnp.mean(centered * centered, -1, keepdims=True)
    inverse = lax.rsqrt(variance + EPS)
    return centered * inverse, inverse


def norm_back(upstream, normed, inverse, gain_vec):
    scaled = upstream * gain_vec
    return inverse * (
        scaled
        - jnp.mean(scaled, -1, keepdims=True)
        - normed * jnp.mean(scaled * normed, -1, keepdims=True)
    )


def gelu_parts(pre_act):
    tangent = jnp.tanh(GELU_C * (pre_act + CUBIC * pre_act * pre_act * pre_act))
    value = 0.5 * pre_act * (1.0 + tangent)
    slope = 0.5 * (1.0 + tangent) + 0.5 * pre_act * (1.0 - tangent * tangent) * GELU_C * (
        1.0 + 3.0 * CUBIC * pre_act * pre_act
    )
    return value, slope


def nn(a, b):
    return lax.dot_general(a, b, (((1,), (0,)), ((), ())), preferred_element_type=F32)


def nt(a, b):
    return lax.dot_general(a, b, (((1,), (1,)), ((), ())), preferred_element_type=F32)


def whole(ref):
    return ref[...].reshape(D, ref.shape[-1])


def pick(ref, rank, width):
    out = ref[:, 0:width]
    for r in range(1, 4):
        out = jnp.where(rank == r, ref[:, r * width : (r + 1) * width], out)
    return out


def layer_kernel(
    stream, valid, pre_gain, pre_shift, wq, bq, wk, wv, bv, wo, out_bias, mid_gain, mid_shift,
    wu, bu, wd, down_bias, cot,
    block_out, input_grad, gq, gk, gv, go, gu, gd, vecs,
    held1, held2, flat1, flat2, turn, wqkv, wout, wup, wdown, arows, crows, mrows, grows,
    qkv, mixed, dmix, mask, logsum, hidden, act, grad, flip, part1, part2, dk_acc, dv_acc, qv,
    upsum, bqkv, bhid, vown, varr,
    s0, s1a, s1b, s2a, s2b, ra, rc, rm, rg, sv,
    f1, f2, f3, fs, h1, h2, h3, hs, ts1, ts2, *scat,
):
    rank, over, sib, cross = ranks()
    x, z = lax.axis_index("x"), lax.axis_index("z")
    yl = lax.axis_index("yl")
    greet(ALL_PAIRS)
    gat1 = WeightGather(held1, CUT1, s0.at[0], s1a, s1b)
    gat2 = WeightGather(held2, CUT2, s0.at[1], s2a, s2b)

    turn[...] = jnp.zeros_like(turn)
    turn[0:COLS, 0:SHARD] = wo[...].astype(F32)
    flat1[:, 0:COLS] = wq[...].astype(F32)
    flat1[:, COLS : 2 * COLS] = wk[...].astype(F32)
    flat1[:, 2 * COLS : 3 * COLS] = wv[...].astype(F32)
    flat1[:, 3 * COLS : QKV] = jnp.zeros((SHARD, QKV - 3 * COLS), F32)
    flat1[:, QKV:] = turn[0:OUT, :].T[0:SHARD]
    pack_own(held1.at[yl, z, x], flat1, WIDE1, PIECE1)
    gat1.start()

    rows_a, rows_c = RowGather(arows, ra), RowGather(crows, rc)
    for j in range(CHUNKS):
        at = pl.ds(j * CH, CH)
        normed, _ = layer_norm(stream[at])
        arows[rank, at] = (normed * pre_gain[...] + pre_shift[...]).astype(BF)
        rows_a.put(j)

    turn[0:TRUE_HID, 0:SHARD] = wd[...].astype(F32)
    flat2[:, HID - 128 : HID] = jnp.zeros((SHARD, 128), F32)
    flat2[:, 0:TRUE_HID] = wu[...].astype(F32)
    flat2[:, HID:] = turn[...].T[0:SHARD]
    pack_own(held2.at[yl, z, x], flat2, WIDE2, PIECE2)
    gat1.step1()
    gat2.start()
    crows[rank] = cot[...].astype(BF)
    for j in range(CHUNKS):
        rows_c.put(j)
    live = jnp.broadcast_to(valid[...].astype(F32), (128, SEQ)).T
    mask[...] = jnp.where(live > 0, 0.0, -jnp.inf)
    bqkv[...] = jnp.zeros_like(bqkv)
    bqkv[:, 0:COLS] = pick(bq, rank, COLS)
    bqkv[:, 2 * COLS : 3 * COLS] = pick(bv, rank, COLS)
    bhid[...] = jnp.zeros_like(bhid)
    bhid[:, 0:TRUE_HID] = pick(bu, rank, TRUE_HID)
    mixed[...] = jnp.zeros_like(mixed)
    upsum[...] = jnp.zeros_like(upsum)
    qv[...] = jnp.zeros_like(qv)
    gat1.step2()
    for j in range(CHUNKS):
        rows_a.forward(j)
    rows_a.chip()
    rows_a.rest()
    for j in range(CHUNKS):
        rows_c.forward(j)
    gat1.finish()
    gat2.step1()
    unpack(held1, (wqkv, wout), SPLIT1, PIECE1, WIDE1)

    def project(r, carry):
        at = pl.ds(pl.multiple_of(r * ROWS, ROWS), ROWS)
        qkv[at] = (nn(arows[r], whole(wqkv)) + bqkv[...]).astype(BF)
        return carry

    lax.fori_loop(0, 4, project, 0)
    gat2.step2()

    def head_slices(h):
        lo = HD * h
        return (
            qkv[:, lo : lo + HD],
            qkv[:, COLS + lo : COLS + lo + HD],
            qkv[:, 2 * COLS + lo : 2 * COLS + lo + HD],
        )

    def scores_of(h, at):
        query = qkv[at, :][:, HD * h : HD * h + HD]
        key = head_slices(h)[1]
        bias = mask[...]
        return nt(key, query) * SCALE + jnp.concatenate([bias] * (QC // 128), 1), query

    for h in range(HEADS):

        def attend(i, carry, h=h):
            at = pl.ds(pl.multiple_of(i * QC, QC), QC)
            scores, _ = scores_of(h, at)
            top = jnp.max(scores, 0, keepdims=True)
            total = top + jnp.log(jnp.sum(jnp.exp(scores - top), 0, keepdims=True))
            logsum[h, i] = total
            probs = jnp.exp(scores - total).astype(BF)
            value = head_slices(h)[2]
            o_t = lax.dot_general(
                value, probs, (((0,), (0,)), ((), ())), preferred_element_type=F32
            )
            mixed[at, HD * h : HD * h + HD] = o_t.T.astype(BF)
            return carry

        lax.fori_loop(0, SEQ // QC, attend, 0)

    def out_block(r):
        at = pl.ds(pl.multiple_of(r * ROWS, ROWS), ROWS)
        part1[r] = nt(mixed[at], whole(wout)).astype(BF)

    sum1 = TpSum(part1, f1, f2, f3, fs)
    out_block(cross)
    sum1.start_cross()
    out_block(over)
    out_block(sib)
    sum1.start_sib()
    sum1.middle()
    out_block(rank)
    gat2.finish()
    unpack(held2, (wup, wdown), SPLIT2, PIECE2, WIDE2)
    rows_c.chip()
    rows_c.rest()
    rows_m = RowGather(mrows, rm)
    for j in range(CHUNKS):
        at = pl.ds(j * CH, CH)
        mid = stream[at] + sum1.total(j) + out_bias[...]
        block_out[at] = mid
        normed, _ = layer_norm(mid)
        mrows[rank, at] = (normed * mid_gain[...] + mid_shift[...]).astype(BF)
        rows_m.put(j)
    sum1.end()

    def mlp(r):
        pre_act = nn(mrows[r], whole(wup)) + bhid[...]
        value, slope = gelu_parts(pre_act)
        hidden[r] = value.astype(BF)
        act_grad = nn(crows[r], whole(wdown)) * slope
        act[r] = act_grad.astype(BF)
        upsum[...] += jnp.sum(act_grad, 0, keepdims=True)
        part1[r] = nt(act[r], whole(wup)).astype(BF)

    def mlp_step(n, carry):
        mlp(n)
        return carry

    for j in range(CHUNKS):
        rows_m.forward(j)
    rows_m.chip()
    rows_m.rest()
    lax.fori_loop(0, 4, mlp_step, 0)
    sum2 = TpSum(part1, f1, f2, f3, fs)
    sum2.start_cross()
    sum2.start_sib()
    sum2.middle()

    gat2.end()
    sc1 = GradScatter(held1, CUT1, scat[:12])
    sc2 = GradScatter(held2, CUT2, scat[12:])

    def turn_rows(rows):
        for j in range(3):
            blk = rows[:, :, 384 * j : 384 * (j + 1)].reshape(SEQ, 384)
            flip[384 * j : 384 * (j + 1), :] = blk.T

    def product(right, width, held, base, piece, wide):
        for lo in range(0, width, 384):
            hi = min(lo + 384, width)
            grad[:, :, 0 : hi - lo] = nn(flip[...], right(slice(lo, hi))).reshape(8, BAND, hi - lo)
            pack(held, grad, base + lo, base + hi, piece, wide)

    turn_rows(mrows)
    product(lambda at: act[:, :, at].reshape(SEQ, 384), HID, held2, 0, PIECE2, WIDE2)

    rows_g = RowGather(grows, rg)
    sums = [jnp.zeros((1, D), F32)] * 4
    for j in range(CHUNKS):
        at = pl.ds(j * CH, CH)
        normed, inverse = layer_norm(block_out[at])
        g = sum2.total(j)
        back = cot[at] + norm_back(g, normed, inverse, mid_gain[...])
        input_grad[at] = back
        grows[rank, at] = back.astype(BF)
        rows_g.put(j)
        for k, v in enumerate((back, g * normed, g, cot[at])):
            sums[k] = sums[k] + jnp.sum(v, 0, keepdims=True)
    vown[0] = jnp.zeros((16, D), F32)
    for k in range(4):
        vown[0, 2 + k : 3 + k, :] = sums[k]
    vown[0, pl.ds(8 + rank, 1), :] = upsum[...]
    sum2.end()

    turn_rows(crows)
    product(lambda at: hidden[:, :, at].reshape(SEQ, 384), HID, held2, HID, PIECE2, WIDE2)
    held2[:, :, :, 24:32, WIDE2:PACK2] = jnp.zeros((2, 4, 4, 8, PACK2 - WIDE2), BF)
    sc2.step1()

    def down_block(r, carry):
        part2[r] = nt(hidden[r], whole(wdown)).astype(BF)
        return carry

    lax.fori_loop(0, 4, down_block, 0)
    sum3 = TpSum(part2, h1, h2, h3, hs)
    sum3.start_cross()
    sum3.start_sib()
    for j in range(CHUNKS):
        rows_g.forward(j)
    sum3.middle()
    rows_g.chip()
    rows_g.rest()

    def mix_back(r, carry):
        at = pl.ds(pl.multiple_of(r * ROWS, ROWS), ROWS)
        dmix[at] = nn(grows[r], whole(wout)).astype(BF)
        return carry

    lax.fori_loop(0, 4, mix_back, 0)
    gat1.end()
    turn_rows(grows)
    product(lambda at: mixed[:, at], OUT, held1, QKV, PIECE1, WIDE1)

    for h in range(HEADS):
        dk_acc[...] = jnp.zeros_like(dk_acc)
        dv_acc[...] = jnp.zeros_like(dv_acc)
        lo = HD * h

        def attend_back(i, carry, h=h, lo=lo):
            at = pl.ds(pl.multiple_of(i * QC, QC), QC)
            scores, query = scores_of(h, at)
            probs = jnp.exp(scores - logsum[h, i])
            key, value = head_slices(h)[1:]
            dout = dmix[at, :][:, lo : lo + HD]
            dv_acc[...] += nn(probs.astype(BF), dout)
            prob_grad = nt(value, dout)
            delta = jnp.sum(probs * prob_grad, 0, keepdims=True)
            ds = (probs * (prob_grad - delta) * SCALE).astype(BF)
            dk_acc[...] += nn(ds, query)
            dq_t = lax.dot_general(
                key, ds, (((0,), (0,)), ((), ())), preferred_element_type=F32
            )
            dq = dq_t.T
            qv[0:1, lo : lo + HD] += jnp.sum(dq, 0, keepdims=True)
            qkv[at, lo : lo + HD] = dq.astype(BF)
            return carry

        lax.fori_loop(0, SEQ // QC, attend_back, 0)
        qv[0:1, COLS + lo : COLS + lo + HD] = jnp.sum(dv_acc[...], 0, keepdims=True)
        qkv[:, COLS + lo : COLS + lo + HD] = dk_acc[...].astype(BF)
        qkv[:, 2 * COLS + lo : 2 * COLS + lo + HD] = dv_acc[...].astype(BF)
    qkv[:, 3 * COLS : QKV] = jnp.zeros((SEQ, QKV - 3 * COLS), BF)

    def attn_block(r):
        at = pl.ds(pl.multiple_of(r * ROWS, ROWS), ROWS)
        part1[r] = nt(qkv[at], whole(wqkv)).astype(BF)

    sum4 = TpSum(part1, f1, f2, f3, fs)
    attn_block(cross)
    sum4.start_cross()
    attn_block(over)
    attn_block(sib)
    sum4.start_sib()
    sum4.middle()
    attn_block(rank)
    turn_rows(arows)
    product(lambda at: qkv[:, at], QKV, held1, 0, PIECE1, WIDE1)
    held1[:, :, :, 20:32, WIDE1:PACK1] = jnp.zeros((2, 4, 4, 12, PACK1 - WIDE1), BF)
    sc1.step1()
    sc2.step2()

    sums = [jnp.zeros((1, D), F32)] * 2
    for j in range(CHUNKS):
        at = pl.ds(j * CH, CH)
        normed, inverse = layer_norm(stream[at])
        g = sum4.total(j)
        input_grad[at] = input_grad[at] + norm_back(g, normed, inverse, pre_gain[...])
        for k, v in enumerate((g * normed, g)):
            sums[k] = sums[k] + jnp.sum(v, 0, keepdims=True)
        block_out[at] = block_out[at] + sum3.total(j) + down_bias[...]
    vown[0, 0:1, :] = sums[0]
    vown[0, 1:2, :] = sums[1]
    vown[0, pl.ds(12 + rank, 1), :] = qv[...]
    vc = [send(vown.at[0], varr.at[0], sv, 0, "c")]
    sc1.step2()
    vc[0].wait_recv()
    vown[1] = vown[0] + varr[0]
    vc.append(send(vown.at[1], varr.at[1], sv, 1, "yh"))
    sc2.step3()
    vc[1].wait_recv()
    vown[2] = vown[1] + varr[1]
    vc.append(send(vown.at[2], varr.at[2], sv, 2, "yl"))
    sc2.finish(flat2, WIDE2, PIECE2)
    gu[...] = flat2[:, 0:TRUE_HID]
    turn[...] = jnp.concatenate([flat2[:, HID:], jnp.zeros((128 - SHARD, HID), F32)], 0).T
    gd[...] = turn[0:TRUE_HID, 0:SHARD]
    vc[2].wait_recv()
    vown[3] = vown[2] + varr[2]
    for k, step in enumerate(NEAR):
        vc.append(send(vown.at[3], varr.at[3 + x], sv, 3 + k, "x", step))
    varr[3 + x] = vown[3]
    sc1.step3()
    for copy in vc[3:6]:
        copy.wait_recv()
    vown[4] = varr[3] + varr[4] + varr[5] + varr[6]
    for k, step in enumerate(NEAR):
        vc.append(send(vown.at[4], varr.at[7 + z], sv, 6 + k, "z", step))
    varr[7 + z] = vown[4]
    sc1.finish(flat1, WIDE1, PIECE1)
    gq[...] = flat1[:, 0:COLS]
    gk[...] = flat1[:, COLS : 2 * COLS]
    gv[...] = flat1[:, 2 * COLS : 3 * COLS]
    turn[0:OUT] = jnp.concatenate([flat1[:, QKV:], jnp.zeros((128 - SHARD, OUT), F32)], 0).T
    go[...] = turn[0:COLS, 0:SHARD]
    for copy in vc[6:9]:
        copy.wait_recv()
    vecs[...] = varr[7] + varr[8] + varr[9] + varr[10]
    for copy in vc:
        copy.wait_send()
    for item in (rows_a, rows_c, rows_m, rows_g, sum3, sum4, sc1, sc2):
        item.end()


def per_device(*args):
    (
        residual, valid_keys, pre_gain, pre_shift, wq, bq, wk, wv, bv, wo, out_bias, mid_gain,
        mid_shift, wu, bu, wd, down_bias, cotangent,
    ) = args
    row = lambda v: v.reshape(1, -1)
    vm = pl.BlockSpec(memory_space=pltpu.VMEM)
    ins = (
        residual[0], valid_keys, row(pre_gain), row(pre_shift), wq, row(bq), wk, wv, row(bv), wo,
        row(out_bias), row(mid_gain), row(mid_shift), wu, row(bu), wd, row(down_bias),
        cotangent[0],
    )
    outs = [
        (ROWS, D), (ROWS, D), (SHARD, COLS), (SHARD, COLS), (SHARD, COLS), (COLS, SHARD),
        (SHARD, TRUE_HID), (TRUE_HID, SHARD), (16, D),
    ]
    rows = (4, ROWS, D)
    dma = lambda *n: pltpu.SemaphoreType.DMA(n)
    tp_sum = [
        pltpu.VMEM((2, ROWS, D), BF),
        pltpu.VMEM((ROWS, D), BF),
        pltpu.VMEM((ROWS, D), BF),
        dma(2, 2 + CHUNKS),
    ]
    scratch = [
        pltpu.VMEM((2, 4, 4, MAIN, PACK1), BF),
        pltpu.VMEM((2, 4, 4, MAIN, PACK2), BF),
        pltpu.VMEM((SHARD, WIDE1), F32),
        pltpu.VMEM((SHARD, WIDE2), F32),
        pltpu.VMEM((HID, 128), F32),
        pltpu.VMEM((8, BAND, QKV), BF),
        pltpu.VMEM((8, BAND, OUT), BF),
        pltpu.VMEM((8, BAND, HID), BF),
        pltpu.VMEM((8, BAND, HID), BF),
        pltpu.VMEM(rows, BF),
        pltpu.VMEM(rows, BF),
        pltpu.VMEM(rows, BF),
        pltpu.VMEM(rows, BF),
        pltpu.VMEM((SEQ, QKV), BF),
        pltpu.VMEM((SEQ, OUT), BF),
        pltpu.VMEM((SEQ, OUT), BF),
        pltpu.VMEM((SEQ, 128), F32),
        pltpu.VMEM((HEADS, SEQ // QC, 1, QC), F32),
        pltpu.VMEM(rows, BF),
        pltpu.VMEM(rows, BF),
        pltpu.VMEM((8, BAND, 384), F32),
        pltpu.VMEM((D, SEQ), BF),
        pltpu.VMEM(rows, BF),
        pltpu.VMEM(rows, BF),
        pltpu.VMEM((SEQ, HD), F32),
        pltpu.VMEM((SEQ, HD), F32),
        pltpu.VMEM((1, D), F32),
        pltpu.VMEM((1, HID), F32),
        pltpu.VMEM((1, QKV), F32),
        pltpu.VMEM((1, HID), F32),
        pltpu.VMEM((5, 16, D), F32),
        pltpu.VMEM((11, 16, D), F32),
        dma(2, 2, 1),
        dma(2, 6),
        dma(2, 6),
        dma(2, 6),
        dma(2, 6),
        dma(2, 3 * CHUNKS),
        dma(2, 3 * CHUNKS),
        dma(2, 3 * CHUNKS),
        dma(2, 3 * CHUNKS),
        dma(2, 9),
        *tp_sum,
        *tp_sum,
        dma(1),
        dma(1),
        *scatter_scratch(CUT1, PACK1),
        *scatter_scratch(CUT2, PACK2),
    ]
    out = pl.pallas_call(
        layer_kernel,
        name="layer",
        out_shape=[jax.ShapeDtypeStruct(s, F32) for s in outs],
        in_specs=[vm] * len(ins),
        out_specs=[vm] * len(outs),
        scratch_shapes=scratch,
        compiler_params=pltpu.CompilerParams(
            collective_id=0, has_side_effects=True, vmem_limit_bytes=62 * 2**20
        ),
    )(*ins)
    block_out, input_grad, gq, gk, gv, go, gu, gd, vecs = out
    return (
        block_out[None], input_grad[None], gq, gk, gv, go, gu, gd,
        vecs[0],
        vecs[1],
        vecs[12:16, :COLS].reshape(D),
        vecs[12:16, COLS : 2 * COLS].reshape(D),
        vecs[2],
        vecs[3],
        vecs[4],
        vecs[8:12, :TRUE_HID].reshape(4 * TRUE_HID),
        vecs[5],
    )


def solution(mesh):
    split = Mesh(mesh.devices.reshape(2, 4, 4, 2, 2), ("yl", "z", "x", "yh", "c"))
    rows3 = P(FSDP, TP, None)
    down_cols = P(FSDP, TP)
    across = P(TP, FSDP)
    return jax.shard_map(
        per_device,
        mesh=split,
        in_specs=(
            rows3, P(FSDP, None), P(), P(), down_cols, P(), down_cols, down_cols, P(), across,
            P(), P(), P(), down_cols, P(), across, P(), rows3,
        ),
        out_specs=(
            rows3, rows3, down_cols, down_cols, down_cols, across, down_cols, across,
            P(), P(), P(), P(), P(), P(), P(), P(), P(),
        ),
        check_vma=False,
    )
```

```python
import math

import jax
import jax.numpy as jnp
from jax import lax
from jax.experimental import pallas as pl
from jax.experimental.pallas import tpu as pltpu
from jax.sharding import Mesh
from jax.sharding import PartitionSpec as P

HD = 72
HEADS = 4
COLS = HEADS * HD
D = 1152
SEQ = 768
ROWS = 192
CHUNKS = 2
CH = ROWS // CHUNKS
SHARD = 36
MAIN = 32
BAND = 4 * SHARD
QKV = 896
OUT = 384
HID = 1152
TRUE_HID = 1076
QC = 384
EPS = 1e-06
GELU_C = math.sqrt(2.0 / math.pi)
CUBIC = 0.044715
SCALE = 1.0 / math.sqrt(HD)
SIZE = {"yl": 2, "z": 4, "x": 4, "yh": 2, "c": 2}
FSDP = ("yl", "z", "x")
TP = ("yh", "c")
MESH = pl.DeviceIdType.MESH
BF = jnp.bfloat16
F32 = jnp.float32
NEAR = (1, 3, 2)
SPLIT1, PIECE1, WIDE1, PACK1 = ((0, QKV),), 128, QKV, QKV + 128
SPLIT3, PIECE3, WIDE3, PACK3 = ((0, OUT),), 128, OUT, OUT + 128
SPLIT2, PIECE2, WIDE2, PACK2 = ((0, HID), (HID, 2 * HID)), 384, 2 * HID, 2 * HID + 384
CUT1, CUT2, CUT3 = 512, 1408, 256
LINE = tuple(
    tuple((a, 1) for a, on in (("yl", i & 4), ("yh", i & 2), ("c", i & 1)) if on)
    for i in range(1, 8)
)
ALL_PEERS = LINE + tuple(((a, s),) for a in ("x", "z") for s in NEAR)


def ahead(axis, step):
    return lax.rem(lax.axis_index(axis) + step, SIZE[axis])


def peer(moves):
    return {axis: ahead(axis, step) for axis, step in moves}


def greet(peers):
    barrier = pltpu.get_barrier_semaphore()
    for moves in peers:
        pl.semaphore_signal(barrier, inc=1, device_id=peer(moves), device_id_type=MESH)
    pl.semaphore_wait(barrier, len(peers))


def send(src, dst, sems, k, axis, step=1):
    return send_to(src, dst, sems, k, ((axis, step),))


def send_to(src, dst, sems, k, moves):
    copy = pltpu.make_async_remote_copy(
        src_ref=src,
        dst_ref=dst,
        send_sem=sems.at[0, k],
        recv_sem=sems.at[1, k],
        device_id=peer(moves),
        device_id_type=MESH,
    )
    copy.start()
    return copy


def ranks():
    yh, c = lax.axis_index("yh"), lax.axis_index("c")
    return yh * 2 + c, (1 - yh) * 2 + c, yh * 2 + 1 - c, (1 - yh) * 2 + 1 - c


class RowGather:
    def __init__(self, rows, sems):
        self.rows, self.sems, self.over, self.sib, self.fwd = rows, sems, {}, {}, {}

    def put(self, j):
        blk = self.rows.at[ranks()[0], pl.ds(j * CH, CH)]
        self.over[j] = send(blk, blk, self.sems, 3 * j, "yh")
        self.sib[j] = send(blk, blk, self.sems, 3 * j + 1, "c")

    def forward(self, j):
        blk = self.rows.at[ranks()[1], pl.ds(j * CH, CH)]
        self.over[j].wait_recv()
        self.fwd[j] = send(blk, blk, self.sems, 3 * j + 2, "c")

    def chip(self):
        for j in range(CHUNKS):
            self.sib[j].wait_recv()

    def rest(self):
        for j in range(CHUNKS):
            self.fwd[j].wait_recv()

    def end(self):
        for j in range(CHUNKS):
            self.over[j].wait_send()
            self.sib[j].wait_send()
            self.fwd[j].wait_send()


class TpSum:
    def __init__(self, part, first, second, out, sems):
        self.part, self.first, self.second, self.out, self.sems = part, first, second, out, sems

    def start_cross(self):
        self.cross = send(self.part.at[ranks()[3]], self.first.at[0], self.sems, 0, "c")

    def start_sib(self):
        self.sib = send(self.part.at[ranks()[2]], self.first.at[1], self.sems, 1, "c")

    def middle(self):
        over = ranks()[1]
        self.cross.wait_recv()
        self.over = []
        for j in range(CHUNKS):
            rows = pl.ds(j * CH, CH)
            self.out[rows] = (
                self.part[over, rows].astype(F32) + self.first[0, rows].astype(F32)
            ).astype(BF)
            self.over.append(
                send(self.out.at[rows], self.second.at[rows], self.sems, 2 + j, "yh")
            )

    def total(self, j):
        mine = ranks()[0]
        rows = pl.ds(j * CH, CH)
        if j == 0:
            self.sib.wait_recv()
        self.over[j].wait_recv()
        return (
            self.part[mine, rows].astype(F32)
            + self.first[1, rows].astype(F32)
            + self.second[rows].astype(F32)
        )

    def end(self):
        self.cross.wait_send()
        self.sib.wait_send()
        for copy in self.over:
            copy.wait_send()


class WeightGather:
    def __init__(self, held, cut, sems, ring=False):
        self.held, self.cut, self.ring, self.done = held, cut, ring, []
        self.s0, self.sa, self.sb = sems
        self.yl, self.z, self.x = (lax.axis_index(a) for a in FSDP)
        self.lo, self.hi = pl.ds(0, cut), pl.ds(cut, held.shape[-1] - cut)

    def start(self):
        blk = self.held.at[self.yl, self.z, self.x]
        self.zero = send(blk, blk, self.s0, 0, "yl")

    def step1(self):
        self.zero.wait_recv()
        self.one = []
        for k, step in enumerate(NEAR):
            blk = self.held.at[:, self.z, self.x, :, self.lo]
            self.one.append(send(blk, blk, self.sa, k, "x", step))
            blk = self.held.at[:, self.z, self.x, :, self.hi]
            self.one.append(send(blk, blk, self.sb, k, "z", step))

    def step2(self):
        for copy in self.one:
            copy.wait_recv()
        self.two = []
        for k, step in enumerate(NEAR[:2] if self.ring else NEAR):
            blk = self.held.at[:, self.z, :, :, self.lo]
            self.two.append(send(blk, blk, self.sa, 3 + k, "z", step))
            blk = self.held.at[:, :, self.x, :, self.hi]
            self.two.append(send(blk, blk, self.sb, 3 + k, "x", step))

    def relay(self):
        for copy in self.two:
            copy.wait_recv()
        wide = self.held.shape[-1]
        more = []
        for k, (step, back) in enumerate(((1, 3), (3, 1))):
            mid = self.cut // 256 * 128
            at = pl.ds(0, mid) if k == 0 else pl.ds(mid, self.cut - mid)
            blk = self.held.at[:, ahead("z", back), :, :, at]
            more.append(send(blk, blk, self.sa, 5 + k, "z", step))
            mid = (wide - self.cut) // 256 * 128
            at = pl.ds(self.cut, mid) if k == 0 else pl.ds(self.cut + mid, wide - self.cut - mid)
            blk = self.held.at[:, :, ahead("x", back), :, at]
            more.append(send(blk, blk, self.sb, 5 + k, "x", step))
        self.done, self.two = self.two, more

    def finish(self):
        for copy in self.two:
            copy.wait_recv()

    def end(self):
        self.zero.wait_send()
        for copy in self.one + self.two + self.done:
            copy.wait_send()


class GradScatter:
    def __init__(self, held, cut, bufs):
        self.held, self.cut = held, cut
        (
            self.ra1, self.rb1, self.qa, self.qb, self.ra2, self.rb2, self.ta, self.tb,
            self.ra3, self.rb3, self.sa, self.sb,
        ) = bufs
        self.yl, self.z, self.x = (lax.axis_index(a) for a in FSDP)
        self.lo, self.hi = pl.ds(0, cut), pl.ds(cut, held.shape[-1] - cut)

    def step1(self):
        self.one = []
        for k, step in enumerate(NEAR):
            src = self.held.at[:, ahead("z", step), :, :, self.lo]
            self.one.append(send(src, self.ra1.at[k], self.sa, k, "z", step))
            src = self.held.at[:, :, ahead("x", step), :, self.hi]
            self.one.append(send(src, self.rb1.at[k], self.sb, k, "x", step))

    def step2(self):
        for copy in self.one:
            copy.wait_recv()

        def add(n, carry):
            a, b = n // 4, n % 4
            at_a = self.held[a, self.z, b, :, self.lo].astype(F32)
            at_b = self.held[a, b, self.x, :, self.hi].astype(F32)
            for k in range(3):
                at_a = at_a + self.ra1[k, a, b].astype(F32)
                at_b = at_b + self.rb1[k, a, b].astype(F32)
            self.qa[a, b] = at_a.astype(BF)
            self.qb[a, b] = at_b.astype(BF)
            return carry

        lax.fori_loop(0, 8, add, 0)
        self.two = []
        for k, step in enumerate(NEAR):
            src = self.qa.at[:, ahead("x", step)]
            self.two.append(send(src, self.ra2.at[k], self.sa, 3 + k, "x", step))
            src = self.qb.at[:, ahead("z", step)]
            self.two.append(send(src, self.rb2.at[k], self.sb, 3 + k, "z", step))

    def step3(self):
        for copy in self.two:
            copy.wait_recv()
        for a in range(2):
            at_a = self.qa[a, self.x].astype(F32)
            at_b = self.qb[a, self.z].astype(F32)
            for k in range(3):
                at_a = at_a + self.ra2[k, a].astype(F32)
                at_b = at_b + self.rb2[k, a].astype(F32)
            self.ta[a] = at_a.astype(BF)
            self.tb[a] = at_b.astype(BF)
        self.three = [
            send(self.ta.at[1 - self.yl], self.ra3, self.sa, 6, "yl"),
            send(self.tb.at[1 - self.yl], self.rb3, self.sb, 6, "yl"),
        ]

    def finish(self, flat, wide, piece):
        for copy in self.three:
            copy.wait_recv()
        half = self.cut
        fa = self.ta[self.yl].astype(F32) + self.ra3[...].astype(F32)
        fb = self.tb[self.yl].astype(F32) + self.rb3[...].astype(F32)
        flat[0:MAIN, 0:half] = fa
        flat[0:MAIN, half:wide] = fb[:, : wide - half]
        for j in range(wide // piece):
            flat[MAIN:SHARD, j * piece : (j + 1) * piece] = fb[4 * j : 4 * j + 4, wide - half :]

    def end(self):
        for copy in self.one + self.two + self.three:
            copy.wait_send()


def scatter_scratch(cut, lanes):
    shapes = ((3, 2, 4, MAIN), (2, 4, MAIN), (3, 2, MAIN), (2, MAIN), (MAIN,))
    return [pltpu.VMEM((*s, n), BF) for s in shapes for n in (cut, lanes - cut)] + [
        pltpu.SemaphoreType.DMA((2, 7)),
        pltpu.SemaphoreType.DMA((2, 7)),
    ]


def tail_pieces(b, e, piece):
    j = b
    while j < e:
        p = j // piece
        stop = min(e, (p + 1) * piece)
        yield p, j, stop
        j = stop


def unpack(held, refs, split, piece, wide):
    def band(g, carry):
        for j in range(4):
            src = held.at[g // 4, g % 4, j]
            for ref, (b, e) in zip(refs, split):
                ref[g, SHARD * j : SHARD * j + MAIN, :] = src[:, b:e]
                for p, lo, hi in tail_pieces(b, e, piece):
                    ref[g, SHARD * j + MAIN : SHARD * (j + 1), lo - b : hi - b] = src[
                        4 * p : 4 * p + 4, wide + lo - p * piece : wide + hi - p * piece
                    ]
        return carry

    lax.fori_loop(0, 8, band, 0)


def pack(held, grad, b, e, piece, wide):
    def band(g, carry):
        for j in range(4):
            dst = held.at[g // 4, g % 4, j]
            dst[:, b:e] = grad[g, SHARD * j : SHARD * j + MAIN, : e - b].astype(BF)
            for p, lo, hi in tail_pieces(b, e, piece):
                dst[4 * p : 4 * p + 4, wide + lo - p * piece : wide + hi - p * piece] = grad[
                    g, SHARD * j + MAIN : SHARD * (j + 1), lo - b : hi - b
                ].astype(BF)
        return carry

    lax.fori_loop(0, 8, band, 0)


def pack_own(dst, flat, wide, piece):
    dst[:, 0:wide] = flat[0:MAIN, 0:wide].astype(BF)
    for p in range(wide // piece):
        dst[4 * p : 4 * p + 4, wide : wide + piece] = flat[
            MAIN:SHARD, p * piece : (p + 1) * piece
        ].astype(BF)
    rest = 4 * (wide // piece)
    dst[rest:MAIN, wide : wide + piece] = jnp.zeros((MAIN - rest, piece), BF)


def layer_norm(stream):
    average = jnp.mean(stream, -1, keepdims=True)
    centered = stream - average
    variance = jnp.mean(centered * centered, -1, keepdims=True)
    inverse = lax.rsqrt(variance + EPS)
    return centered * inverse, inverse


def norm_back(upstream, normed, inverse, gain_vec):
    scaled = upstream * gain_vec
    return inverse * (
        scaled
        - jnp.mean(scaled, -1, keepdims=True)
        - normed * jnp.mean(scaled * normed, -1, keepdims=True)
    )


def gelu_parts(pre_act):
    tangent = jnp.tanh(GELU_C * (pre_act + CUBIC * pre_act * pre_act * pre_act))
    value = 0.5 * pre_act * (1.0 + tangent)
    slope = 0.5 * (1.0 + tangent) + 0.5 * pre_act * (1.0 - tangent * tangent) * GELU_C * (
        1.0 + 3.0 * CUBIC * pre_act * pre_act
    )
    return value, slope


def nn(a, b):
    return lax.dot_general(a, b, (((1,), (0,)), ((), ())), preferred_element_type=F32)


def nt(a, b):
    return lax.dot_general(a, b, (((1,), (1,)), ((), ())), preferred_element_type=F32)


def whole(ref):
    return ref[...].reshape(D, ref.shape[-1])


def vec(ref):
    return ref[...].reshape(1, -1)


def pick(ref, rank, width):
    flat = vec(ref)
    out = flat[:, 0:width]
    for r in range(1, 4):
        out = jnp.where(rank == r, flat[:, r * width : (r + 1) * width], out)
    return out


def layer_kernel(
    stream, valid, pre_gain, pre_shift, wq, bq, wk, wv, bv, wo, out_bias, mid_gain, mid_shift,
    wu, bu, wd, down_bias, cot,
    block_out, input_grad, gq, gk, gv, go, gu, gd, early_out, late_out,
    held1, held2, held3, flat1, flat2, flat3, wqkv, wout, wup, wdown, arows, crows, mrows, grows,
    qkv, mixed, dmix, mask, logsum, hidden, act, grad, flip, part1, dk_acc, dv_acc, qv,
    upsum, bqkv, bhid, early, early_in, late, late_in,
    s1y, s1a, s1b, s2y, s2a, s2b, s3y, s3a, s3b, ra, rc, rm, rg, se, sl,
    f1, f2, f3, fs, h1, h2, h3, hs, *scat,
):
    rank, over, sib, cross = ranks()
    yl, z, x = (lax.axis_index(a) for a in FSDP)
    yh, c = (lax.axis_index(a) for a in TP)
    greet(ALL_PEERS)
    gat1 = WeightGather(held1, CUT1, (s1y, s1a, s1b))
    gat2 = WeightGather(held2, CUT2, (s2y, s2a, s2b), ring=True)
    gat3 = WeightGather(held3, CUT3, (s3y, s3a, s3b))

    flat1[:, 0:COLS] = wq[...].astype(F32)
    flat1[:, COLS : 2 * COLS] = wk[...].astype(F32)
    flat1[:, 2 * COLS : 3 * COLS] = wv[...].astype(F32)
    flat1[:, 3 * COLS : QKV] = jnp.zeros((SHARD, QKV - 3 * COLS), F32)
    pack_own(held1.at[yl, z, x], flat1, WIDE1, PIECE1)
    gat1.start()

    rows_a, rows_c = RowGather(arows, ra), RowGather(crows, rc)
    for j in range(CHUNKS):
        at = pl.ds(j * CH, CH)
        normed, _ = layer_norm(stream[at])
        arows[rank, at] = (normed * vec(pre_gain) + vec(pre_shift)).astype(BF)
        rows_a.put(j)

    gat1.step1()
    flat3[:, 0:COLS] = wo[...].astype(F32)
    flat3[:, COLS:] = jnp.zeros((SHARD, OUT - COLS), F32)
    pack_own(held3.at[yl, z, x], flat3, WIDE3, PIECE3)
    gat3.start()
    for at in (0, HID):
        flat2[:, at + HID - 128 : at + HID] = jnp.zeros((SHARD, 128), F32)
    flat2[:, 0:TRUE_HID] = wu[...].astype(F32)
    flat2[:, HID : HID + TRUE_HID] = wd[...].astype(F32)
    pack_own(held2.at[yl, z, x], flat2, WIDE2, PIECE2)
    gat2.start()
    gat1.step2()
    gat3.step1()
    for j in range(CHUNKS):
        rows_a.forward(j)
    crows[rank] = cot[...].astype(BF)
    for j in range(CHUNKS):
        rows_c.put(j)
    live = jnp.broadcast_to(valid[...].astype(F32), (128, SEQ)).T
    mask[...] = jnp.where(live > 0, 0.0, -jnp.inf)
    bqkv[...] = jnp.zeros_like(bqkv)
    bqkv[:, 0:COLS] = pick(bq, rank, COLS)
    bqkv[:, 2 * COLS : 3 * COLS] = pick(bv, rank, COLS)
    bhid[...] = jnp.zeros_like(bhid)
    bhid[:, 0:TRUE_HID] = pick(bu, rank, TRUE_HID)
    mixed[...] = jnp.zeros_like(mixed)
    upsum[...] = jnp.zeros_like(upsum)
    qv[...] = jnp.zeros_like(qv)
    dk_acc[...] = jnp.zeros_like(dk_acc)
    dv_acc[...] = jnp.zeros_like(dv_acc)
    rows_a.chip()
    rows_a.rest()
    gat1.finish()
    gat3.step2()
    gat2.step1()
    unpack(held1, (wqkv,), SPLIT1, PIECE1, WIDE1)

    def project(r, carry):
        at = pl.ds(pl.multiple_of(r * ROWS, ROWS), ROWS)
        qkv[at] = (nn(arows[r], whole(wqkv)) + bqkv[...]).astype(BF)
        return carry

    lax.fori_loop(0, 4, project, 0)
    for j in range(CHUNKS):
        rows_c.forward(j)

    def head_slices(h):
        lo = HD * h
        return (
            qkv[:, COLS + lo : COLS + lo + HD],
            qkv[:, 2 * COLS + lo : 2 * COLS + lo + HD],
        )

    def half_rows(chip):
        return pl.ds(pl.multiple_of(chip * QC, QC), QC)

    def scores_of(h, at):
        query = qkv[at, :][:, HD * h : HD * h + HD]
        key = head_slices(h)[0]
        bias = mask[...]
        return nt(key, query) * SCALE + jnp.concatenate([bias] * (QC // 128), 1), query

    def attend(chip):
        at = half_rows(chip)
        for h in range(HEADS):
            scores, _ = scores_of(h, at)
            top = jnp.max(scores, 0, keepdims=True)
            raised = jnp.exp(scores - top)
            total = jnp.sum(raised, 0, keepdims=True)
            logsum[h, chip] = top + jnp.log(total)
            probs = (raised * (1.0 / total)).astype(BF)
            value = head_slices(h)[1]
            o_t = lax.dot_general(
                value, probs, (((0,), (0,)), ((), ())), preferred_element_type=F32
            )
            mixed[at, HD * h : HD * h + HD] = o_t.T.astype(BF)

    def out_block(r):
        at = pl.ds(pl.multiple_of(r * ROWS, ROWS), ROWS)
        part1[r] = nt(mixed[at], whole(wout)).astype(BF)

    sum1 = TpSum(part1, f1, f2, f3, fs)
    attend(1 - yh)
    gat3.finish()
    unpack(held3, (wout,), SPLIT3, PIECE3, WIDE3)
    out_block(cross)
    sum1.start_cross()
    out_block(over)
    gat2.step2()
    sum1.middle()
    attend(yh)
    out_block(sib)
    sum1.start_sib()
    out_block(rank)
    gat2.relay()
    rows_c.chip()
    rows_c.rest()
    rows_m = RowGather(mrows, rm)
    for j in range(CHUNKS):
        at = pl.ds(j * CH, CH)
        mid = stream[at] + sum1.total(j) + vec(out_bias)
        block_out[at] = mid
        normed, _ = layer_norm(mid)
        mrows[rank, at] = (normed * vec(mid_gain) + vec(mid_shift)).astype(BF)
        rows_m.put(j)
    sum1.end()
    gat2.finish()
    unpack(held2, (wup, wdown), SPLIT2, PIECE2, WIDE2)

    def mlp_pair(a, b):
        def step(n, carry):
            r = (1 - n) * a + n * b
            pre_act = nn(mrows[r], whole(wup)) + bhid[...]
            value, slope = gelu_parts(pre_act)
            hidden[r] = value.astype(BF)
            act_grad = nn(crows[r], whole(wdown)) * slope
            act[r] = act_grad.astype(BF)
            upsum[...] += jnp.sum(act_grad, 0, keepdims=True)
            part1[r] = nt(act[r], whole(wup)).astype(BF)
            return carry

        lax.fori_loop(0, 2, step, 0)

    rows_m.chip()
    mlp_pair(rank, sib)
    sum2 = TpSum(part1, f1, f2, f3, fs)
    sum2.start_sib()
    for j in range(CHUNKS):
        rows_m.forward(j)
    rows_m.rest()
    mlp_pair(over, cross)
    sum2.start_cross()
    sum2.middle()

    gat1.end()
    gat2.end()
    gat3.end()
    rows_m.end()
    sc1 = GradScatter(held1, CUT1, scat[:12])
    sc2 = GradScatter(held2, CUT2, scat[12:24])
    sc3 = GradScatter(held3, CUT3, scat[24:])

    def turn_rows(rows):
        for j in range(3):
            blk = rows[:, :, 384 * j : 384 * (j + 1)].reshape(SEQ, 384)
            flip[384 * j : 384 * (j + 1), :] = blk.T

    def product(right, width, held, base, piece, wide):
        for lo in range(0, width, 384):
            hi = min(lo + 384, width)
            grad[:, :, 0 : hi - lo] = nn(flip[...], right(slice(lo, hi))).reshape(8, BAND, hi - lo)
            pack(held, grad, base + lo, base + hi, piece, wide)

    def blank(held, piece, wide):
        used = 4 * (wide // piece)
        held[:, :, :, used:MAIN, wide : wide + piece] = jnp.zeros((2, 4, 4, MAIN - used, piece), BF)

    turn_rows(mrows)
    product(lambda at: act[:, :, at].reshape(SEQ, 384), HID, held2, 0, PIECE2, WIDE2)
    turn_rows(crows)
    product(lambda at: hidden[:, :, at].reshape(SEQ, 384), HID, held2, HID, PIECE2, WIDE2)
    blank(held2, PIECE2, WIDE2)
    sc2.step1()

    rows_g = RowGather(grows, rg)
    sums = [jnp.zeros((1, D), F32)] * 4
    for j in range(CHUNKS):
        at = pl.ds(j * CH, CH)
        normed, inverse = layer_norm(block_out[at])
        g = sum2.total(j)
        back = cot[at] + norm_back(g, normed, inverse, vec(mid_gain))
        input_grad[at] = back
        grows[rank, at] = back.astype(BF)
        rows_g.put(j)
        for k, v in enumerate((back, g * normed, g, cot[at])):
            sums[k] = sums[k] + jnp.sum(v, 0, keepdims=True)
    early[0] = jnp.zeros((8, D), F32)
    for k in range(4):
        early[0, k : k + 1, :] = sums[k]
    early[0, pl.ds(4 + rank, 1), :] = upsum[...]
    ec = [send(early.at[0], early_in.at[0], se, 0, "c")]
    sum2.end()

    def down_block(r, carry):
        mrows[r] = nt(hidden[r], whole(wdown)).astype(BF)
        return carry

    lax.fori_loop(0, 4, down_block, 0)
    sum3 = TpSum(mrows, h1, h2, h3, hs)
    sum3.start_cross()
    sum3.start_sib()
    ec[0].wait_recv()
    early[1] = early[0] + early_in[0]
    ec.append(send(early.at[1], early_in.at[1], se, 1, "yh"))

    def mix_back(a, b):
        def step(n, carry):
            r = (1 - n) * a + n * b
            at = pl.ds(pl.multiple_of(r * ROWS, ROWS), ROWS)
            dmix[at] = nn(grows[r], whole(wout)).astype(BF)
            return carry

        lax.fori_loop(0, 2, step, 0)

    def attend_back(chip):
        at = half_rows(chip)
        for h in range(HEADS):
            lo = HD * h
            scores, query = scores_of(h, at)
            probs = jnp.exp(scores - logsum[h, chip])
            key, value = head_slices(h)
            dout = dmix[at, :][:, lo : lo + HD]
            dv_acc[h] += nn(probs.astype(BF), dout)
            prob_grad = nt(value, dout)
            delta = jnp.sum(probs * prob_grad, 0, keepdims=True)
            ds = (probs * (prob_grad - delta) * SCALE).astype(BF)
            dk_acc[h] += nn(ds, query)
            dq = lax.dot_general(
                key, ds, (((0,), (0,)), ((), ())), preferred_element_type=F32
            ).T
            qv[0:1, lo : lo + HD] += jnp.sum(dq, 0, keepdims=True)
            qkv[at, lo : lo + HD] = dq.astype(BF)

    rows_g.chip()
    mix_back(rank, sib)
    for j in range(CHUNKS):
        rows_g.forward(j)
    sum3.middle()
    attend_back(yh)
    ec[1].wait_recv()
    early[2] = early[1] + early_in[1]
    ec.append(send(early.at[2], early_in.at[2], se, 2, "yl"))
    rows_g.rest()
    mix_back(over, cross)
    turn_rows(grows)
    product(lambda at: mixed[:, at], OUT, held3, 0, PIECE3, WIDE3)
    blank(held3, PIECE3, WIDE3)
    sc3.step1()
    ec[2].wait_recv()
    early[3] = early[2] + early_in[2]
    for k, step in enumerate(NEAR):
        ec.append(send(early.at[3], early_in.at[3 + x], se, 3 + k, "x", step))
    early_in[3 + x] = early[3]
    attend_back(1 - yh)
    for h in range(HEADS):
        lo = HD * h
        qv[0:1, COLS + lo : COLS + lo + HD] = jnp.sum(dv_acc[h], 0, keepdims=True)
        qkv[:, COLS + lo : COLS + lo + HD] = dk_acc[h].astype(BF)
        qkv[:, 2 * COLS + lo : 2 * COLS + lo + HD] = dv_acc[h].astype(BF)
    qkv[:, 3 * COLS : QKV] = jnp.zeros((SEQ, QKV - 3 * COLS), BF)

    def attn_block(r):
        at = pl.ds(pl.multiple_of(r * ROWS, ROWS), ROWS)
        part1[r] = nt(qkv[at], whole(wqkv)).astype(BF)

    sum4 = TpSum(part1, f1, f2, f3, fs)
    attn_block(cross)
    sum4.start_cross()
    attn_block(over)
    sum4.middle()
    attn_block(sib)
    sum4.start_sib()
    attn_block(rank)
    turn_rows(arows)
    product(lambda at: qkv[:, at], QKV, held1, 0, PIECE1, WIDE1)
    blank(held1, PIECE1, WIDE1)
    sc1.step1()
    sc2.step2()
    sc3.step2()
    for copy in ec[3:6]:
        copy.wait_recv()
    early[4] = early_in[3] + early_in[4] + early_in[5] + early_in[6]
    for k, step in enumerate(NEAR):
        ec.append(send(early.at[4], early_in.at[7 + z], se, 6 + k, "z", step))
    early_in[7 + z] = early[4]

    sums = [jnp.zeros((1, D), F32)] * 2
    for j in range(CHUNKS):
        at = pl.ds(j * CH, CH)
        normed, inverse = layer_norm(stream[at])
        g = sum4.total(j)
        input_grad[at] = input_grad[at] + norm_back(g, normed, inverse, vec(pre_gain))
        for k, v in enumerate((g * normed, g)):
            sums[k] = sums[k] + jnp.sum(v, 0, keepdims=True)
    late[0] = jnp.zeros((8, D), F32)
    late[0, 0:1, :] = sums[0]
    late[0, 1:2, :] = sums[1]
    late[0, pl.ds(4 + rank, 1), :] = qv[...]
    here = yl * 4 + yh * 2 + c
    lc = [
        send_to(late.at[0], late_in.at[here], sl, k, moves) for k, moves in enumerate(LINE)
    ]
    late_in[here] = late[0]
    for j in range(CHUNKS):
        at = pl.ds(j * CH, CH)
        block_out[at] = block_out[at] + sum3.total(j) + vec(down_bias)
    sc1.step2()
    for copy in lc:
        copy.wait_recv()
    late[1] = sum((late_in[k] for k in range(1, 8)), late_in[0])
    for k, step in enumerate(NEAR):
        lc.append(send(late.at[1], late_in.at[8 + x], sl, 7 + k, "x", step))
    late_in[8 + x] = late[1]
    sc2.step3()
    sc3.step3()
    for copy in lc[7:10]:
        copy.wait_recv()
    late[2] = late_in[8] + late_in[9] + late_in[10] + late_in[11]
    for k, step in enumerate(NEAR):
        lc.append(send(late.at[2], late_in.at[12 + z], sl, 10 + k, "z", step))
    late_in[12 + z] = late[2]
    sc1.step3()
    sc2.finish(flat2, WIDE2, PIECE2)
    gu[...] = flat2[:, 0:TRUE_HID]
    gd[...] = flat2[:, HID : HID + TRUE_HID]
    sc3.finish(flat3, WIDE3, PIECE3)
    go[...] = flat3[:, 0:COLS]
    for copy in ec[6:9]:
        copy.wait_recv()
    early_out[...] = early_in[7] + early_in[8] + early_in[9] + early_in[10]
    for copy in lc[10:13]:
        copy.wait_recv()
    late_out[...] = late_in[12] + late_in[13] + late_in[14] + late_in[15]
    sc1.finish(flat1, WIDE1, PIECE1)
    gq[...] = flat1[:, 0:COLS]
    gk[...] = flat1[:, COLS : 2 * COLS]
    gv[...] = flat1[:, 2 * COLS : 3 * COLS]
    for copy in ec + lc:
        copy.wait_send()
    for item in (rows_a, rows_c, rows_g, sum3, sum4, sc1, sc2, sc3):
        item.end()


def split_kernel(*refs):
    early, late = refs[8:10]
    outs = refs[10:]
    for k in range(8):
        outs[k][...] = refs[k][...]

    def joined(ref, lo, width):
        rows = [ref[4 + r : 5 + r, lo : lo + width] for r in range(4)]
        return jnp.concatenate(rows, 1).reshape(4 * width)

    pregain, preshift, query, value, outbias, midgain, midshift, up, downbias = outs[8:]
    pregain[...] = late[0]
    preshift[...] = late[1]
    query[...] = joined(late, 0, COLS)
    value[...] = joined(late, COLS, COLS)
    outbias[...] = early[0]
    midgain[...] = early[1]
    midshift[...] = early[2]
    downbias[...] = early[3]
    up[...] = joined(early, 0, TRUE_HID)


def per_device(*args):
    (
        residual, valid_keys, pre_gain, pre_shift, wq, bq, wk, wv, bv, wo, out_bias, mid_gain,
        mid_shift, wu, bu, wd, down_bias, cotangent,
    ) = args
    vm = pl.BlockSpec(memory_space=pltpu.VMEM)
    ins = (
        residual[0], valid_keys, pre_gain, pre_shift, wq, bq, wk, wv, bv, wo.T, out_bias,
        mid_gain, mid_shift, wu, bu, wd.T, down_bias, cotangent[0],
    )
    arrays = [
        (ROWS, D), (ROWS, D), (SHARD, COLS), (SHARD, COLS), (SHARD, COLS), (SHARD, COLS),
        (SHARD, TRUE_HID), (SHARD, TRUE_HID),
    ]
    outs = arrays + [(8, D), (8, D)]
    rows = (4, ROWS, D)
    dma = lambda *n: pltpu.SemaphoreType.DMA(n)
    tp_sum = [
        pltpu.VMEM((2, ROWS, D), BF),
        pltpu.VMEM((ROWS, D), BF),
        pltpu.VMEM((ROWS, D), BF),
        dma(2, 2 + CHUNKS),
    ]
    scratch = [
        pltpu.VMEM((2, 4, 4, MAIN, PACK1), BF),
        pltpu.VMEM((2, 4, 4, MAIN, PACK2), BF),
        pltpu.VMEM((2, 4, 4, MAIN, PACK3), BF),
        pltpu.VMEM((SHARD, WIDE1), F32),
        pltpu.VMEM((SHARD, WIDE2), F32),
        pltpu.VMEM((SHARD, WIDE3), F32),
        pltpu.VMEM((8, BAND, QKV), BF),
        pltpu.VMEM((8, BAND, OUT), BF),
        pltpu.VMEM((8, BAND, HID), BF),
        pltpu.VMEM((8, BAND, HID), BF),
        pltpu.VMEM(rows, BF),
        pltpu.VMEM(rows, BF),
        pltpu.VMEM(rows, BF),
        pltpu.VMEM(rows, BF),
        pltpu.VMEM((SEQ, QKV), BF),
        pltpu.VMEM((SEQ, OUT), BF),
        pltpu.VMEM((SEQ, OUT), BF),
        pltpu.VMEM((SEQ, 128), F32),
        pltpu.VMEM((HEADS, SEQ // QC, 1, QC), F32),
        pltpu.VMEM(rows, BF),
        pltpu.VMEM(rows, BF),
        pltpu.VMEM((8, BAND, 384), F32),
        pltpu.VMEM((D, SEQ), BF),
        pltpu.VMEM(rows, BF),
        pltpu.VMEM((HEADS, SEQ, HD), F32),
        pltpu.VMEM((HEADS, SEQ, HD), F32),
        pltpu.VMEM((1, D), F32),
        pltpu.VMEM((1, HID), F32),
        pltpu.VMEM((1, QKV), F32),
        pltpu.VMEM((1, HID), F32),
        pltpu.VMEM((5, 8, D), F32),
        pltpu.VMEM((11, 8, D), F32),
        pltpu.VMEM((3, 8, D), F32),
        pltpu.VMEM((16, 8, D), F32),
        *([dma(2, 1), dma(2, 7), dma(2, 7)] * 3),
        *([dma(2, 3 * CHUNKS)] * 4),
        dma(2, 9),
        dma(2, 13),
        *tp_sum,
        *tp_sum,
        *scatter_scratch(CUT1, PACK1),
        *scatter_scratch(CUT2, PACK2),
        *scatter_scratch(CUT3, PACK3),
    ]
    out = pl.pallas_call(
        layer_kernel,
        name="layer",
        out_shape=[jax.ShapeDtypeStruct(s, F32) for s in outs],
        in_specs=[vm] * len(ins),
        out_specs=[vm] * len(outs),
        scratch_shapes=scratch,
        compiler_params=pltpu.CompilerParams(
            collective_id=0, has_side_effects=True, vmem_limit_bytes=63 * 2**20
        ),
    )(*ins)
    ends = arrays + [(D,)] * 7 + [(4 * TRUE_HID,), (D,)]
    done = pl.pallas_call(
        split_kernel,
        name="split",
        out_shape=[jax.ShapeDtypeStruct(s, F32) for s in ends],
        in_specs=[vm] * len(out),
        out_specs=[vm] * len(ends),
    )(*out)
    return (
        done[0][None], done[1][None], done[2], done[3], done[4], done[5].T, done[6], done[7].T,
        *done[8:],
    )


def solution(mesh):
    split = Mesh(mesh.devices.reshape(2, 4, 4, 2, 2), ("yl", "z", "x", "yh", "c"))
    rows3 = P(FSDP, TP, None)
    down_cols = P(FSDP, TP)
    across = P(TP, FSDP)
    return jax.shard_map(
        per_device,
        mesh=split,
        in_specs=(
            rows3, P(FSDP, None), P(), P(), down_cols, P(), down_cols, down_cols, P(), across,
            P(), P(), P(), down_cols, P(), across, P(), rows3,
        ),
        out_specs=(
            rows3, rows3, down_cols, down_cols, down_cols, across, down_cols, across,
            P(), P(), P(), P(), P(), P(), P(), P(), P(),
        ),
        check_vma=False,
    )
```

```python
import math

import jax
import jax.numpy as jnp
from jax import lax
from jax.experimental import pallas as pl
from jax.experimental.pallas import tpu as pltpu
from jax.sharding import Mesh
from jax.sharding import PartitionSpec as P

HD = 72
HEADS = 4
COLS = HEADS * HD
D = 1152
SEQ = 768
ROWS = 192
CHUNKS = 2
CH = ROWS // CHUNKS
SHARD = 36
MAIN = 32
BAND = 4 * SHARD
QKV = 896
OUT = 384
HID = 1152
TRUE_HID = 1076
QC = 384
EPS = 1e-06
GELU_C = math.sqrt(2.0 / math.pi)
CUBIC = 0.044715
SCALE = 1.0 / math.sqrt(HD)
SIZE = {"yl": 2, "z": 4, "x": 4, "yh": 2, "c": 2}
FSDP = ("yl", "z", "x")
TP = ("yh", "c")
MESH = pl.DeviceIdType.MESH
BF = jnp.bfloat16
F32 = jnp.float32
NEAR = (1, 3, 2)
SPLIT1, PIECE1, WIDE1, PACK1 = ((0, QKV),), 128, QKV, QKV + 128
SPLIT3, PIECE3, WIDE3, PACK3 = ((0, OUT),), 128, OUT, OUT + 128
SPLIT2, PIECE2, WIDE2, PACK2 = ((0, HID), (HID, 2 * HID)), 384, 2 * HID, 2 * HID + 384
CUT1, CUT2, CUT3 = 512, 1408, 256
LINE = tuple(
    tuple((a, 1) for a, on in (("yl", i & 4), ("yh", i & 2), ("c", i & 1)) if on)
    for i in range(1, 8)
)
ALL_PEERS = LINE + tuple(((a, s),) for a in ("x", "z") for s in NEAR)


def ahead(axis, step):
    return lax.rem(lax.axis_index(axis) + step, SIZE[axis])


def peer(moves):
    return {axis: ahead(axis, step) for axis, step in moves}


def greet(peers):
    barrier = pltpu.get_barrier_semaphore()
    for moves in peers:
        pl.semaphore_signal(barrier, inc=1, device_id=peer(moves), device_id_type=MESH)
    pl.semaphore_wait(barrier, len(peers))


def send(src, dst, sems, k, axis, step=1):
    return send_to(src, dst, sems, k, ((axis, step),))


def link_to(src, dst, sems, k, moves):
    return pltpu.make_async_remote_copy(
        src_ref=src,
        dst_ref=dst,
        send_sem=sems.at[0, k],
        recv_sem=sems.at[1, k],
        device_id=peer(moves),
        device_id_type=MESH,
    )


def link(src, dst, sems, k, axis, step=1):
    return link_to(src, dst, sems, k, ((axis, step),))


def send_to(src, dst, sems, k, moves):
    copy = link_to(src, dst, sems, k, moves)
    copy.start()
    return copy


def ranks():
    yh, c = lax.axis_index("yh"), lax.axis_index("c")
    return yh * 2 + c, (1 - yh) * 2 + c, yh * 2 + 1 - c, (1 - yh) * 2 + 1 - c


class RowGather:
    def __init__(self, rows, sems):
        self.over, self.sib, self.fwd = [], [], []
        mine, far = ranks()[:2]
        for j in range(CHUNKS):
            blk = rows.at[mine, pl.ds(j * CH, CH)]
            self.over.append(link(blk, blk, sems, 3 * j, "yh"))
            self.sib.append(link(blk, blk, sems, 3 * j + 1, "c"))
            blk = rows.at[far, pl.ds(j * CH, CH)]
            self.fwd.append(link(blk, blk, sems, 3 * j + 2, "c"))

    def put(self, j):
        self.over[j].start()
        self.sib[j].start()

    def forward(self, j):
        self.over[j].wait_recv()
        self.fwd[j].start()

    def chip(self):
        for j in range(CHUNKS):
            self.sib[j].wait_recv()

    def rest(self):
        for j in range(CHUNKS):
            self.fwd[j].wait_recv()

    def end(self):
        for j in range(CHUNKS):
            self.over[j].wait_send()
            self.sib[j].wait_send()
            self.fwd[j].wait_send()


class TpSum:
    def __init__(self, part, first, second, out, sems):
        self.part, self.first, self.second, self.out = part, first, second, out
        self.cross = link(part.at[ranks()[3]], first.at[0], sems, 0, "c")
        self.sib = link(part.at[ranks()[2]], first.at[1], sems, 1, "c")
        self.over = []
        for j in range(CHUNKS):
            rows = pl.ds(j * CH, CH)
            self.over.append(link(out.at[rows], second.at[rows], sems, 2 + j, "yh"))

    def start_cross(self):
        self.cross.start()

    def start_sib(self):
        self.sib.start()

    def middle(self):
        over = ranks()[1]
        self.cross.wait_recv()
        for j in range(CHUNKS):
            rows = pl.ds(j * CH, CH)
            self.out[rows] = (
                self.part[over, rows].astype(F32) + self.first[0, rows].astype(F32)
            ).astype(BF)
            self.over[j].start()

    def total(self, j):
        mine = ranks()[0]
        rows = pl.ds(j * CH, CH)
        if j == 0:
            self.sib.wait_recv()
        self.over[j].wait_recv()
        return (
            self.part[mine, rows].astype(F32)
            + self.first[1, rows].astype(F32)
            + self.second[rows].astype(F32)
        )

    def end(self):
        self.cross.wait_send()
        self.sib.wait_send()
        for copy in self.over:
            copy.wait_send()


class WeightGather:
    def __init__(self, held, cut, sems, ring=False):
        self.held, self.cut, self.ring, self.done = held, cut, ring, []
        self.s0, self.sa, self.sb = sems
        self.yl, self.z, self.x = (lax.axis_index(a) for a in FSDP)
        self.lo, self.hi = pl.ds(0, cut), pl.ds(cut, held.shape[-1] - cut)

    def start(self):
        blk = self.held.at[self.yl, self.z, self.x]
        self.zero = send(blk, blk, self.s0, 0, "yl")

    def step1(self):
        self.zero.wait_recv()
        self.one = []
        for k, step in enumerate(NEAR):
            blk = self.held.at[:, self.z, self.x, :, self.lo]
            self.one.append(send(blk, blk, self.sa, k, "x", step))
            blk = self.held.at[:, self.z, self.x, :, self.hi]
            self.one.append(send(blk, blk, self.sb, k, "z", step))

    def plan2(self):
        self.two = []
        for k, step in enumerate(NEAR[:2] if self.ring else NEAR):
            blk = self.held.at[:, self.z, :, :, self.lo]
            self.two.append(link(blk, blk, self.sa, 3 + k, "z", step))
            blk = self.held.at[:, :, self.x, :, self.hi]
            self.two.append(link(blk, blk, self.sb, 3 + k, "x", step))

    def go2(self):
        for copy in self.one:
            copy.wait_recv()
        for copy in self.two:
            copy.start()

    def step2(self):
        self.plan2()
        self.go2()

    def relay(self):
        for copy in self.two:
            copy.wait_recv()
        wide = self.held.shape[-1]
        more = []
        for k, (step, back) in enumerate(((1, 3), (3, 1))):
            mid = self.cut // 256 * 128
            at = pl.ds(0, mid) if k == 0 else pl.ds(mid, self.cut - mid)
            blk = self.held.at[:, ahead("z", back), :, :, at]
            more.append(send(blk, blk, self.sa, 5 + k, "z", step))
            mid = (wide - self.cut) // 256 * 128
            at = pl.ds(self.cut, mid) if k == 0 else pl.ds(self.cut + mid, wide - self.cut - mid)
            blk = self.held.at[:, :, ahead("x", back), :, at]
            more.append(send(blk, blk, self.sb, 5 + k, "x", step))
        self.done, self.two = self.two, more

    def finish(self):
        for copy in self.two:
            copy.wait_recv()

    def end(self):
        self.zero.wait_send()
        for copy in self.one + self.two + self.done:
            copy.wait_send()


class GradScatter:
    def __init__(self, held, cut, bufs):
        self.held, self.cut = held, cut
        (
            self.ra1, self.rb1, self.qa, self.qb, self.ra2, self.rb2, self.ta, self.tb,
            self.ra3, self.rb3, self.sa, self.sb,
        ) = bufs
        self.yl, self.z, self.x = (lax.axis_index(a) for a in FSDP)
        self.lo, self.hi = pl.ds(0, cut), pl.ds(cut, held.shape[-1] - cut)

    def plan1(self):
        self.one = []
        for k, step in enumerate(NEAR):
            src = self.held.at[:, ahead("z", step), :, :, self.lo]
            self.one.append(link(src, self.ra1.at[k], self.sa, k, "z", step))
            src = self.held.at[:, :, ahead("x", step), :, self.hi]
            self.one.append(link(src, self.rb1.at[k], self.sb, k, "x", step))

    def go1(self):
        for copy in self.one:
            copy.start()

    def step1(self):
        self.plan1()
        self.go1()

    def step2(self):
        for copy in self.one:
            copy.wait_recv()

        def add(n, carry):
            a, b = n // 4, n % 4
            at_a = self.held[a, self.z, b, :, self.lo].astype(F32)
            at_b = self.held[a, b, self.x, :, self.hi].astype(F32)
            for k in range(3):
                at_a = at_a + self.ra1[k, a, b].astype(F32)
                at_b = at_b + self.rb1[k, a, b].astype(F32)
            self.qa[a, b] = at_a.astype(BF)
            self.qb[a, b] = at_b.astype(BF)
            return carry

        lax.fori_loop(0, 8, add, 0)
        self.two = []
        for k, step in enumerate(NEAR):
            src = self.qa.at[:, ahead("x", step)]
            self.two.append(send(src, self.ra2.at[k], self.sa, 3 + k, "x", step))
            src = self.qb.at[:, ahead("z", step)]
            self.two.append(send(src, self.rb2.at[k], self.sb, 3 + k, "z", step))

    def step3(self):
        for copy in self.two:
            copy.wait_recv()
        for a in range(2):
            at_a = self.qa[a, self.x].astype(F32)
            at_b = self.qb[a, self.z].astype(F32)
            for k in range(3):
                at_a = at_a + self.ra2[k, a].astype(F32)
                at_b = at_b + self.rb2[k, a].astype(F32)
            self.ta[a] = at_a.astype(BF)
            self.tb[a] = at_b.astype(BF)
        self.three = [
            send(self.ta.at[1 - self.yl], self.ra3, self.sa, 6, "yl"),
            send(self.tb.at[1 - self.yl], self.rb3, self.sb, 6, "yl"),
        ]

    def finish(self, flat, wide, piece):
        for copy in self.three:
            copy.wait_recv()
        half = self.cut
        fa = self.ta[self.yl].astype(F32) + self.ra3[...].astype(F32)
        fb = self.tb[self.yl].astype(F32) + self.rb3[...].astype(F32)
        flat[0:MAIN, 0:half] = fa
        flat[0:MAIN, half:wide] = fb[:, : wide - half]
        for j in range(wide // piece):
            flat[MAIN:SHARD, j * piece : (j + 1) * piece] = fb[4 * j : 4 * j + 4, wide - half :]

    def end(self):
        for copy in self.one + self.two + self.three:
            copy.wait_send()


def scatter_scratch(cut, lanes):
    shapes = ((3, 2, 4, MAIN), (2, 4, MAIN), (3, 2, MAIN), (2, MAIN), (MAIN,))
    return [pltpu.VMEM((*s, n), BF) for s in shapes for n in (cut, lanes - cut)] + [
        pltpu.SemaphoreType.DMA((2, 7)),
        pltpu.SemaphoreType.DMA((2, 7)),
    ]


def tail_pieces(b, e, piece):
    j = b
    while j < e:
        p = j // piece
        stop = min(e, (p + 1) * piece)
        yield p, j, stop
        j = stop


def unpack(held, refs, split, piece, wide):
    def band(g, carry):
        for j in range(4):
            src = held.at[g // 4, g % 4, j]
            for ref, (b, e) in zip(refs, split):
                ref[g, SHARD * j : SHARD * j + MAIN, :] = src[:, b:e]
                for p, lo, hi in tail_pieces(b, e, piece):
                    ref[g, SHARD * j + MAIN : SHARD * (j + 1), lo - b : hi - b] = src[
                        4 * p : 4 * p + 4, wide + lo - p * piece : wide + hi - p * piece
                    ]
        return carry

    lax.fori_loop(0, 8, band, 0)


def pack(held, grad, b, e, piece, wide):
    def band(g, carry):
        for j in range(4):
            dst = held.at[g // 4, g % 4, j]
            dst[:, b:e] = grad[g, SHARD * j : SHARD * j + MAIN, : e - b].astype(BF)
            for p, lo, hi in tail_pieces(b, e, piece):
                dst[4 * p : 4 * p + 4, wide + lo - p * piece : wide + hi - p * piece] = grad[
                    g, SHARD * j + MAIN : SHARD * (j + 1), lo - b : hi - b
                ].astype(BF)
        return carry

    lax.fori_loop(0, 8, band, 0)


def pack_own(dst, flat, wide, piece):
    dst[:, 0:wide] = flat[0:MAIN, 0:wide].astype(BF)
    for p in range(wide // piece):
        dst[4 * p : 4 * p + 4, wide : wide + piece] = flat[
            MAIN:SHARD, p * piece : (p + 1) * piece
        ].astype(BF)
    rest = 4 * (wide // piece)
    dst[rest:MAIN, wide : wide + piece] = jnp.zeros((MAIN - rest, piece), BF)


def layer_norm(stream):
    average = jnp.mean(stream, -1, keepdims=True)
    centered = stream - average
    variance = jnp.mean(centered * centered, -1, keepdims=True)
    inverse = lax.rsqrt(variance + EPS)
    return centered * inverse, inverse


def norm_back(upstream, normed, inverse, gain_vec):
    scaled = upstream * gain_vec
    return inverse * (
        scaled
        - jnp.mean(scaled, -1, keepdims=True)
        - normed * jnp.mean(scaled * normed, -1, keepdims=True)
    )


def gelu_parts(pre_act):
    square = pre_act * pre_act
    tangent = jnp.tanh(pre_act * (GELU_C + GELU_C * CUBIC * square))
    share = 0.5 + 0.5 * tangent
    value = pre_act * share
    slope = share + value * (1.0 - tangent) * (GELU_C + 3.0 * GELU_C * CUBIC * square)
    return value, slope


def nn(a, b):
    return lax.dot_general(a, b, (((1,), (0,)), ((), ())), preferred_element_type=F32)


def nt(a, b):
    return lax.dot_general(a, b, (((1,), (1,)), ((), ())), preferred_element_type=F32)


def whole(ref):
    return ref[...].reshape(D, ref.shape[-1])


def vec(ref):
    return ref[...].reshape(1, -1)


def pick(ref, rank, width):
    flat = vec(ref)
    out = flat[:, 0:width]
    for r in range(1, 4):
        out = jnp.where(rank == r, flat[:, r * width : (r + 1) * width], out)
    return out


def layer_kernel(
    stream, valid, pre_gain, pre_shift, wq, bq, wk, wv, bv, wo, out_bias, mid_gain, mid_shift,
    wu, bu, wd, down_bias, cot,
    block_out, input_grad, gq, gk, gv, go, gu, gd, early_out, late_out,
    held1, held2, held3, flat1, flat2, flat3, wqkv, wout, wup, wdown, arows, crows, mrows, grows,
    qkv, mixed, dmix, mask, logsum, hidden, act, grad, flip, part1, dk_acc, dv_acc, qv,
    upsum, bqkv, bhid, early, early_in, late, late_in,
    s1y, s1a, s1b, s2y, s2a, s2b, s3y, s3a, s3b, ra, rc, rm, rg, se, sl,
    f1, f2, f3, fs, h1, h2, h3, hs, *scat,
):
    rank, over, sib, cross = ranks()
    yl, z, x = (lax.axis_index(a) for a in FSDP)
    yh, c = (lax.axis_index(a) for a in TP)
    greet(ALL_PEERS)
    gat1 = WeightGather(held1, CUT1, (s1y, s1a, s1b))
    gat2 = WeightGather(held2, CUT2, (s2y, s2a, s2b), ring=True)
    gat3 = WeightGather(held3, CUT3, (s3y, s3a, s3b))

    flat1[:, 0:COLS] = wq[...].astype(F32)
    flat1[:, COLS : 2 * COLS] = wk[...].astype(F32)
    flat1[:, 2 * COLS : 3 * COLS] = wv[...].astype(F32)
    flat1[:, 3 * COLS : QKV] = jnp.zeros((SHARD, QKV - 3 * COLS), F32)
    pack_own(held1.at[yl, z, x], flat1, WIDE1, PIECE1)
    gat1.start()

    rows_a, rows_c = RowGather(arows, ra), RowGather(crows, rc)
    for j in range(CHUNKS):
        at = pl.ds(j * CH, CH)
        normed, _ = layer_norm(stream[at])
        arows[rank, at] = (normed * vec(pre_gain) + vec(pre_shift)).astype(BF)
        rows_a.put(j)

    gat1.step1()
    flat3[:, 0:COLS] = wo[...].astype(F32)
    flat3[:, COLS:] = jnp.zeros((SHARD, OUT - COLS), F32)
    pack_own(held3.at[yl, z, x], flat3, WIDE3, PIECE3)
    gat3.start()
    for at in (0, HID):
        flat2[:, at + HID - 128 : at + HID] = jnp.zeros((SHARD, 128), F32)
    flat2[:, 0:TRUE_HID] = wu[...].astype(F32)
    flat2[:, HID : HID + TRUE_HID] = wd[...].astype(F32)
    pack_own(held2.at[yl, z, x], flat2, WIDE2, PIECE2)
    gat2.start()
    gat1.step2()
    gat3.step1()
    for j in range(CHUNKS):
        rows_a.forward(j)
    crows[rank] = cot[...].astype(BF)
    for j in range(CHUNKS):
        rows_c.put(j)
    live = jnp.broadcast_to(valid[...].astype(F32), (128, SEQ)).T
    mask[...] = jnp.where(live > 0, 0.0, -jnp.inf)
    bqkv[...] = jnp.zeros_like(bqkv)
    bqkv[:, 0:COLS] = pick(bq, rank, COLS)
    bqkv[:, 2 * COLS : 3 * COLS] = pick(bv, rank, COLS)
    bhid[...] = jnp.zeros_like(bhid)
    bhid[:, 0:TRUE_HID] = pick(bu, rank, TRUE_HID)
    mixed[...] = jnp.zeros_like(mixed)
    upsum[...] = jnp.zeros_like(upsum)
    qv[...] = jnp.zeros_like(qv)
    dk_acc[...] = jnp.zeros_like(dk_acc)
    dv_acc[...] = jnp.zeros_like(dv_acc)
    rows_a.chip()
    rows_a.rest()
    gat1.finish()
    gat3.step2()
    gat2.step1()
    unpack(held1, (wqkv,), SPLIT1, PIECE1, WIDE1)

    def project(r, carry):
        at = pl.ds(pl.multiple_of(r * ROWS, ROWS), ROWS)
        qkv[at] = (nn(arows[r], whole(wqkv)) + bqkv[...]).astype(BF)
        return carry

    lax.fori_loop(0, 4, project, 0)
    for j in range(CHUNKS):
        rows_c.forward(j)

    def head_slices(h):
        lo = HD * h
        return (
            qkv[:, COLS + lo : COLS + lo + HD],
            qkv[:, 2 * COLS + lo : 2 * COLS + lo + HD],
        )

    def half_rows(chip):
        return pl.ds(pl.multiple_of(chip * QC, QC), QC)

    def scores_of(h, at):
        query = qkv[at, :][:, HD * h : HD * h + HD]
        key = head_slices(h)[0]
        bias = mask[...]
        return nt(key, query) * SCALE + jnp.concatenate([bias] * (QC // 128), 1), query

    def attend(chip):
        at = half_rows(chip)
        for h in range(HEADS):
            scores, _ = scores_of(h, at)
            top = jnp.max(scores, 0, keepdims=True)
            raised = jnp.exp(scores - top)
            total = jnp.sum(raised, 0, keepdims=True)
            logsum[h, chip] = top + jnp.log(total)
            probs = (raised * (1.0 / total)).astype(BF)
            value = head_slices(h)[1]
            o_t = lax.dot_general(
                value, probs, (((0,), (0,)), ((), ())), preferred_element_type=F32
            )
            mixed[at, HD * h : HD * h + HD] = o_t.T.astype(BF)

    def out_block(r):
        at = pl.ds(pl.multiple_of(r * ROWS, ROWS), ROWS)
        part1[r] = nt(mixed[at], whole(wout)).astype(BF)

    sum1 = TpSum(part1, f1, f2, f3, fs)
    gat2.plan2()

    def out_pair(a, b):
        def step(n, carry):
            out_block((1 - n) * a + n * b)
            return carry

        lax.fori_loop(0, 2, step, 0)

    def attend_step(n, carry):
        attend((1 - yh) + n * (2 * yh - 1))

        @pl.when(n == 0)
        def _():
            gat3.finish()
            unpack(held3, (wout,), SPLIT3, PIECE3, WIDE3)
            out_pair(cross, over)
            sum1.start_cross()
            gat2.go2()
            sum1.middle()

        return carry

    lax.fori_loop(0, 2, attend_step, 0)
    out_pair(sib, rank)
    sum1.start_sib()
    gat2.relay()
    rows_c.chip()
    rows_c.rest()
    rows_m = RowGather(mrows, rm)
    for j in range(CHUNKS):
        at = pl.ds(j * CH, CH)
        mid = stream[at] + sum1.total(j) + vec(out_bias)
        block_out[at] = mid
        normed, _ = layer_norm(mid)
        mrows[rank, at] = (normed * vec(mid_gain) + vec(mid_shift)).astype(BF)
        rows_m.put(j)
    sum1.end()
    gat2.finish()
    unpack(held2, (wup, wdown), SPLIT2, PIECE2, WIDE2)

    sum2 = TpSum(part1, f1, f2, f3, fs)

    def mlp_step(n, carry):
        @pl.when(n == 2)
        def _():
            sum2.start_sib()
            for j in range(CHUNKS):
                rows_m.forward(j)
            rows_m.rest()

        far, odd = n // 2, n % 2
        r = 2 * (yh + far * (1 - 2 * yh)) + c + odd * (1 - 2 * c)
        pre_act = nn(mrows[r], whole(wup)) + bhid[...]
        value, slope = gelu_parts(pre_act)
        hidden[r] = value.astype(BF)
        act_grad = nn(crows[r], whole(wdown)) * slope
        act[r] = act_grad.astype(BF)
        upsum[...] += jnp.sum(act_grad, 0, keepdims=True)
        part1[r] = nt(act[r], whole(wup)).astype(BF)
        return carry

    rows_m.chip()
    lax.fori_loop(0, 4, mlp_step, 0)
    sum2.start_cross()
    sum2.middle()

    gat1.end()
    gat2.end()
    gat3.end()
    rows_m.end()
    sc1 = GradScatter(held1, CUT1, scat[:12])
    sc2 = GradScatter(held2, CUT2, scat[12:24])
    sc3 = GradScatter(held3, CUT3, scat[24:])

    def turn_rows(rows):
        for j in range(3):
            blk = rows[:, :, 384 * j : 384 * (j + 1)].reshape(SEQ, 384)
            flip[384 * j : 384 * (j + 1), :] = blk.T

    def product(right, width, held, base, piece, wide):
        for lo in range(0, width, 384):
            hi = min(lo + 384, width)
            grad[:, :, 0 : hi - lo] = nn(flip[...], right(slice(lo, hi))).reshape(8, BAND, hi - lo)
            pack(held, grad, base + lo, base + hi, piece, wide)

    def blank(held, piece, wide):
        used = 4 * (wide // piece)
        held[:, :, :, used:MAIN, wide : wide + piece] = jnp.zeros((2, 4, 4, MAIN - used, piece), BF)

    turn_rows(mrows)
    product(lambda at: act[:, :, at].reshape(SEQ, 384), HID, held2, 0, PIECE2, WIDE2)
    turn_rows(crows)
    product(lambda at: hidden[:, :, at].reshape(SEQ, 384), HID, held2, HID, PIECE2, WIDE2)
    blank(held2, PIECE2, WIDE2)
    sc2.step1()

    rows_g = RowGather(grows, rg)
    sums = [jnp.zeros((1, D), F32)] * 4
    for j in range(CHUNKS):
        at = pl.ds(j * CH, CH)
        normed, inverse = layer_norm(block_out[at])
        g = sum2.total(j)
        back = cot[at] + norm_back(g, normed, inverse, vec(mid_gain))
        input_grad[at] = back
        grows[rank, at] = back.astype(BF)
        rows_g.put(j)
        for k, v in enumerate((back, g * normed, g, cot[at])):
            sums[k] = sums[k] + jnp.sum(v, 0, keepdims=True)
    early[0] = jnp.zeros((8, D), F32)
    for k in range(4):
        early[0, k : k + 1, :] = sums[k]
    early[0, pl.ds(4 + rank, 1), :] = upsum[...]
    ec = [send(early.at[0], early_in.at[0], se, 0, "c")]
    sum2.end()

    def down_block(r, carry):
        mrows[r] = nt(hidden[r], whole(wdown)).astype(BF)
        return carry

    lax.fori_loop(0, 4, down_block, 0)
    sum3 = TpSum(mrows, h1, h2, h3, hs)
    sum3.start_cross()
    sum3.start_sib()
    ec[0].wait_recv()
    early[1] = early[0] + early_in[0]
    ec.append(send(early.at[1], early_in.at[1], se, 1, "yh"))

    def mix_back(a, b):
        def step(n, carry):
            r = (1 - n) * a + n * b
            at = pl.ds(pl.multiple_of(r * ROWS, ROWS), ROWS)
            dmix[at] = nn(grows[r], whole(wout)).astype(BF)
            return carry

        lax.fori_loop(0, 2, step, 0)

    def attend_back(chip, between):
        at = half_rows(chip)
        for h in range(HEADS):
            lo = HD * h
            if h == 3:
                between()
            scores, query = scores_of(h, at)
            probs = jnp.exp(scores - logsum[h, chip])
            key, value = head_slices(h)
            dout = dmix[at, :][:, lo : lo + HD]
            dv_acc[h] += nn(probs.astype(BF), dout)
            prob_grad = nt(value, dout)
            delta = jnp.sum(probs * prob_grad, 0, keepdims=True)
            ds = (probs * (prob_grad - delta) * SCALE).astype(BF)
            dk_acc[h] += nn(ds, query)
            dq = lax.dot_general(
                key, ds, (((0,), (0,)), ((), ())), preferred_element_type=F32
            ).T
            qv[0:1, lo : lo + HD] += jnp.sum(dq, 0, keepdims=True)
            qkv[at, lo : lo + HD] = dq.astype(BF)

    rows_g.chip()
    mix_back(rank, sib)
    sum3.middle()
    sc3.plan1()

    def back_step(n, carry):
        def between():
            @pl.when(n == 0)
            def _():
                for j in range(CHUNKS):
                    rows_g.forward(j)

        attend_back(yh + n * (1 - 2 * yh), between)

        @pl.when(n == 0)
        def _():
            rows_g.rest()
            mix_back(over, cross)
            turn_rows(grows)
            product(lambda at: mixed[:, at], OUT, held3, 0, PIECE3, WIDE3)
            blank(held3, PIECE3, WIDE3)
            sc3.go1()

        return carry

    lax.fori_loop(0, 2, back_step, 0)
    ec[1].wait_recv()
    early[2] = early[1] + early_in[1]
    ec.append(send(early.at[2], early_in.at[2], se, 2, "yl"))
    for h in range(HEADS):
        lo = HD * h
        qv[0:1, COLS + lo : COLS + lo + HD] = jnp.sum(dv_acc[h], 0, keepdims=True)
        qkv[:, COLS + lo : COLS + lo + HD] = dk_acc[h].astype(BF)
        qkv[:, 2 * COLS + lo : 2 * COLS + lo + HD] = dv_acc[h].astype(BF)
    qkv[:, 3 * COLS : QKV] = jnp.zeros((SEQ, QKV - 3 * COLS), BF)

    def attn_block(r):
        at = pl.ds(pl.multiple_of(r * ROWS, ROWS), ROWS)
        part1[r] = nt(qkv[at], whole(wqkv)).astype(BF)

    sum4 = TpSum(part1, f1, f2, f3, fs)
    attn_block(cross)
    sum4.start_cross()
    attn_block(over)
    sum4.middle()
    attn_block(sib)
    sum4.start_sib()
    attn_block(rank)
    turn_rows(arows)
    product(lambda at: qkv[:, at], QKV, held1, 0, PIECE1, WIDE1)
    blank(held1, PIECE1, WIDE1)
    sc1.step1()
    ec[2].wait_recv()
    early[3] = early[2] + early_in[2]
    for k, step in enumerate(NEAR):
        ec.append(send(early.at[3], early_in.at[3 + x], se, 3 + k, "x", step))
    early_in[3 + x] = early[3]
    sc2.step2()
    sc3.step2()
    for copy in ec[3:6]:
        copy.wait_recv()
    early[4] = early_in[3] + early_in[4] + early_in[5] + early_in[6]
    for k, step in enumerate(NEAR):
        ec.append(send(early.at[4], early_in.at[7 + z], se, 6 + k, "z", step))
    early_in[7 + z] = early[4]

    sums = [jnp.zeros((1, D), F32)] * 2
    for j in range(CHUNKS):
        at = pl.ds(j * CH, CH)
        normed, inverse = layer_norm(stream[at])
        g = sum4.total(j)
        input_grad[at] = input_grad[at] + norm_back(g, normed, inverse, vec(pre_gain))
        for k, v in enumerate((g * normed, g)):
            sums[k] = sums[k] + jnp.sum(v, 0, keepdims=True)
    late[0] = jnp.zeros((8, D), F32)
    late[0, 0:1, :] = sums[0]
    late[0, 1:2, :] = sums[1]
    late[0, pl.ds(4 + rank, 1), :] = qv[...]
    here = yl * 4 + yh * 2 + c
    lc = [
        send_to(late.at[0], late_in.at[here], sl, k, moves) for k, moves in enumerate(LINE)
    ]
    late_in[here] = late[0]
    for j in range(CHUNKS):
        at = pl.ds(j * CH, CH)
        block_out[at] = block_out[at] + sum3.total(j) + vec(down_bias)
    sc1.step2()
    for copy in lc:
        copy.wait_recv()
    late[1] = sum((late_in[k] for k in range(1, 8)), late_in[0])
    for k, step in enumerate(NEAR):
        lc.append(send(late.at[1], late_in.at[8 + x], sl, 7 + k, "x", step))
    late_in[8 + x] = late[1]
    sc2.step3()
    sc3.step3()
    for copy in lc[7:10]:
        copy.wait_recv()
    late[2] = late_in[8] + late_in[9] + late_in[10] + late_in[11]
    for k, step in enumerate(NEAR):
        lc.append(send(late.at[2], late_in.at[12 + z], sl, 10 + k, "z", step))
    late_in[12 + z] = late[2]
    sc1.step3()
    sc2.finish(flat2, WIDE2, PIECE2)
    gu[...] = flat2[:, 0:TRUE_HID]
    gd[...] = flat2[:, HID : HID + TRUE_HID]
    sc3.finish(flat3, WIDE3, PIECE3)
    go[...] = flat3[:, 0:COLS]
    for copy in ec[6:9]:
        copy.wait_recv()
    early_out[...] = early_in[7] + early_in[8] + early_in[9] + early_in[10]
    for copy in lc[10:13]:
        copy.wait_recv()
    late_out[...] = late_in[12] + late_in[13] + late_in[14] + late_in[15]
    sc1.finish(flat1, WIDE1, PIECE1)
    gq[...] = flat1[:, 0:COLS]
    gk[...] = flat1[:, COLS : 2 * COLS]
    gv[...] = flat1[:, 2 * COLS : 3 * COLS]
    for copy in ec + lc:
        copy.wait_send()
    for item in (rows_a, rows_c, rows_g, sum3, sum4, sc1, sc2, sc3):
        item.end()


def split_kernel(*refs):
    early, late = refs[8:10]
    outs = refs[10:]
    for k in range(8):
        outs[k][...] = refs[k][...]

    def joined(ref, lo, width):
        rows = [ref[4 + r : 5 + r, lo : lo + width] for r in range(4)]
        return jnp.concatenate(rows, 1).reshape(4 * width)

    pregain, preshift, query, value, outbias, midgain, midshift, up, downbias = outs[8:]
    pregain[...] = late[0]
    preshift[...] = late[1]
    query[...] = joined(late, 0, COLS)
    value[...] = joined(late, COLS, COLS)
    outbias[...] = early[0]
    midgain[...] = early[1]
    midshift[...] = early[2]
    downbias[...] = early[3]
    up[...] = joined(early, 0, TRUE_HID)


def per_device(*args):
    (
        residual, valid_keys, pre_gain, pre_shift, wq, bq, wk, wv, bv, wo, out_bias, mid_gain,
        mid_shift, wu, bu, wd, down_bias, cotangent,
    ) = args
    vm = pl.BlockSpec(memory_space=pltpu.VMEM)
    ins = (
        residual[0], valid_keys, pre_gain, pre_shift, wq, bq, wk, wv, bv, wo.T, out_bias,
        mid_gain, mid_shift, wu, bu, wd.T, down_bias, cotangent[0],
    )
    arrays = [
        (ROWS, D), (ROWS, D), (SHARD, COLS), (SHARD, COLS), (SHARD, COLS), (SHARD, COLS),
        (SHARD, TRUE_HID), (SHARD, TRUE_HID),
    ]
    outs = arrays + [(8, D), (8, D)]
    rows = (4, ROWS, D)
    dma = lambda *n: pltpu.SemaphoreType.DMA(n)
    tp_sum = [
        pltpu.VMEM((2, ROWS, D), BF),
        pltpu.VMEM((ROWS, D), BF),
        pltpu.VMEM((ROWS, D), BF),
        dma(2, 2 + CHUNKS),
    ]
    scratch = [
        pltpu.VMEM((2, 4, 4, MAIN, PACK1), BF),
        pltpu.VMEM((2, 4, 4, MAIN, PACK2), BF),
        pltpu.VMEM((2, 4, 4, MAIN, PACK3), BF),
        pltpu.VMEM((SHARD, WIDE1), F32),
        pltpu.VMEM((SHARD, WIDE2), F32),
        pltpu.VMEM((SHARD, WIDE3), F32),
        pltpu.VMEM((8, BAND, QKV), BF),
        pltpu.VMEM((8, BAND, OUT), BF),
        pltpu.VMEM((8, BAND, HID), BF),
        pltpu.VMEM((8, BAND, HID), BF),
        pltpu.VMEM(rows, BF),
        pltpu.VMEM(rows, BF),
        pltpu.VMEM(rows, BF),
        pltpu.VMEM(rows, BF),
        pltpu.VMEM((SEQ, QKV), BF),
        pltpu.VMEM((SEQ, OUT), BF),
        pltpu.VMEM((SEQ, OUT), BF),
        pltpu.VMEM((SEQ, 128), F32),
        pltpu.VMEM((HEADS, SEQ // QC, 1, QC), F32),
        pltpu.VMEM(rows, BF),
        pltpu.VMEM(rows, BF),
        pltpu.VMEM((8, BAND, 384), F32),
        pltpu.VMEM((D, SEQ), BF),
        pltpu.VMEM(rows, BF),
        pltpu.VMEM((HEADS, SEQ, HD), F32),
        pltpu.VMEM((HEADS, SEQ, HD), F32),
        pltpu.VMEM((1, D), F32),
        pltpu.VMEM((1, HID), F32),
        pltpu.VMEM((1, QKV), F32),
        pltpu.VMEM((1, HID), F32),
        pltpu.VMEM((5, 8, D), F32),
        pltpu.VMEM((11, 8, D), F32),
        pltpu.VMEM((3, 8, D), F32),
        pltpu.VMEM((16, 8, D), F32),
        *([dma(2, 1), dma(2, 7), dma(2, 7)] * 3),
        *([dma(2, 3 * CHUNKS)] * 4),
        dma(2, 9),
        dma(2, 13),
        *tp_sum,
        *tp_sum,
        *scatter_scratch(CUT1, PACK1),
        *scatter_scratch(CUT2, PACK2),
        *scatter_scratch(CUT3, PACK3),
    ]
    out = pl.pallas_call(
        layer_kernel,
        name="layer",
        out_shape=[jax.ShapeDtypeStruct(s, F32) for s in outs],
        in_specs=[vm] * len(ins),
        out_specs=[vm] * len(outs),
        scratch_shapes=scratch,
        compiler_params=pltpu.CompilerParams(
            collective_id=0, has_side_effects=True, vmem_limit_bytes=63 * 2**20
        ),
    )(*ins)
    ends = arrays + [(D,)] * 7 + [(4 * TRUE_HID,), (D,)]
    done = pl.pallas_call(
        split_kernel,
        name="split",
        out_shape=[jax.ShapeDtypeStruct(s, F32) for s in ends],
        in_specs=[vm] * len(out),
        out_specs=[vm] * len(ends),
    )(*out)
    return (
        done[0][None], done[1][None], done[2], done[3], done[4], done[5].T, done[6], done[7].T,
        *done[8:],
    )


def solution(mesh):
    split = Mesh(mesh.devices.reshape(2, 4, 4, 2, 2), ("yl", "z", "x", "yh", "c"))
    rows3 = P(FSDP, TP, None)
    down_cols = P(FSDP, TP)
    across = P(TP, FSDP)
    return jax.shard_map(
        per_device,
        mesh=split,
        in_specs=(
            rows3, P(FSDP, None), P(), P(), down_cols, P(), down_cols, down_cols, P(), across,
            P(), P(), P(), down_cols, P(), across, P(), rows3,
        ),
        out_specs=(
            rows3, rows3, down_cols, down_cols, down_cols, across, down_cols, across,
            P(), P(), P(), P(), P(), P(), P(), P(), P(),
        ),
        check_vma=False,
    )
```

```python
import math

import jax
import jax.numpy as jnp
from jax import lax
from jax.experimental import pallas as pl
from jax.experimental.pallas import tpu as pltpu
from jax.sharding import Mesh
from jax.sharding import PartitionSpec as P

HD = 72
HEADS = 4
COLS = HEADS * HD
D = 1152
SEQ = 768
ROWS = 192
CHUNKS = 2
CH = ROWS // CHUNKS
SHARD = 36
MAIN = 32
BAND = 4 * SHARD
QKV = 896
OUT = 384
HID = 1152
TRUE_HID = 1076
QC = 384
EPS = 1e-06
GELU_C = math.sqrt(2.0 / math.pi)
CUBIC = 0.044715
SCALE = 1.0 / math.sqrt(HD)
SIZE = {"yl": 2, "z": 4, "x": 4, "yh": 2, "c": 2}
FSDP = ("yl", "z", "x")
TP = ("yh", "c")
MESH = pl.DeviceIdType.MESH
BF = jnp.bfloat16
F32 = jnp.float32
NEAR = (1, 3, 2)
SPLIT1, PIECE1, WIDE1, PACK1 = ((0, QKV),), 128, QKV, QKV + 128
SPLIT3, PIECE3, WIDE3, PACK3 = ((0, OUT),), 128, OUT, OUT + 128
SPLIT2, PIECE2, WIDE2, PACK2 = ((0, HID), (HID, 2 * HID)), 384, 2 * HID, 2 * HID + 384
CUT1, CUT2, CUT3 = 512, 1408, 256
LINE = tuple(
    tuple((a, 1) for a, on in (("yl", i & 4), ("yh", i & 2), ("c", i & 1)) if on)
    for i in range(1, 8)
)
ALL_PEERS = LINE + tuple(((a, s),) for a in ("x", "z") for s in NEAR)


def ahead(axis, step):
    return lax.rem(lax.axis_index(axis) + step, SIZE[axis])


def peer(moves):
    return {axis: ahead(axis, step) for axis, step in moves}


def greet(peers):
    barrier = pltpu.get_barrier_semaphore()
    for moves in peers:
        pl.semaphore_signal(barrier, inc=1, device_id=peer(moves), device_id_type=MESH)
    return barrier


def send(src, dst, sems, k, axis, step=1):
    return send_to(src, dst, sems, k, ((axis, step),))


def link_to(src, dst, sems, k, moves):
    return pltpu.make_async_remote_copy(
        src_ref=src,
        dst_ref=dst,
        send_sem=sems.at[0, k],
        recv_sem=sems.at[1, k],
        device_id=peer(moves),
        device_id_type=MESH,
    )


def link(src, dst, sems, k, axis, step=1):
    return link_to(src, dst, sems, k, ((axis, step),))


def send_to(src, dst, sems, k, moves):
    copy = link_to(src, dst, sems, k, moves)
    copy.start()
    return copy


def ranks():
    yh, c = lax.axis_index("yh"), lax.axis_index("c")
    return yh * 2 + c, (1 - yh) * 2 + c, yh * 2 + 1 - c, (1 - yh) * 2 + 1 - c


class RowGather:
    def __init__(self, rows, sems):
        self.over, self.sib, self.fwd = [], [], []
        mine, far = ranks()[:2]
        for j in range(CHUNKS):
            blk = rows.at[mine, pl.ds(j * CH, CH)]
            self.over.append(link(blk, blk, sems, 3 * j, "yh"))
            self.sib.append(link(blk, blk, sems, 3 * j + 1, "c"))
            blk = rows.at[far, pl.ds(j * CH, CH)]
            self.fwd.append(link(blk, blk, sems, 3 * j + 2, "c"))

    def put(self, j):
        self.over[j].start()
        self.sib[j].start()

    def forward(self, j):
        self.over[j].wait_recv()
        self.fwd[j].start()

    def chip(self):
        for j in range(CHUNKS):
            self.sib[j].wait_recv()

    def rest(self):
        for j in range(CHUNKS):
            self.fwd[j].wait_recv()

    def end(self):
        for j in range(CHUNKS):
            self.over[j].wait_send()
            self.sib[j].wait_send()
            self.fwd[j].wait_send()


class TpSum:
    def __init__(self, part, first, second, out, sems):
        self.part, self.first, self.second, self.out = part, first, second, out
        self.cross = link(part.at[ranks()[3]], first.at[0], sems, 0, "c")
        self.sib = link(part.at[ranks()[2]], first.at[1], sems, 1, "c")
        self.over = []
        for j in range(CHUNKS):
            rows = pl.ds(j * CH, CH)
            self.over.append(link(out.at[rows], second.at[rows], sems, 2 + j, "yh"))

    def start_cross(self):
        self.cross.start()

    def start_sib(self):
        self.sib.start()

    def middle(self):
        over = ranks()[1]
        self.cross.wait_recv()
        for j in range(CHUNKS):
            rows = pl.ds(j * CH, CH)
            self.out[rows] = (
                self.part[over, rows].astype(F32) + self.first[0, rows].astype(F32)
            ).astype(BF)
            self.over[j].start()

    def total(self, j):
        mine = ranks()[0]
        rows = pl.ds(j * CH, CH)
        if j == 0:
            self.sib.wait_recv()
        self.over[j].wait_recv()
        return (
            self.part[mine, rows].astype(F32)
            + self.first[1, rows].astype(F32)
            + self.second[rows].astype(F32)
        )

    def end(self):
        self.cross.wait_send()
        self.sib.wait_send()
        for copy in self.over:
            copy.wait_send()


class WeightGather:
    def __init__(self, held, cut, sems, ring=False):
        self.held, self.cut, self.ring, self.done = held, cut, ring, []
        self.s0, self.sa, self.sb = sems
        self.yl, self.z, self.x = (lax.axis_index(a) for a in FSDP)
        self.lo, self.hi = pl.ds(0, cut), pl.ds(cut, held.shape[-1] - cut)

    def start(self):
        blk = self.held.at[self.yl, self.z, self.x]
        self.zero = send(blk, blk, self.s0, 0, "yl")

    def step1(self):
        self.zero.wait_recv()
        self.one = []
        for k, step in enumerate(NEAR):
            blk = self.held.at[:, self.z, self.x, :, self.lo]
            self.one.append(send(blk, blk, self.sa, k, "x", step))
            blk = self.held.at[:, self.z, self.x, :, self.hi]
            self.one.append(send(blk, blk, self.sb, k, "z", step))

    def plan2(self):
        self.two = []
        for k, step in enumerate(NEAR[:2] if self.ring else NEAR):
            blk = self.held.at[:, self.z, :, :, self.lo]
            self.two.append(link(blk, blk, self.sa, 3 + k, "z", step))
            blk = self.held.at[:, :, self.x, :, self.hi]
            self.two.append(link(blk, blk, self.sb, 3 + k, "x", step))

    def go2(self):
        for copy in self.one:
            copy.wait_recv()
        for copy in self.two:
            copy.start()

    def step2(self):
        self.plan2()
        self.go2()

    def relay(self):
        for copy in self.two:
            copy.wait_recv()
        wide = self.held.shape[-1]
        more = []
        for k, (step, back) in enumerate(((1, 3), (3, 1))):
            mid = self.cut // 256 * 128
            at = pl.ds(0, mid) if k == 0 else pl.ds(mid, self.cut - mid)
            blk = self.held.at[:, ahead("z", back), :, :, at]
            more.append(send(blk, blk, self.sa, 5 + k, "z", step))
            mid = (wide - self.cut) // 256 * 128
            at = pl.ds(self.cut, mid) if k == 0 else pl.ds(self.cut + mid, wide - self.cut - mid)
            blk = self.held.at[:, :, ahead("x", back), :, at]
            more.append(send(blk, blk, self.sb, 5 + k, "x", step))
        self.done, self.two = self.two, more

    def finish(self):
        for copy in self.two:
            copy.wait_recv()

    def end(self):
        self.zero.wait_send()
        for copy in self.one + self.two + self.done:
            copy.wait_send()


class GradScatter:
    def __init__(self, held, cut, bufs):
        self.held, self.cut = held, cut
        (
            self.ra1, self.rb1, self.qa, self.qb, self.ra2, self.rb2, self.ta, self.tb,
            self.ra3, self.rb3, self.sa, self.sb,
        ) = bufs
        self.yl, self.z, self.x = (lax.axis_index(a) for a in FSDP)
        self.lo, self.hi = pl.ds(0, cut), pl.ds(cut, held.shape[-1] - cut)

    def plan1(self):
        self.one = []
        for k, step in enumerate(NEAR):
            src = self.held.at[:, ahead("z", step), :, :, self.lo]
            self.one.append(link(src, self.ra1.at[k], self.sa, k, "z", step))
            src = self.held.at[:, :, ahead("x", step), :, self.hi]
            self.one.append(link(src, self.rb1.at[k], self.sb, k, "x", step))

    def go1(self):
        for copy in self.one:
            copy.start()

    def step1(self):
        self.plan1()
        self.go1()

    def step2(self):
        for copy in self.one:
            copy.wait_recv()

        def add(n, carry):
            a, b = n // 4, n % 4
            at_a = self.held[a, self.z, b, :, self.lo].astype(F32)
            at_b = self.held[a, b, self.x, :, self.hi].astype(F32)
            for k in range(3):
                at_a = at_a + self.ra1[k, a, b].astype(F32)
                at_b = at_b + self.rb1[k, a, b].astype(F32)
            self.qa[a, b] = at_a.astype(BF)
            self.qb[a, b] = at_b.astype(BF)
            return carry

        lax.fori_loop(0, 8, add, 0)
        self.two = []
        for k, step in enumerate(NEAR):
            src = self.qa.at[:, ahead("x", step)]
            self.two.append(send(src, self.ra2.at[k], self.sa, 3 + k, "x", step))
            src = self.qb.at[:, ahead("z", step)]
            self.two.append(send(src, self.rb2.at[k], self.sb, 3 + k, "z", step))

    def step3(self):
        for copy in self.two:
            copy.wait_recv()
        for a in range(2):
            at_a = self.qa[a, self.x].astype(F32)
            at_b = self.qb[a, self.z].astype(F32)
            for k in range(3):
                at_a = at_a + self.ra2[k, a].astype(F32)
                at_b = at_b + self.rb2[k, a].astype(F32)
            self.ta[a] = at_a.astype(BF)
            self.tb[a] = at_b.astype(BF)
        self.three = [
            send(self.ta.at[1 - self.yl], self.ra3, self.sa, 6, "yl"),
            send(self.tb.at[1 - self.yl], self.rb3, self.sb, 6, "yl"),
        ]

    def finish(self, flat, wide, piece):
        for copy in self.three:
            copy.wait_recv()
        half = self.cut
        fa = self.ta[self.yl].astype(F32) + self.ra3[...].astype(F32)
        fb = self.tb[self.yl].astype(F32) + self.rb3[...].astype(F32)
        flat[0:MAIN, 0:half] = fa
        flat[0:MAIN, half:wide] = fb[:, : wide - half]
        for j in range(wide // piece):
            flat[MAIN:SHARD, j * piece : (j + 1) * piece] = fb[4 * j : 4 * j + 4, wide - half :]

    def end(self):
        for copy in self.one + self.two + self.three:
            copy.wait_send()


def scatter_scratch(cut, lanes):
    shapes = ((3, 2, 4, MAIN), (2, 4, MAIN), (3, 2, MAIN), (2, MAIN), (MAIN,))
    return [pltpu.VMEM((*s, n), BF) for s in shapes for n in (cut, lanes - cut)] + [
        pltpu.SemaphoreType.DMA((2, 7)),
        pltpu.SemaphoreType.DMA((2, 7)),
    ]


def tail_pieces(b, e, piece):
    j = b
    while j < e:
        p = j // piece
        stop = min(e, (p + 1) * piece)
        yield p, j, stop
        j = stop


def unpack(held, refs, split, piece, wide):
    def band(g, carry):
        for j in range(4):
            src = held.at[g // 4, g % 4, j]
            for ref, (b, e) in zip(refs, split):
                ref[g, SHARD * j : SHARD * j + MAIN, :] = src[:, b:e]
                for p, lo, hi in tail_pieces(b, e, piece):
                    ref[g, SHARD * j + MAIN : SHARD * (j + 1), lo - b : hi - b] = src[
                        4 * p : 4 * p + 4, wide + lo - p * piece : wide + hi - p * piece
                    ]
        return carry

    lax.fori_loop(0, 8, band, 0)


def pack(held, grad, b, e, piece, wide):
    def band(g, carry):
        for j in range(4):
            dst = held.at[g // 4, g % 4, j]
            dst[:, b:e] = grad[g, SHARD * j : SHARD * j + MAIN, : e - b].astype(BF)
            for p, lo, hi in tail_pieces(b, e, piece):
                dst[4 * p : 4 * p + 4, wide + lo - p * piece : wide + hi - p * piece] = grad[
                    g, SHARD * j + MAIN : SHARD * (j + 1), lo - b : hi - b
                ].astype(BF)
        return carry

    lax.fori_loop(0, 8, band, 0)


def pack_own(dst, flat, wide, piece):
    dst[:, 0:wide] = flat[0:MAIN, 0:wide].astype(BF)
    for p in range(wide // piece):
        dst[4 * p : 4 * p + 4, wide : wide + piece] = flat[
            MAIN:SHARD, p * piece : (p + 1) * piece
        ].astype(BF)
    rest = 4 * (wide // piece)
    dst[rest:MAIN, wide : wide + piece] = jnp.zeros((MAIN - rest, piece), BF)


def layer_norm(stream):
    average = jnp.mean(stream, -1, keepdims=True)
    centered = stream - average
    variance = jnp.mean(centered * centered, -1, keepdims=True)
    inverse = lax.rsqrt(variance + EPS)
    return centered * inverse, inverse


def norm_back(upstream, normed, inverse, gain_vec):
    scaled = upstream * gain_vec
    return inverse * (
        scaled
        - jnp.mean(scaled, -1, keepdims=True)
        - normed * jnp.mean(scaled * normed, -1, keepdims=True)
    )


def gelu_parts(pre_act):
    square = pre_act * pre_act
    tangent = jnp.tanh(pre_act * (GELU_C + GELU_C * CUBIC * square))
    share = 0.5 + 0.5 * tangent
    value = pre_act * share
    slope = share + value * (1.0 - tangent) * (GELU_C + 3.0 * GELU_C * CUBIC * square)
    return value, slope


def nn(a, b):
    return lax.dot_general(a, b, (((1,), (0,)), ((), ())), preferred_element_type=F32)


def nt(a, b):
    return lax.dot_general(a, b, (((1,), (1,)), ((), ())), preferred_element_type=F32)


def whole(ref):
    return ref[...].reshape(D, ref.shape[-1])


def vec(ref):
    return ref[...].reshape(1, -1)


def pick(ref, rank, width):
    flat = vec(ref)
    out = flat[:, 0:width]
    for r in range(1, 4):
        out = jnp.where(rank == r, flat[:, r * width : (r + 1) * width], out)
    return out


def layer_kernel(
    stream, valid, pre_gain, pre_shift, wq, bq, wk, wv, bv, wo, out_bias, mid_gain, mid_shift,
    wu, bu, wd, down_bias, cot,
    block_out, input_grad, gq, gk, gv, go, gu, gd, early_out, late_out,
    held1, held2, held3, flat1, flat2, flat3, wqkv, wout, wup, wdown, arows, crows, mrows, grows,
    qkv, mixed, dmix, mask, logsum, hidden, act, grad, flip, part1, dk_acc, dv_acc, qv,
    upsum, bqkv, bhid, early, early_in, late, late_in,
    s1y, s1a, s1b, s2y, s2a, s2b, s3y, s3a, s3b, ra, rc, rm, rg, se, sl,
    f1, f2, f3, fs, h1, h2, h3, hs, *scat,
):
    rank, over, sib, cross = ranks()
    yl, z, x = (lax.axis_index(a) for a in FSDP)
    yh, c = (lax.axis_index(a) for a in TP)
    barrier = greet(ALL_PEERS)
    gat1 = WeightGather(held1, CUT1, (s1y, s1a, s1b))
    gat2 = WeightGather(held2, CUT2, (s2y, s2a, s2b), ring=True)
    gat3 = WeightGather(held3, CUT3, (s3y, s3a, s3b))

    flat1[:, 0:COLS] = wq[...].astype(F32)
    flat1[:, COLS : 2 * COLS] = wk[...].astype(F32)
    flat1[:, 2 * COLS : 3 * COLS] = wv[...].astype(F32)
    flat1[:, 3 * COLS : QKV] = jnp.zeros((SHARD, QKV - 3 * COLS), F32)
    pack_own(held1.at[yl, z, x], flat1, WIDE1, PIECE1)
    rows_a, rows_c = RowGather(arows, ra), RowGather(crows, rc)
    for j in range(CHUNKS):
        at = pl.ds(j * CH, CH)
        normed, _ = layer_norm(stream[at])
        arows[rank, at] = (normed * vec(pre_gain) + vec(pre_shift)).astype(BF)
    pl.semaphore_wait(barrier, len(ALL_PEERS))
    gat1.start()
    for j in range(CHUNKS):
        rows_a.put(j)

    gat1.step1()
    flat3[:, 0:COLS] = wo[...].astype(F32)
    flat3[:, COLS:] = jnp.zeros((SHARD, OUT - COLS), F32)
    pack_own(held3.at[yl, z, x], flat3, WIDE3, PIECE3)
    gat3.start()
    for at in (0, HID):
        flat2[:, at + HID - 128 : at + HID] = jnp.zeros((SHARD, 128), F32)
    flat2[:, 0:TRUE_HID] = wu[...].astype(F32)
    flat2[:, HID : HID + TRUE_HID] = wd[...].astype(F32)
    pack_own(held2.at[yl, z, x], flat2, WIDE2, PIECE2)
    gat2.start()
    gat1.step2()
    gat3.step1()
    for j in range(CHUNKS):
        rows_a.forward(j)
    crows[rank] = cot[...].astype(BF)
    for j in range(CHUNKS):
        rows_c.put(j)
    live = jnp.broadcast_to(valid[...].astype(F32), (128, SEQ)).T
    mask[...] = jnp.where(live > 0, 0.0, -jnp.inf)
    bqkv[...] = jnp.zeros_like(bqkv)
    bqkv[:, 0:COLS] = pick(bq, rank, COLS)
    bqkv[:, 2 * COLS : 3 * COLS] = pick(bv, rank, COLS)
    bhid[...] = jnp.zeros_like(bhid)
    bhid[:, 0:TRUE_HID] = pick(bu, rank, TRUE_HID)
    mixed[...] = jnp.zeros_like(mixed)
    upsum[...] = jnp.zeros_like(upsum)
    qv[...] = jnp.zeros_like(qv)
    dk_acc[...] = jnp.zeros_like(dk_acc)
    dv_acc[...] = jnp.zeros_like(dv_acc)
    rows_a.chip()
    rows_a.rest()
    gat1.finish()
    gat3.step2()
    unpack(held1, (wqkv,), SPLIT1, PIECE1, WIDE1)

    def project(r, carry):
        at = pl.ds(pl.multiple_of(r * ROWS, ROWS), ROWS)
        qkv[at] = (nn(arows[r], whole(wqkv)) + bqkv[...]).astype(BF)
        return carry

    lax.fori_loop(0, 4, project, 0)
    gat2.step1()
    for j in range(CHUNKS):
        rows_c.forward(j)

    def head_slices(h):
        lo = HD * h
        return (
            qkv[:, COLS + lo : COLS + lo + HD],
            qkv[:, 2 * COLS + lo : 2 * COLS + lo + HD],
        )

    def half_rows(chip):
        return pl.ds(pl.multiple_of(chip * QC, QC), QC)

    def scores_of(h, at):
        query = qkv[at, :][:, HD * h : HD * h + HD]
        key = head_slices(h)[0]
        bias = mask[...]
        return nt(key, query) * SCALE + jnp.concatenate([bias] * (QC // 128), 1), query

    def attend(chip):
        at = half_rows(chip)
        for h in range(HEADS):
            scores, _ = scores_of(h, at)
            top = jnp.max(scores, 0, keepdims=True)
            raised = jnp.exp(scores - top)
            total = jnp.sum(raised, 0, keepdims=True)
            logsum[h, chip] = top + jnp.log(total)
            probs = (raised * (1.0 / total)).astype(BF)
            value = head_slices(h)[1]
            o_t = lax.dot_general(
                value, probs, (((0,), (0,)), ((), ())), preferred_element_type=F32
            )
            mixed[at, HD * h : HD * h + HD] = o_t.T.astype(BF)

    def out_block(r):
        at = pl.ds(pl.multiple_of(r * ROWS, ROWS), ROWS)
        part1[r] = nt(mixed[at], whole(wout)).astype(BF)

    sum1 = TpSum(part1, f1, f2, f3, fs)
    gat2.plan2()

    def out_pair(a, b):
        def step(n, carry):
            out_block((1 - n) * a + n * b)
            return carry

        lax.fori_loop(0, 2, step, 0)

    def attend_step(n, carry):
        attend((1 - yh) + n * (2 * yh - 1))

        @pl.when(n == 0)
        def _():
            gat3.finish()
            unpack(held3, (wout,), SPLIT3, PIECE3, WIDE3)
            out_pair(cross, over)
            sum1.start_cross()
            gat2.go2()
            sum1.middle()

        return carry

    lax.fori_loop(0, 2, attend_step, 0)
    out_pair(sib, rank)
    sum1.start_sib()
    gat2.relay()
    rows_c.chip()
    rows_c.rest()
    rows_m = RowGather(mrows, rm)
    for j in range(CHUNKS):
        at = pl.ds(j * CH, CH)
        mid = stream[at] + sum1.total(j) + vec(out_bias)
        block_out[at] = mid
        normed, _ = layer_norm(mid)
        mrows[rank, at] = (normed * vec(mid_gain) + vec(mid_shift)).astype(BF)
        rows_m.put(j)
    sum1.end()
    gat2.finish()
    unpack(held2, (wup, wdown), SPLIT2, PIECE2, WIDE2)

    sum2 = TpSum(part1, f1, f2, f3, fs)

    def mlp_step(n, carry):
        @pl.when(n == 2)
        def _():
            sum2.start_sib()
            for j in range(CHUNKS):
                rows_m.forward(j)
            rows_m.rest()

        far, odd = n // 2, n % 2
        r = 2 * (yh + far * (1 - 2 * yh)) + c + odd * (1 - 2 * c)
        pre_act = nn(mrows[r], whole(wup)) + bhid[...]
        value, slope = gelu_parts(pre_act)
        hidden[r] = value.astype(BF)
        act_grad = nn(crows[r], whole(wdown)) * slope
        act[r] = act_grad.astype(BF)
        upsum[...] += jnp.sum(act_grad, 0, keepdims=True)
        part1[r] = nt(act[r], whole(wup)).astype(BF)
        return carry

    rows_m.chip()
    lax.fori_loop(0, 4, mlp_step, 0)
    sum2.start_cross()
    sum2.middle()

    gat1.end()
    gat2.end()
    gat3.end()
    rows_m.end()
    sc1 = GradScatter(held1, CUT1, scat[:12])
    sc2 = GradScatter(held2, CUT2, scat[12:24])
    sc3 = GradScatter(held3, CUT3, scat[24:])

    def turn_rows(rows):
        for j in range(3):
            blk = rows[:, :, 384 * j : 384 * (j + 1)].reshape(SEQ, 384)
            flip[384 * j : 384 * (j + 1), :] = blk.T

    def product(right, width, held, base, piece, wide):
        for lo in range(0, width, 384):
            hi = min(lo + 384, width)
            grad[:, :, 0 : hi - lo] = nn(flip[...], right(slice(lo, hi))).reshape(8, BAND, hi - lo)
            pack(held, grad, base + lo, base + hi, piece, wide)

    def blank(held, piece, wide):
        used = 4 * (wide // piece)
        held[:, :, :, used:MAIN, wide : wide + piece] = jnp.zeros((2, 4, 4, MAIN - used, piece), BF)

    turn_rows(mrows)
    product(lambda at: act[:, :, at].reshape(SEQ, 384), HID, held2, 0, PIECE2, WIDE2)
    turn_rows(crows)
    product(lambda at: hidden[:, :, at].reshape(SEQ, 384), HID, held2, HID, PIECE2, WIDE2)
    blank(held2, PIECE2, WIDE2)
    sc2.step1()

    rows_g = RowGather(grows, rg)
    sums = [jnp.zeros((1, D), F32)] * 4
    for j in range(CHUNKS):
        at = pl.ds(j * CH, CH)
        normed, inverse = layer_norm(block_out[at])
        g = sum2.total(j)
        back = cot[at] + norm_back(g, normed, inverse, vec(mid_gain))
        input_grad[at] = back
        grows[rank, at] = back.astype(BF)
        rows_g.put(j)
        for k, v in enumerate((back, g * normed, g, cot[at])):
            sums[k] = sums[k] + jnp.sum(v, 0, keepdims=True)
    early[0] = jnp.zeros((8, D), F32)
    for k in range(4):
        early[0, k : k + 1, :] = sums[k]
    early[0, pl.ds(4 + rank, 1), :] = upsum[...]
    ec = [send(early.at[0], early_in.at[0], se, 0, "c")]
    sum2.end()

    def down_block(r, carry):
        mrows[r] = nt(hidden[r], whole(wdown)).astype(BF)
        return carry

    lax.fori_loop(0, 4, down_block, 0)
    sum3 = TpSum(mrows, h1, h2, h3, hs)
    sum3.start_cross()
    sum3.start_sib()
    ec[0].wait_recv()
    early[1] = early[0] + early_in[0]
    ec.append(send(early.at[1], early_in.at[1], se, 1, "yh"))

    def mix_back(a, b):
        def step(n, carry):
            r = (1 - n) * a + n * b
            at = pl.ds(pl.multiple_of(r * ROWS, ROWS), ROWS)
            dmix[at] = nn(grows[r], whole(wout)).astype(BF)
            return carry

        lax.fori_loop(0, 2, step, 0)

    def attend_back(chip, between):
        at = half_rows(chip)
        for h in range(HEADS):
            lo = HD * h
            if h == 3:
                between()
            scores, query = scores_of(h, at)
            probs = jnp.exp(scores - logsum[h, chip])
            key, value = head_slices(h)
            dout = dmix[at, :][:, lo : lo + HD]
            dv_acc[h] += nn(probs.astype(BF), dout)
            prob_grad = nt(value, dout)
            delta = jnp.sum(probs * prob_grad, 0, keepdims=True)
            ds = (probs * (prob_grad - delta) * SCALE).astype(BF)
            dk_acc[h] += nn(ds, query)
            dq = lax.dot_general(
                key, ds, (((0,), (0,)), ((), ())), preferred_element_type=F32
            ).T
            qv[0:1, lo : lo + HD] += jnp.sum(dq, 0, keepdims=True)
            qkv[at, lo : lo + HD] = dq.astype(BF)

    rows_g.chip()
    mix_back(rank, sib)
    sum3.middle()
    sc3.plan1()

    def back_step(n, carry):
        def between():
            @pl.when(n == 0)
            def _():
                for j in range(CHUNKS):
                    rows_g.forward(j)

        attend_back(yh + n * (1 - 2 * yh), between)

        @pl.when(n == 0)
        def _():
            rows_g.rest()
            mix_back(over, cross)
            turn_rows(grows)
            product(lambda at: mixed[:, at], OUT, held3, 0, PIECE3, WIDE3)
            blank(held3, PIECE3, WIDE3)
            sc3.go1()

        return carry

    lax.fori_loop(0, 2, back_step, 0)
    ec[1].wait_recv()
    early[2] = early[1] + early_in[1]
    ec.append(send(early.at[2], early_in.at[2], se, 2, "yl"))
    for h in range(HEADS):
        lo = HD * h
        qv[0:1, COLS + lo : COLS + lo + HD] = jnp.sum(dv_acc[h], 0, keepdims=True)
        qkv[:, COLS + lo : COLS + lo + HD] = dk_acc[h].astype(BF)
        qkv[:, 2 * COLS + lo : 2 * COLS + lo + HD] = dv_acc[h].astype(BF)
    qkv[:, 3 * COLS : QKV] = jnp.zeros((SEQ, QKV - 3 * COLS), BF)

    def attn_block(r):
        at = pl.ds(pl.multiple_of(r * ROWS, ROWS), ROWS)
        part1[r] = nt(qkv[at], whole(wqkv)).astype(BF)

    sum4 = TpSum(part1, f1, f2, f3, fs)
    attn_block(cross)
    sum4.start_cross()
    attn_block(over)
    sum4.middle()
    sc2.step2()
    attn_block(sib)
    sum4.start_sib()
    attn_block(rank)
    turn_rows(arows)
    product(lambda at: qkv[:, at], QKV, held1, 0, PIECE1, WIDE1)
    blank(held1, PIECE1, WIDE1)
    sc3.step2()
    sc1.step1()
    ec[2].wait_recv()
    early[3] = early[2] + early_in[2]
    for k, step in enumerate(NEAR):
        ec.append(send(early.at[3], early_in.at[3 + x], se, 3 + k, "x", step))
    early_in[3 + x] = early[3]

    sums = [jnp.zeros((1, D), F32)] * 2
    for j in range(CHUNKS):
        at = pl.ds(j * CH, CH)
        normed, inverse = layer_norm(stream[at])
        g = sum4.total(j)
        input_grad[at] = input_grad[at] + norm_back(g, normed, inverse, vec(pre_gain))
        for k, v in enumerate((g * normed, g)):
            sums[k] = sums[k] + jnp.sum(v, 0, keepdims=True)
    late[0] = jnp.zeros((8, D), F32)
    late[0, 0:1, :] = sums[0]
    late[0, 1:2, :] = sums[1]
    late[0, pl.ds(4 + rank, 1), :] = qv[...]
    here = yl * 4 + yh * 2 + c
    lc = [
        send_to(late.at[0], late_in.at[here], sl, k, moves) for k, moves in enumerate(LINE)
    ]
    late_in[here] = late[0]
    for j in range(CHUNKS):
        at = pl.ds(j * CH, CH)
        block_out[at] = block_out[at] + sum3.total(j) + vec(down_bias)
    for copy in ec[3:6]:
        copy.wait_recv()
    early[4] = early_in[3] + early_in[4] + early_in[5] + early_in[6]
    for k, step in enumerate(NEAR):
        ec.append(send(early.at[4], early_in.at[7 + z], se, 6 + k, "z", step))
    early_in[7 + z] = early[4]
    for copy in lc:
        copy.wait_recv()
    late[1] = sum((late_in[k] for k in range(1, 8)), late_in[0])
    for k, step in enumerate(NEAR):
        lc.append(send(late.at[1], late_in.at[8 + x], sl, 7 + k, "x", step))
    late_in[8 + x] = late[1]
    sc2.step3()
    sc1.step2()
    for copy in lc[7:10]:
        copy.wait_recv()
    late[2] = late_in[8] + late_in[9] + late_in[10] + late_in[11]
    for k, step in enumerate(NEAR):
        lc.append(send(late.at[2], late_in.at[12 + z], sl, 10 + k, "z", step))
    late_in[12 + z] = late[2]
    sc3.step3()
    sc1.step3()
    sc2.finish(flat2, WIDE2, PIECE2)
    gu[...] = flat2[:, 0:TRUE_HID]
    gd[...] = flat2[:, HID : HID + TRUE_HID]
    sc3.finish(flat3, WIDE3, PIECE3)
    go[...] = flat3[:, 0:COLS]
    for copy in ec[6:9]:
        copy.wait_recv()
    early_out[...] = early_in[7] + early_in[8] + early_in[9] + early_in[10]
    for copy in lc[10:13]:
        copy.wait_recv()
    late_out[...] = late_in[12] + late_in[13] + late_in[14] + late_in[15]
    sc1.finish(flat1, WIDE1, PIECE1)
    gq[...] = flat1[:, 0:COLS]
    gk[...] = flat1[:, COLS : 2 * COLS]
    gv[...] = flat1[:, 2 * COLS : 3 * COLS]
    for copy in ec + lc:
        copy.wait_send()
    for item in (rows_a, rows_c, rows_g, sum3, sum4, sc1, sc2, sc3):
        item.end()


def split_kernel(*refs):
    early, late = refs[8:10]
    outs = refs[10:]
    for k in range(8):
        outs[k][...] = refs[k][...]

    def joined(ref, lo, width):
        rows = [ref[4 + r : 5 + r, lo : lo + width] for r in range(4)]
        return jnp.concatenate(rows, 1).reshape(4 * width)

    pregain, preshift, query, value, outbias, midgain, midshift, up, downbias = outs[8:]
    pregain[...] = late[0]
    preshift[...] = late[1]
    query[...] = joined(late, 0, COLS)
    value[...] = joined(late, COLS, COLS)
    outbias[...] = early[0]
    midgain[...] = early[1]
    midshift[...] = early[2]
    downbias[...] = early[3]
    up[...] = joined(early, 0, TRUE_HID)


def per_device(*args):
    (
        residual, valid_keys, pre_gain, pre_shift, wq, bq, wk, wv, bv, wo, out_bias, mid_gain,
        mid_shift, wu, bu, wd, down_bias, cotangent,
    ) = args
    vm = pl.BlockSpec(memory_space=pltpu.VMEM)
    ins = (
        residual[0], valid_keys, pre_gain, pre_shift, wq, bq, wk, wv, bv, wo.T, out_bias,
        mid_gain, mid_shift, wu, bu, wd.T, down_bias, cotangent[0],
    )
    arrays = [
        (ROWS, D), (ROWS, D), (SHARD, COLS), (SHARD, COLS), (SHARD, COLS), (SHARD, COLS),
        (SHARD, TRUE_HID), (SHARD, TRUE_HID),
    ]
    outs = arrays + [(8, D), (8, D)]
    rows = (4, ROWS, D)
    dma = lambda *n: pltpu.SemaphoreType.DMA(n)
    tp_sum = [
        pltpu.VMEM((2, ROWS, D), BF),
        pltpu.VMEM((ROWS, D), BF),
        pltpu.VMEM((ROWS, D), BF),
        dma(2, 2 + CHUNKS),
    ]
    scratch = [
        pltpu.VMEM((2, 4, 4, MAIN, PACK1), BF),
        pltpu.VMEM((2, 4, 4, MAIN, PACK2), BF),
        pltpu.VMEM((2, 4, 4, MAIN, PACK3), BF),
        pltpu.VMEM((SHARD, WIDE1), F32),
        pltpu.VMEM((SHARD, WIDE2), F32),
        pltpu.VMEM((SHARD, WIDE3), F32),
        pltpu.VMEM((8, BAND, QKV), BF),
        pltpu.VMEM((8, BAND, OUT), BF),
        pltpu.VMEM((8, BAND, HID), BF),
        pltpu.VMEM((8, BAND, HID), BF),
        pltpu.VMEM(rows, BF),
        pltpu.VMEM(rows, BF),
        pltpu.VMEM(rows, BF),
        pltpu.VMEM(rows, BF),
        pltpu.VMEM((SEQ, QKV), BF),
        pltpu.VMEM((SEQ, OUT), BF),
        pltpu.VMEM((SEQ, OUT), BF),
        pltpu.VMEM((SEQ, 128), F32),
        pltpu.VMEM((HEADS, SEQ // QC, 1, QC), F32),
        pltpu.VMEM(rows, BF),
        pltpu.VMEM(rows, BF),
        pltpu.VMEM((8, BAND, 384), F32),
        pltpu.VMEM((D, SEQ), BF),
        pltpu.VMEM(rows, BF),
        pltpu.VMEM((HEADS, SEQ, HD), F32),
        pltpu.VMEM((HEADS, SEQ, HD), F32),
        pltpu.VMEM((1, D), F32),
        pltpu.VMEM((1, HID), F32),
        pltpu.VMEM((1, QKV), F32),
        pltpu.VMEM((1, HID), F32),
        pltpu.VMEM((5, 8, D), F32),
        pltpu.VMEM((11, 8, D), F32),
        pltpu.VMEM((3, 8, D), F32),
        pltpu.VMEM((16, 8, D), F32),
        *([dma(2, 1), dma(2, 7), dma(2, 7)] * 3),
        *([dma(2, 3 * CHUNKS)] * 4),
        dma(2, 9),
        dma(2, 13),
        *tp_sum,
        *tp_sum,
        *scatter_scratch(CUT1, PACK1),
        *scatter_scratch(CUT2, PACK2),
        *scatter_scratch(CUT3, PACK3),
    ]
    out = pl.pallas_call(
        layer_kernel,
        name="layer",
        out_shape=[jax.ShapeDtypeStruct(s, F32) for s in outs],
        in_specs=[vm] * len(ins),
        out_specs=[vm] * len(outs),
        scratch_shapes=scratch,
        compiler_params=pltpu.CompilerParams(
            collective_id=0, has_side_effects=True, vmem_limit_bytes=63 * 2**20
        ),
    )(*ins)
    ends = arrays + [(D,)] * 7 + [(4 * TRUE_HID,), (D,)]
    done = pl.pallas_call(
        split_kernel,
        name="split",
        out_shape=[jax.ShapeDtypeStruct(s, F32) for s in ends],
        in_specs=[vm] * len(out),
        out_specs=[vm] * len(ends),
    )(*out)
    return (
        done[0][None], done[1][None], done[2], done[3], done[4], done[5].T, done[6], done[7].T,
        *done[8:],
    )


def solution(mesh):
    split = Mesh(mesh.devices.reshape(2, 4, 4, 2, 2), ("yl", "z", "x", "yh", "c"))
    rows3 = P(FSDP, TP, None)
    down_cols = P(FSDP, TP)
    across = P(TP, FSDP)
    return jax.shard_map(
        per_device,
        mesh=split,
        in_specs=(
            rows3, P(FSDP, None), P(), P(), down_cols, P(), down_cols, down_cols, P(), across,
            P(), P(), P(), down_cols, P(), across, P(), rows3,
        ),
        out_specs=(
            rows3, rows3, down_cols, down_cols, down_cols, across, down_cols, across,
            P(), P(), P(), P(), P(), P(), P(), P(), P(),
        ),
        check_vma=False,
    )
```

```python
import math

import jax
import jax.numpy as jnp
from jax import lax
from jax.experimental import pallas as pl
from jax.experimental.pallas import tpu as pltpu
from jax.sharding import Mesh
from jax.sharding import PartitionSpec as P

HD = 72
HEADS = 4
COLS = HEADS * HD
D = 1152
SEQ = 768
ROWS = 192
CHUNKS = 2
CH = ROWS // CHUNKS
SHARD = 36
MAIN = 32
BAND = 4 * SHARD
QKV = 896
OUT = 384
HID = 1152
TRUE_HID = 1076
QC = 384
EPS = 1e-06
GELU_C = math.sqrt(2.0 / math.pi)
CUBIC = 0.044715
SCALE = 1.0 / math.sqrt(HD)
SIZE = {"yl": 2, "z": 4, "x": 4, "yh": 2, "c": 2}
FSDP = ("yl", "z", "x")
TP = ("yh", "c")
MESH = pl.DeviceIdType.MESH
BF = jnp.bfloat16
F32 = jnp.float32
NEAR = (1, 3, 2)
SPLIT1, PIECE1, WIDE1, PACK1 = ((0, QKV),), 128, QKV, QKV + 128
SPLIT3, PIECE3, WIDE3, PACK3 = ((0, OUT),), 128, OUT, OUT + 128
SPLIT2, PIECE2, WIDE2, PACK2 = ((0, HID), (HID, 2 * HID)), 384, 2 * HID, 2 * HID + 384
CUT1, CUT2, CUT3 = 512, 1408, 256
LINE = tuple(
    tuple((a, 1) for a, on in (("yl", i & 4), ("yh", i & 2), ("c", i & 1)) if on)
    for i in range(1, 8)
)
ALL_PEERS = LINE + tuple(((a, s),) for a in ("x", "z") for s in NEAR)


def ahead(axis, step):
    return lax.rem(lax.axis_index(axis) + step, SIZE[axis])


def peer(moves):
    return {axis: ahead(axis, step) for axis, step in moves}


def greet(peers):
    barrier = pltpu.get_barrier_semaphore()
    for moves in peers:
        pl.semaphore_signal(barrier, inc=1, device_id=peer(moves), device_id_type=MESH)
    return barrier


def send(src, dst, sems, k, axis, step=1):
    return send_to(src, dst, sems, k, ((axis, step),))


def link_to(src, dst, sems, k, moves):
    return pltpu.make_async_remote_copy(
        src_ref=src,
        dst_ref=dst,
        send_sem=sems.at[0, k],
        recv_sem=sems.at[1, k],
        device_id=peer(moves),
        device_id_type=MESH,
    )


def link(src, dst, sems, k, axis, step=1):
    return link_to(src, dst, sems, k, ((axis, step),))


def send_to(src, dst, sems, k, moves):
    copy = link_to(src, dst, sems, k, moves)
    copy.start()
    return copy


def ranks():
    yh, c = lax.axis_index("yh"), lax.axis_index("c")
    return yh * 2 + c, (1 - yh) * 2 + c, yh * 2 + 1 - c, (1 - yh) * 2 + 1 - c


class RowGather:
    def __init__(self, rows, sems):
        self.over, self.sib, self.fwd = [], [], []
        mine, far = ranks()[:2]
        for j in range(CHUNKS):
            blk = rows.at[mine, pl.ds(j * CH, CH)]
            self.over.append(link(blk, blk, sems, 3 * j, "yh"))
            self.sib.append(link(blk, blk, sems, 3 * j + 1, "c"))
            blk = rows.at[far, pl.ds(j * CH, CH)]
            self.fwd.append(link(blk, blk, sems, 3 * j + 2, "c"))

    def put(self, j):
        self.over[j].start()
        self.sib[j].start()

    def forward(self, j):
        self.over[j].wait_recv()
        self.fwd[j].start()

    def chip(self):
        for j in range(CHUNKS):
            self.sib[j].wait_recv()

    def rest(self):
        for j in range(CHUNKS):
            self.fwd[j].wait_recv()

    def end(self):
        for j in range(CHUNKS):
            self.over[j].wait_send()
            self.sib[j].wait_send()
            self.fwd[j].wait_send()


class TpSum:
    def __init__(self, part, first, second, out, sems):
        self.part, self.first, self.second, self.out = part, first, second, out
        self.cross = link(part.at[ranks()[3]], first.at[0], sems, 0, "c")
        self.sib = link(part.at[ranks()[2]], first.at[1], sems, 1, "c")
        self.over = []
        for j in range(CHUNKS):
            rows = pl.ds(j * CH, CH)
            self.over.append(link(out.at[rows], second.at[rows], sems, 2 + j, "yh"))

    def start_cross(self):
        self.cross.start()

    def start_sib(self):
        self.sib.start()

    def middle(self):
        over = ranks()[1]
        self.cross.wait_recv()
        for j in range(CHUNKS):
            rows = pl.ds(j * CH, CH)
            self.out[rows] = (
                self.part[over, rows].astype(F32) + self.first[0, rows].astype(F32)
            ).astype(BF)
            self.over[j].start()

    def total(self, j):
        mine = ranks()[0]
        rows = pl.ds(j * CH, CH)
        if j == 0:
            self.sib.wait_recv()
        self.over[j].wait_recv()
        return (
            self.part[mine, rows].astype(F32)
            + self.first[1, rows].astype(F32)
            + self.second[rows].astype(F32)
        )

    def end(self):
        self.cross.wait_send()
        self.sib.wait_send()
        for copy in self.over:
            copy.wait_send()


class WeightGather:
    def __init__(self, held, cut, sems, ring=False):
        self.held, self.cut, self.ring, self.done = held, cut, ring, []
        self.s0, self.sa, self.sb = sems
        self.yl, self.z, self.x = (lax.axis_index(a) for a in FSDP)
        self.lo, self.hi = pl.ds(0, cut), pl.ds(cut, held.shape[-1] - cut)

    def start(self):
        blk = self.held.at[self.yl, self.z, self.x]
        self.zero = send(blk, blk, self.s0, 0, "yl")

    def step1(self):
        self.zero.wait_recv()
        self.one = []
        for k, step in enumerate(NEAR):
            blk = self.held.at[:, self.z, self.x, :, self.lo]
            self.one.append(send(blk, blk, self.sa, k, "x", step))
            blk = self.held.at[:, self.z, self.x, :, self.hi]
            self.one.append(send(blk, blk, self.sb, k, "z", step))

    def plan2(self):
        self.two = []
        for k, step in enumerate(NEAR[:2] if self.ring else NEAR):
            blk = self.held.at[:, self.z, :, :, self.lo]
            self.two.append(link(blk, blk, self.sa, 3 + k, "z", step))
            blk = self.held.at[:, :, self.x, :, self.hi]
            self.two.append(link(blk, blk, self.sb, 3 + k, "x", step))

    def go2(self):
        for copy in self.one:
            copy.wait_recv()
        for copy in self.two:
            copy.start()

    def step2(self):
        self.plan2()
        self.go2()

    def relay(self):
        for copy in self.two:
            copy.wait_recv()
        wide = self.held.shape[-1]
        more = []
        for k, (step, back) in enumerate(((1, 3), (3, 1))):
            mid = self.cut // 256 * 128
            at = pl.ds(0, mid) if k == 0 else pl.ds(mid, self.cut - mid)
            blk = self.held.at[:, ahead("z", back), :, :, at]
            more.append(send(blk, blk, self.sa, 5 + k, "z", step))
            mid = (wide - self.cut) // 256 * 128
            at = pl.ds(self.cut, mid) if k == 0 else pl.ds(self.cut + mid, wide - self.cut - mid)
            blk = self.held.at[:, :, ahead("x", back), :, at]
            more.append(send(blk, blk, self.sb, 5 + k, "x", step))
        self.done, self.two = self.two, more

    def finish(self):
        for copy in self.two:
            copy.wait_recv()

    def end(self):
        self.zero.wait_send()
        for copy in self.one + self.two + self.done:
            copy.wait_send()


class GradScatter:
    def __init__(self, held, cut, bufs):
        self.held, self.cut = held, cut
        (
            self.ra1, self.rb1, self.qa, self.qb, self.ra2, self.rb2, self.ta, self.tb,
            self.ra3, self.rb3, self.sa, self.sb,
        ) = bufs
        self.yl, self.z, self.x = (lax.axis_index(a) for a in FSDP)
        self.lo, self.hi = pl.ds(0, cut), pl.ds(cut, held.shape[-1] - cut)

    def plan1(self):
        self.one = []
        for k, step in enumerate(NEAR):
            src = self.held.at[:, ahead("z", step), :, :, self.lo]
            self.one.append(link(src, self.ra1.at[k], self.sa, k, "z", step))
            src = self.held.at[:, :, ahead("x", step), :, self.hi]
            self.one.append(link(src, self.rb1.at[k], self.sb, k, "x", step))

    def go1(self):
        for copy in self.one:
            copy.start()

    def step1(self):
        self.plan1()
        self.go1()

    def step2(self):
        for copy in self.one:
            copy.wait_recv()

        def add(n, carry):
            a, b = n // 4, n % 4
            at_a = self.held[a, self.z, b, :, self.lo].astype(F32)
            at_b = self.held[a, b, self.x, :, self.hi].astype(F32)
            for k in range(3):
                at_a = at_a + self.ra1[k, a, b].astype(F32)
                at_b = at_b + self.rb1[k, a, b].astype(F32)
            self.qa[a, b] = at_a.astype(BF)
            self.qb[a, b] = at_b.astype(BF)
            return carry

        lax.fori_loop(0, 8, add, 0)
        self.two = []
        for k, step in enumerate(NEAR):
            src = self.qa.at[:, ahead("x", step)]
            self.two.append(send(src, self.ra2.at[k], self.sa, 3 + k, "x", step))
            src = self.qb.at[:, ahead("z", step)]
            self.two.append(send(src, self.rb2.at[k], self.sb, 3 + k, "z", step))

    def step3(self):
        for copy in self.two:
            copy.wait_recv()
        for a in range(2):
            at_a = self.qa[a, self.x].astype(F32)
            at_b = self.qb[a, self.z].astype(F32)
            for k in range(3):
                at_a = at_a + self.ra2[k, a].astype(F32)
                at_b = at_b + self.rb2[k, a].astype(F32)
            self.ta[a] = at_a.astype(BF)
            self.tb[a] = at_b.astype(BF)
        self.three = [
            send(self.ta.at[1 - self.yl], self.ra3, self.sa, 6, "yl"),
            send(self.tb.at[1 - self.yl], self.rb3, self.sb, 6, "yl"),
        ]

    def finish(self, flat, wide, piece):
        for copy in self.three:
            copy.wait_recv()
        half = self.cut
        fa = self.ta[self.yl].astype(F32) + self.ra3[...].astype(F32)
        fb = self.tb[self.yl].astype(F32) + self.rb3[...].astype(F32)
        flat[0:MAIN, 0:half] = fa
        flat[0:MAIN, half:wide] = fb[:, : wide - half]
        for j in range(wide // piece):
            flat[MAIN:SHARD, j * piece : (j + 1) * piece] = fb[4 * j : 4 * j + 4, wide - half :]

    def end(self):
        for copy in self.one + self.two + self.three:
            copy.wait_send()


def scatter_scratch(cut, lanes):
    shapes = ((3, 2, 4, MAIN), (2, 4, MAIN), (3, 2, MAIN), (2, MAIN), (MAIN,))
    return [pltpu.VMEM((*s, n), BF) for s in shapes for n in (cut, lanes - cut)] + [
        pltpu.SemaphoreType.DMA((2, 7)),
        pltpu.SemaphoreType.DMA((2, 7)),
    ]


def tail_pieces(b, e, piece):
    j = b
    while j < e:
        p = j // piece
        stop = min(e, (p + 1) * piece)
        yield p, j, stop
        j = stop


def unpack(held, refs, split, piece, wide):
    def band(g, carry):
        for j in range(4):
            src = held.at[g // 4, g % 4, j]
            for ref, (b, e) in zip(refs, split):
                ref[g, SHARD * j : SHARD * j + MAIN, :] = src[:, b:e]
                for p, lo, hi in tail_pieces(b, e, piece):
                    ref[g, SHARD * j + MAIN : SHARD * (j + 1), lo - b : hi - b] = src[
                        4 * p : 4 * p + 4, wide + lo - p * piece : wide + hi - p * piece
                    ]
        return carry

    lax.fori_loop(0, 8, band, 0)


def pack(held, grad, b, e, piece, wide):
    def band(g, carry):
        for j in range(4):
            dst = held.at[g // 4, g % 4, j]
            dst[:, b:e] = grad[g, SHARD * j : SHARD * j + MAIN, : e - b].astype(BF)
            for p, lo, hi in tail_pieces(b, e, piece):
                dst[4 * p : 4 * p + 4, wide + lo - p * piece : wide + hi - p * piece] = grad[
                    g, SHARD * j + MAIN : SHARD * (j + 1), lo - b : hi - b
                ].astype(BF)
        return carry

    lax.fori_loop(0, 8, band, 0)


def pack_own(dst, flat, wide, piece):
    dst[:, 0:wide] = flat[0:MAIN, 0:wide].astype(BF)
    for p in range(wide // piece):
        dst[4 * p : 4 * p + 4, wide : wide + piece] = flat[
            MAIN:SHARD, p * piece : (p + 1) * piece
        ].astype(BF)
    rest = 4 * (wide // piece)
    dst[rest:MAIN, wide : wide + piece] = jnp.zeros((MAIN - rest, piece), BF)


def layer_norm(stream):
    average = jnp.mean(stream, -1, keepdims=True)
    centered = stream - average
    variance = jnp.mean(centered * centered, -1, keepdims=True)
    inverse = lax.rsqrt(variance + EPS)
    return centered * inverse, inverse


def norm_back(upstream, normed, inverse, gain_vec):
    scaled = upstream * gain_vec
    return inverse * (
        scaled
        - jnp.mean(scaled, -1, keepdims=True)
        - normed * jnp.mean(scaled * normed, -1, keepdims=True)
    )


def gelu_parts(pre_act):
    square = pre_act * pre_act
    tangent = jnp.tanh(pre_act * (GELU_C + GELU_C * CUBIC * square))
    share = 0.5 + 0.5 * tangent
    value = pre_act * share
    slope = share + value * (1.0 - tangent) * (GELU_C + 3.0 * GELU_C * CUBIC * square)
    return value, slope


def nn(a, b):
    return lax.dot_general(a, b, (((1,), (0,)), ((), ())), preferred_element_type=F32)


def nt(a, b):
    return lax.dot_general(a, b, (((1,), (1,)), ((), ())), preferred_element_type=F32)


def whole(ref):
    return ref[...].reshape(D, ref.shape[-1])


def vec(ref):
    return ref[...].reshape(1, -1)


def pick(ref, rank, width):
    flat = vec(ref)
    out = flat[:, 0:width]
    for r in range(1, 4):
        out = jnp.where(rank == r, flat[:, r * width : (r + 1) * width], out)
    return out


def layer_kernel(
    stream, valid, pre_gain, pre_shift, wq, bq, wk, wv, bv, wo, out_bias, mid_gain, mid_shift,
    wu, bu, wd, down_bias, cot,
    block_out, input_grad, gq, gk, gv, go, gu, gd, early_out, late_out,
    held1, held2, held3, flat1, flat2, flat3, wqkv, wout, wup, wdown, arows, crows, mrows, grows,
    qkv, mixed, dmix, mask, logsum, hidden, act, grad, flip, part1, dk_acc, dv_acc, qv,
    upsum, bqkv, bhid, early, early_in, late, late_in,
    s1y, s1a, s1b, s2y, s2a, s2b, s3y, s3a, s3b, ra, rc, rm, rg, se, sl,
    f1, f2, f3, fs, h1, h2, h3, hs, *scat,
):
    rank, over, sib, cross = ranks()
    yl, z, x = (lax.axis_index(a) for a in FSDP)
    yh, c = (lax.axis_index(a) for a in TP)
    barrier = greet(ALL_PEERS)
    gat1 = WeightGather(held1, CUT1, (s1y, s1a, s1b))
    gat2 = WeightGather(held2, CUT2, (s2y, s2a, s2b), ring=True)
    gat3 = WeightGather(held3, CUT3, (s3y, s3a, s3b))

    flat1[:, 0:COLS] = wq[...].astype(F32)
    flat1[:, COLS : 2 * COLS] = wk[...].astype(F32)
    flat1[:, 2 * COLS : 3 * COLS] = wv[...].astype(F32)
    flat1[:, 3 * COLS : QKV] = jnp.zeros((SHARD, QKV - 3 * COLS), F32)
    pack_own(held1.at[yl, z, x], flat1, WIDE1, PIECE1)
    rows_a, rows_c = RowGather(arows, ra), RowGather(crows, rc)
    for j in range(CHUNKS):
        at = pl.ds(j * CH, CH)
        normed, _ = layer_norm(stream[at])
        arows[rank, at] = (normed * vec(pre_gain) + vec(pre_shift)).astype(BF)
    pl.semaphore_wait(barrier, len(ALL_PEERS))
    gat1.start()
    for j in range(CHUNKS):
        rows_a.put(j)

    gat1.step1()
    flat3[:, 0:COLS] = wo[...].astype(F32)
    flat3[:, COLS:] = jnp.zeros((SHARD, OUT - COLS), F32)
    pack_own(held3.at[yl, z, x], flat3, WIDE3, PIECE3)
    gat3.start()
    for at in (0, HID):
        flat2[:, at + HID - 128 : at + HID] = jnp.zeros((SHARD, 128), F32)
    flat2[:, 0:TRUE_HID] = wu[...].astype(F32)
    flat2[:, HID : HID + TRUE_HID] = wd[...].astype(F32)
    pack_own(held2.at[yl, z, x], flat2, WIDE2, PIECE2)
    gat2.start()
    gat1.step2()
    gat3.step1()
    for j in range(CHUNKS):
        rows_a.forward(j)
    crows[rank] = cot[...].astype(BF)
    for j in range(CHUNKS):
        rows_c.put(j)
    live = jnp.broadcast_to(valid[...].astype(F32), (128, SEQ)).T
    mask[...] = jnp.where(live > 0, 0.0, -jnp.inf)
    bqkv[...] = jnp.zeros_like(bqkv)
    bqkv[:, 0:COLS] = pick(bq, rank, COLS)
    bqkv[:, 2 * COLS : 3 * COLS] = pick(bv, rank, COLS)
    bhid[...] = jnp.zeros_like(bhid)
    bhid[:, 0:TRUE_HID] = pick(bu, rank, TRUE_HID)
    mixed[...] = jnp.zeros_like(mixed)
    upsum[...] = jnp.zeros_like(upsum)
    qv[...] = jnp.zeros_like(qv)
    dk_acc[...] = jnp.zeros_like(dk_acc)
    dv_acc[...] = jnp.zeros_like(dv_acc)
    rows_a.chip()
    rows_a.rest()
    gat1.finish()
    gat3.step2()
    gat2.step1()
    unpack(held1, (wqkv,), SPLIT1, PIECE1, WIDE1)

    def project(r, carry):
        at = pl.ds(pl.multiple_of(r * ROWS, ROWS), ROWS)
        qkv[at] = (nn(arows[r], whole(wqkv)) + bqkv[...]).astype(BF)
        return carry

    lax.fori_loop(0, 4, project, 0)
    for j in range(CHUNKS):
        rows_c.forward(j)

    def head_slices(h):
        lo = HD * h
        return (
            qkv[:, COLS + lo : COLS + lo + HD],
            qkv[:, 2 * COLS + lo : 2 * COLS + lo + HD],
        )

    def half_rows(chip):
        return pl.ds(pl.multiple_of(chip * QC, QC), QC)

    def scores_of(h, at):
        query = qkv[at, :][:, HD * h : HD * h + HD]
        key = head_slices(h)[0]
        bias = mask[...]
        return nt(key, query) * SCALE + jnp.concatenate([bias] * (QC // 128), 1), query

    def attend(chip):
        at = half_rows(chip)
        for h in range(HEADS):
            scores, _ = scores_of(h, at)
            top = jnp.max(scores, 0, keepdims=True)
            raised = jnp.exp(scores - top)
            total = jnp.sum(raised, 0, keepdims=True)
            logsum[h, chip] = top + jnp.log(total)
            probs = (raised * (1.0 / total)).astype(BF)
            value = head_slices(h)[1]
            o_t = lax.dot_general(
                value, probs, (((0,), (0,)), ((), ())), preferred_element_type=F32
            )
            mixed[at, HD * h : HD * h + HD] = o_t.T.astype(BF)

    def out_block(r):
        at = pl.ds(pl.multiple_of(r * ROWS, ROWS), ROWS)
        part1[r] = nt(mixed[at], whole(wout)).astype(BF)

    sum1 = TpSum(part1, f1, f2, f3, fs)
    gat2.plan2()

    def out_pair(a, b):
        def step(n, carry):
            out_block((1 - n) * a + n * b)
            return carry

        lax.fori_loop(0, 2, step, 0)

    def attend_step(n, carry):
        attend((1 - yh) + n * (2 * yh - 1))

        @pl.when(n == 0)
        def _():
            gat3.finish()
            unpack(held3, (wout,), SPLIT3, PIECE3, WIDE3)
            out_pair(cross, over)
            sum1.start_cross()
            gat2.go2()
            sum1.middle()

        return carry

    lax.fori_loop(0, 2, attend_step, 0)
    out_pair(sib, rank)
    sum1.start_sib()
    gat2.relay()
    rows_c.chip()
    rows_c.rest()
    rows_m = RowGather(mrows, rm)
    for j in range(CHUNKS):
        at = pl.ds(j * CH, CH)
        mid = stream[at] + sum1.total(j) + vec(out_bias)
        block_out[at] = mid
        normed, _ = layer_norm(mid)
        mrows[rank, at] = (normed * vec(mid_gain) + vec(mid_shift)).astype(BF)
        rows_m.put(j)
    sum1.end()
    gat2.finish()
    unpack(held2, (wup, wdown), SPLIT2, PIECE2, WIDE2)

    sum2 = TpSum(part1, f1, f2, f3, fs)

    def mlp_step(n, carry):
        @pl.when(n == 2)
        def _():
            sum2.start_sib()
            for j in range(CHUNKS):
                rows_m.forward(j)
            rows_m.rest()

        far, odd = n // 2, n % 2
        r = 2 * (yh + far * (1 - 2 * yh)) + c + odd * (1 - 2 * c)
        pre_act = nn(mrows[r], whole(wup)) + bhid[...]
        value, slope = gelu_parts(pre_act)
        hidden[r] = value.astype(BF)
        act_grad = nn(crows[r], whole(wdown)) * slope
        act[r] = act_grad.astype(BF)
        upsum[...] += jnp.sum(act_grad, 0, keepdims=True)
        part1[r] = nt(act[r], whole(wup)).astype(BF)
        return carry

    rows_m.chip()
    lax.fori_loop(0, 4, mlp_step, 0)
    sum2.start_cross()
    sum2.middle()

    gat1.end()
    gat2.end()
    gat3.end()
    rows_m.end()
    sc1 = GradScatter(held1, CUT1, scat[:12])
    sc2 = GradScatter(held2, CUT2, scat[12:24])
    sc3 = GradScatter(held3, CUT3, scat[24:])

    def turn_rows(rows):
        for j in range(3):
            blk = rows[:, :, 384 * j : 384 * (j + 1)].reshape(SEQ, 384)
            flip[384 * j : 384 * (j + 1), :] = blk.T

    def product(right, width, held, base, piece, wide):
        for lo in range(0, width, 384):
            hi = min(lo + 384, width)
            grad[:, :, 0 : hi - lo] = nn(flip[...], right(slice(lo, hi))).reshape(8, BAND, hi - lo)
            pack(held, grad, base + lo, base + hi, piece, wide)

    def blank(held, piece, wide):
        used = 4 * (wide // piece)
        held[:, :, :, used:MAIN, wide : wide + piece] = jnp.zeros((2, 4, 4, MAIN - used, piece), BF)

    turn_rows(mrows)
    product(lambda at: act[:, :, at].reshape(SEQ, 384), HID, held2, 0, PIECE2, WIDE2)
    turn_rows(crows)
    product(lambda at: hidden[:, :, at].reshape(SEQ, 384), HID, held2, HID, PIECE2, WIDE2)
    blank(held2, PIECE2, WIDE2)
    sc2.step1()

    rows_g = RowGather(grows, rg)
    sums = [jnp.zeros((1, D), F32)] * 4
    for j in range(CHUNKS):
        at = pl.ds(j * CH, CH)
        normed, inverse = layer_norm(block_out[at])
        g = sum2.total(j)
        back = cot[at] + norm_back(g, normed, inverse, vec(mid_gain))
        input_grad[at] = back
        grows[rank, at] = back.astype(BF)
        rows_g.put(j)
        for k, v in enumerate((back, g * normed, g, cot[at])):
            sums[k] = sums[k] + jnp.sum(v, 0, keepdims=True)
    early[0] = jnp.zeros((8, D), F32)
    for k in range(4):
        early[0, k : k + 1, :] = sums[k]
    early[0, pl.ds(4 + rank, 1), :] = upsum[...]
    ec = [send(early.at[0], early_in.at[0], se, 0, "c")]
    sum2.end()

    def down_block(r, carry):
        mrows[r] = nt(hidden[r], whole(wdown)).astype(BF)
        return carry

    lax.fori_loop(0, 4, down_block, 0)
    sum3 = TpSum(mrows, h1, h2, h3, hs)
    sum3.start_cross()
    sum3.start_sib()
    ec[0].wait_recv()
    early[1] = early[0] + early_in[0]
    ec.append(send(early.at[1], early_in.at[1], se, 1, "yh"))

    def mix_back(a, b):
        def step(n, carry):
            r = (1 - n) * a + n * b
            at = pl.ds(pl.multiple_of(r * ROWS, ROWS), ROWS)
            dmix[at] = nn(grows[r], whole(wout)).astype(BF)
            return carry

        lax.fori_loop(0, 2, step, 0)

    def attend_back(chip, between):
        at = half_rows(chip)
        for h in range(HEADS):
            lo = HD * h
            if h == 3:
                between()
            scores, query = scores_of(h, at)
            probs = jnp.exp(scores - logsum[h, chip])
            key, value = head_slices(h)
            dout = dmix[at, :][:, lo : lo + HD]
            dv_acc[h] += nn(probs.astype(BF), dout)
            prob_grad = nt(value, dout)
            delta = jnp.sum(probs * prob_grad, 0, keepdims=True)
            ds = (probs * (prob_grad - delta) * SCALE).astype(BF)
            dk_acc[h] += nn(ds, query)
            dq = lax.dot_general(
                key, ds, (((0,), (0,)), ((), ())), preferred_element_type=F32
            ).T
            qv[0:1, lo : lo + HD] += jnp.sum(dq, 0, keepdims=True)
            qkv[at, lo : lo + HD] = dq.astype(BF)

    rows_g.chip()
    mix_back(rank, sib)
    sum3.middle()
    sc3.plan1()

    def back_step(n, carry):
        def between():
            @pl.when(n == 0)
            def _():
                for j in range(CHUNKS):
                    rows_g.forward(j)

        attend_back(yh + n * (1 - 2 * yh), between)

        @pl.when(n == 0)
        def _():
            rows_g.rest()
            mix_back(over, cross)
            turn_rows(grows)
            product(lambda at: mixed[:, at], OUT, held3, 0, PIECE3, WIDE3)
            blank(held3, PIECE3, WIDE3)
            sc3.go1()

        return carry

    lax.fori_loop(0, 2, back_step, 0)
    ec[1].wait_recv()
    early[2] = early[1] + early_in[1]
    ec.append(send(early.at[2], early_in.at[2], se, 2, "yl"))
    for h in range(HEADS):
        lo = HD * h
        qv[0:1, COLS + lo : COLS + lo + HD] = jnp.sum(dv_acc[h], 0, keepdims=True)
        qkv[:, COLS + lo : COLS + lo + HD] = dk_acc[h].astype(BF)
        qkv[:, 2 * COLS + lo : 2 * COLS + lo + HD] = dv_acc[h].astype(BF)
    qkv[:, 3 * COLS : QKV] = jnp.zeros((SEQ, QKV - 3 * COLS), BF)

    def attn_block(r):
        at = pl.ds(pl.multiple_of(r * ROWS, ROWS), ROWS)
        part1[r] = nt(qkv[at], whole(wqkv)).astype(BF)

    sum4 = TpSum(part1, f1, f2, f3, fs)
    attn_block(cross)
    sum4.start_cross()
    attn_block(over)
    sum4.middle()
    sc2.step2()
    attn_block(sib)
    sum4.start_sib()
    attn_block(rank)
    turn_rows(arows)
    product(lambda at: qkv[:, at], QKV, held1, 0, PIECE1, WIDE1)
    blank(held1, PIECE1, WIDE1)
    sc3.step2()
    sc1.step1()
    ec[2].wait_recv()
    early[3] = early[2] + early_in[2]
    for k, step in enumerate(NEAR):
        ec.append(send(early.at[3], early_in.at[3 + x], se, 3 + k, "x", step))
    early_in[3 + x] = early[3]

    sums = [jnp.zeros((1, D), F32)] * 2
    for j in range(CHUNKS):
        at = pl.ds(j * CH, CH)
        normed, inverse = layer_norm(stream[at])
        g = sum4.total(j)
        input_grad[at] = input_grad[at] + norm_back(g, normed, inverse, vec(pre_gain))
        for k, v in enumerate((g * normed, g)):
            sums[k] = sums[k] + jnp.sum(v, 0, keepdims=True)
    late[0] = jnp.zeros((8, D), F32)
    late[0, 0:1, :] = sums[0]
    late[0, 1:2, :] = sums[1]
    late[0, pl.ds(4 + rank, 1), :] = qv[...]
    here = yl * 4 + yh * 2 + c
    lc = [
        send_to(late.at[0], late_in.at[here], sl, k, moves) for k, moves in enumerate(LINE)
    ]
    late_in[here] = late[0]
    for j in range(CHUNKS):
        at = pl.ds(j * CH, CH)
        block_out[at] = block_out[at] + sum3.total(j) + vec(down_bias)
    for copy in ec[3:6]:
        copy.wait_recv()
    early[4] = early_in[3] + early_in[4] + early_in[5] + early_in[6]
    for k, step in enumerate(NEAR):
        ec.append(send(early.at[4], early_in.at[7 + z], se, 6 + k, "z", step))
    early_in[7 + z] = early[4]
    for copy in lc:
        copy.wait_recv()
    late[1] = sum((late_in[k] for k in range(1, 8)), late_in[0])
    for k, step in enumerate(NEAR):
        lc.append(send(late.at[1], late_in.at[8 + x], sl, 7 + k, "x", step))
    late_in[8 + x] = late[1]
    sc2.step3()
    sc1.step2()
    for copy in lc[7:10]:
        copy.wait_recv()
    late[2] = late_in[8] + late_in[9] + late_in[10] + late_in[11]
    for k, step in enumerate(NEAR):
        lc.append(send(late.at[2], late_in.at[12 + z], sl, 10 + k, "z", step))
    late_in[12 + z] = late[2]
    sc3.step3()
    sc1.step3()
    sc2.finish(flat2, WIDE2, PIECE2)
    gu[...] = flat2[:, 0:TRUE_HID]
    gd[...] = flat2[:, HID : HID + TRUE_HID]
    sc3.finish(flat3, WIDE3, PIECE3)
    go[...] = flat3[:, 0:COLS]
    for copy in ec[6:9]:
        copy.wait_recv()
    early_out[...] = early_in[7] + early_in[8] + early_in[9] + early_in[10]
    for copy in lc[10:13]:
        copy.wait_recv()
    late_out[...] = late_in[12] + late_in[13] + late_in[14] + late_in[15]
    sc1.finish(flat1, WIDE1, PIECE1)
    gq[...] = flat1[:, 0:COLS]
    gk[...] = flat1[:, COLS : 2 * COLS]
    gv[...] = flat1[:, 2 * COLS : 3 * COLS]
    for copy in ec + lc:
        copy.wait_send()
    for item in (rows_a, rows_c, rows_g, sum3, sum4, sc1, sc2, sc3):
        item.end()


def split_kernel(*refs):
    early, late = refs[8:10]
    outs = refs[10:]
    for k in range(8):
        outs[k][...] = refs[k][...]

    def joined(ref, lo, width):
        rows = [ref[4 + r : 5 + r, lo : lo + width] for r in range(4)]
        return jnp.concatenate(rows, 1).reshape(4 * width)

    pregain, preshift, query, value, outbias, midgain, midshift, up, downbias = outs[8:]
    pregain[...] = late[0]
    preshift[...] = late[1]
    query[...] = joined(late, 0, COLS)
    value[...] = joined(late, COLS, COLS)
    outbias[...] = early[0]
    midgain[...] = early[1]
    midshift[...] = early[2]
    downbias[...] = early[3]
    up[...] = joined(early, 0, TRUE_HID)


def per_device(*args):
    (
        residual, valid_keys, pre_gain, pre_shift, wq, bq, wk, wv, bv, wo, out_bias, mid_gain,
        mid_shift, wu, bu, wd, down_bias, cotangent,
    ) = args
    vm = pl.BlockSpec(memory_space=pltpu.VMEM)
    ins = (
        residual[0], valid_keys, pre_gain, pre_shift, wq, bq, wk, wv, bv, wo.T, out_bias,
        mid_gain, mid_shift, wu, bu, wd.T, down_bias, cotangent[0],
    )
    arrays = [
        (ROWS, D), (ROWS, D), (SHARD, COLS), (SHARD, COLS), (SHARD, COLS), (SHARD, COLS),
        (SHARD, TRUE_HID), (SHARD, TRUE_HID),
    ]
    outs = arrays + [(8, D), (8, D)]
    rows = (4, ROWS, D)
    dma = lambda *n: pltpu.SemaphoreType.DMA(n)
    tp_sum = [
        pltpu.VMEM((2, ROWS, D), BF),
        pltpu.VMEM((ROWS, D), BF),
        pltpu.VMEM((ROWS, D), BF),
        dma(2, 2 + CHUNKS),
    ]
    scratch = [
        pltpu.VMEM((2, 4, 4, MAIN, PACK1), BF),
        pltpu.VMEM((2, 4, 4, MAIN, PACK2), BF),
        pltpu.VMEM((2, 4, 4, MAIN, PACK3), BF),
        pltpu.VMEM((SHARD, WIDE1), F32),
        pltpu.VMEM((SHARD, WIDE2), F32),
        pltpu.VMEM((SHARD, WIDE3), F32),
        pltpu.VMEM((8, BAND, QKV), BF),
        pltpu.VMEM((8, BAND, OUT), BF),
        pltpu.VMEM((8, BAND, HID), BF),
        pltpu.VMEM((8, BAND, HID), BF),
        pltpu.VMEM(rows, BF),
        pltpu.VMEM(rows, BF),
        pltpu.VMEM(rows, BF),
        pltpu.VMEM(rows, BF),
        pltpu.VMEM((SEQ, QKV), BF),
        pltpu.VMEM((SEQ, OUT), BF),
        pltpu.VMEM((SEQ, OUT), BF),
        pltpu.VMEM((SEQ, 128), F32),
        pltpu.VMEM((HEADS, SEQ // QC, 1, QC), F32),
        pltpu.VMEM(rows, BF),
        pltpu.VMEM(rows, BF),
        pltpu.VMEM((8, BAND, 384), F32),
        pltpu.VMEM((D, SEQ), BF),
        pltpu.VMEM(rows, BF),
        pltpu.VMEM((HEADS, SEQ, HD), F32),
        pltpu.VMEM((HEADS, SEQ, HD), F32),
        pltpu.VMEM((1, D), F32),
        pltpu.VMEM((1, HID), F32),
        pltpu.VMEM((1, QKV), F32),
        pltpu.VMEM((1, HID), F32),
        pltpu.VMEM((5, 8, D), F32),
        pltpu.VMEM((11, 8, D), F32),
        pltpu.VMEM((3, 8, D), F32),
        pltpu.VMEM((16, 8, D), F32),
        *([dma(2, 1), dma(2, 7), dma(2, 7)] * 3),
        *([dma(2, 3 * CHUNKS)] * 4),
        dma(2, 9),
        dma(2, 13),
        *tp_sum,
        *tp_sum,
        *scatter_scratch(CUT1, PACK1),
        *scatter_scratch(CUT2, PACK2),
        *scatter_scratch(CUT3, PACK3),
    ]
    out = pl.pallas_call(
        layer_kernel,
        name="layer",
        out_shape=[jax.ShapeDtypeStruct(s, F32) for s in outs],
        in_specs=[vm] * len(ins),
        out_specs=[vm] * len(outs),
        scratch_shapes=scratch,
        compiler_params=pltpu.CompilerParams(
            collective_id=0, has_side_effects=True, vmem_limit_bytes=63 * 2**20
        ),
    )(*ins)
    ends = arrays + [(D,)] * 7 + [(4 * TRUE_HID,), (D,)]
    done = pl.pallas_call(
        split_kernel,
        name="split",
        out_shape=[jax.ShapeDtypeStruct(s, F32) for s in ends],
        in_specs=[vm] * len(out),
        out_specs=[vm] * len(ends),
    )(*out)
    return (
        done[0][None], done[1][None], done[2], done[3], done[4], done[5].T, done[6], done[7].T,
        *done[8:],
    )


def solution(mesh):
    split = Mesh(mesh.devices.reshape(2, 4, 4, 2, 2), ("yl", "z", "x", "yh", "c"))
    rows3 = P(FSDP, TP, None)
    down_cols = P(FSDP, TP)
    across = P(TP, FSDP)
    return jax.shard_map(
        per_device,
        mesh=split,
        in_specs=(
            rows3, P(FSDP, None), P(), P(), down_cols, P(), down_cols, down_cols, P(), across,
            P(), P(), P(), down_cols, P(), across, P(), rows3,
        ),
        out_specs=(
            rows3, rows3, down_cols, down_cols, down_cols, across, down_cols, across,
            P(), P(), P(), P(), P(), P(), P(), P(), P(),
        ),
        check_vma=False,
    )
```
